32 devices in a mesh: feat: 4 (over y, x), dom: 8 (over z, core).
Axes of the slice: x: 2, y: 2, z: 4, core: 2. Of those that a mesh axis runs over, the one named last changes fastest.
Arguments:
- features: bfloat16 [4, 8, 512, 1024], P(None, 'dom', None, 'feat'), may hold values from -100 to 100
- w_self: bfloat16 [1024, 256], P('feat'), may hold values from -0.1875 to 0.1875
- w_neigh: bfloat16 [1024, 256], P('feat'), may hold values from -2 to 2
- gain: float32 [256], replicated, may hold values from 0.5 to 1.5
- shift: float32 [256], replicated, may hold values from -1 to 1
- d_hidden: bfloat16 [4, 8, 512, 256], P('feat', 'dom'), may hold values from -32 to 32
- send_rows: int32 [4, 8, 32, 32], P('feat', 'dom'), may hold values from 0 to 511
- send_count: int32 [4, 8, 32], P('feat', 'dom'), may hold values from 0 to 32, as said below
- tile_src: int32 [4, 8, 136], P('feat', 'dom'), may hold values from 0 to 11, as said below
- tile_dst: int32 [4, 8, 136], P('feat', 'dom'), may hold values from 0 to 3
- tile_count: int32 [4, 8], P('feat', 'dom'), may hold values from 12 to 136, as said below
- tile_vals: bfloat16 [4, 8, 136, 128, 128], P('feat', 'dom'), may hold values from 0 to 1, as said below
Outputs:
- hidden: bfloat16 [4, 8, 512, 256], P('feat', 'dom')
- d_self: bfloat16 [4, 8, 512, 256], P('feat', 'dom')
- d_neigh: bfloat16 [4, 8, 512, 256], P('feat', 'dom')
- gain_grad: float32 [256], replicated
- shift_grad: float32 [256], replicated
The draws below stay inside these ranges and needn't reach their ends.
Inputs may be any that keep to these rules, and one draw needn't show every extreme that they name: `send_rows`: rows may repeat within a list. `send_count`: the live slots are the first ones; in every draw some receiving partition gets 32 live slots from every partition. `tile_src`: blocks below 4 are the partition's own nodes, the others the halo rows in order of sender and slot; the first 12 tiles of each partition name every source block once. `tile_count`: the live tiles are the first ones; some partition has all 136 live. `tile_vals`: nonnegative; tiles past a partition's count are not used.
All inputs are finite; a program needn't handle non-finite values.
Results may differ from the reference program's by a relative error of at most 0.0056.
Values may be sent and summed in bfloat16 or wider, within the bound.
A program may use at most 64 MiB of HBM per device.

```python
import jax
import jax.numpy as jnp
from jax import lax

F = 1024
HID = 256
TILE = 128
ROWS_DEV = 512
SLOTS = 32
FGROUPS = 4
DGROUPS = 8
PARTS_SIZE = 32
NODES = 16384
LOCAL_BLOCKS = 4
HALO_ROWS = 1024
SRC_BLOCKS = 12
TILES = 136


def partition_ramp():
    position = jnp.arange(FGROUPS)[:, None] * DGROUPS + jnp.arange(DGROUPS)[None, :]
    return (3.0 ** (position.astype(jnp.float32) / (PARTS_SIZE - 1)))[:, :, None, None]


def draw_features(key, part):
    subkeys = jax.random.split(jax.random.fold_in(key, 101), 3)
    full_shape = (FGROUPS, DGROUPS, ROWS_DEV, F)
    row_scale = jnp.exp(jax.random.uniform(subkeys[1], (FGROUPS, DGROUPS, ROWS_DEV, 1), minval=0.0, maxval=jnp.log(10.0)))
    col_scale = jnp.exp(jax.random.uniform(subkeys[2], (F,), minval=0.0, maxval=jnp.log(10.0)))
    noise = jax.random.truncated_normal(subkeys[0], -4.0, 4.0, full_shape)
    result = noise * row_scale * col_scale * partition_ramp() / 30.0
    return jnp.clip(result, -100.0, 100.0).astype(jnp.bfloat16)


def draw_d_hidden(key, part):
    subkeys = jax.random.split(jax.random.fold_in(key, 202), 3)
    full_shape = (FGROUPS, DGROUPS, ROWS_DEV, HID)
    column_bias = jax.random.uniform(subkeys[1], (HID,), minval=-1.0, maxval=1.0)
    row_scale = jnp.exp(jax.random.uniform(subkeys[2], (FGROUPS, DGROUPS, ROWS_DEV, 1), minval=0.0, maxval=jnp.log(4.0)))
    noise = jax.random.truncated_normal(subkeys[0], -4.0, 4.0, full_shape)
    result = (column_bias + noise) * row_scale * partition_ramp() / 2.0
    return jnp.clip(result, -32.0, 32.0).astype(jnp.bfloat16)


def draw_send_count(key, part):
    subkeys = jax.random.split(jax.random.fold_in(key, 303), 2)
    counts = jax.random.randint(subkeys[0], (FGROUPS, DGROUPS, PARTS_SIZE), 0, SLOTS + 1)
    busiest = jax.random.randint(subkeys[1], (), 0, PARTS_SIZE)
    counts = jnp.where(jnp.arange(PARTS_SIZE)[None, None, :] == busiest, SLOTS, counts)
    return counts.astype(jnp.int32)


def one_order(subkey):
    return jax.random.permutation(subkey, SRC_BLOCKS)


def draw_tile_src(key, part):
    subkeys = jax.random.split(jax.random.fold_in(key, 404), 2)
    orders = jax.vmap(one_order)(jax.random.split(subkeys[0], PARTS_SIZE))
    others = jax.random.randint(subkeys[1], (PARTS_SIZE, TILES - SRC_BLOCKS), 0, SRC_BLOCKS)
    return jnp.concatenate([orders.astype(jnp.int32), others.astype(jnp.int32)], axis=1).reshape(FGROUPS, DGROUPS, TILES)


def draw_tile_count(key, part):
    subkeys = jax.random.split(jax.random.fold_in(key, 505), 2)
    room = TILES - SRC_BLOCKS
    picks = jax.random.randint(subkeys[0], (PARTS_SIZE,), 0, room + 1)
    extra = picks * picks // max(room, 1)
    busiest = jax.random.randint(subkeys[1], (), 0, PARTS_SIZE)
    extra = jnp.where(jnp.arange(PARTS_SIZE) == busiest, room, extra)
    return (SRC_BLOCKS + extra).reshape(FGROUPS, DGROUPS).astype(jnp.int32)


def draw_tile_vals(key, part):
    subkeys = jax.random.split(jax.random.fold_in(key, 606), 2)
    full_shape = (FGROUPS, DGROUPS, TILES, TILE, TILE)
    present = jax.random.uniform(subkeys[0], full_shape) < 0.0625
    weights = jax.random.uniform(subkeys[1], full_shape, minval=0.25, maxval=1.0)
    return jnp.where(present, weights, 0.0).astype(jnp.bfloat16)


def set_ends(values, key, smallest, top_value):
    extent = values.shape
    spot = [jax.random.randint(jax.random.fold_in(key, axis), (), 0, extent[axis]) for axis in range(len(extent))]
    values = values.at[tuple(spot)].set(smallest)
    longest = extent.index(max(extent))
    spot[longest] = (spot[longest] + 1) % extent[longest]
    return values.at[tuple(spot)].set(top_value)


def shard_levels(rng, dims, shards, smallest, high):
    loudness, own = 1.0, jax.random.fold_in(rng, 6)
    for axis_at, parts in shards:
        steps = jnp.exp(jax.random.uniform(jax.random.fold_in(own, axis_at), (parts,), jnp.float32, smallest / len(shards), high / len(shards)))
        loudness = loudness * jnp.repeat(steps, dims[axis_at] // parts).reshape([-1 if axis == axis_at else 1 for axis in range(len(dims))])
    return loudness


def bell_draw(stream_key, dims, width, limit, pieces=(), held_as=jnp.bfloat16):
    values = jax.random.normal(stream_key, dims, jnp.float32) * width
    if len(pieces) > 0:
        values = shard_levels(stream_key, dims, pieces, -0.22, 0.18) * values
    return jnp.clip(values, min=-limit, max=limit).astype(held_as)


def setup_inputs(seed: int = 0) -> dict:
    key_list = jax.random.split(jax.random.key(seed), 13)
    return {
        "features": draw_features(jax.random.fold_in(key_list[12], 71), 0),
        "w_self": bell_draw(key_list[1], (F, HID), F ** -0.5, 0.1875, ((0, 4),)),
        "w_neigh": bell_draw(key_list[2], (F, HID), (max(F // 128, 1)) ** -0.5, 2.0, ((0, 4),)),
        "gain": jnp.clip(1.0 + 0.1 * jax.random.normal(key_list[3], (HID,), jnp.float32), 0.5, 1.5),
        "shift": jnp.clip(jax.random.uniform(key_list[4], (HID,), jnp.float32, -1.0, 1.0), -1.0, 1.0),
        "d_hidden": draw_d_hidden(jax.random.fold_in(key_list[12], 71), 0),
        "send_rows": set_ends(jax.random.randint(key_list[6], (FGROUPS, DGROUPS, PARTS_SIZE, SLOTS), 0, ROWS_DEV), jax.random.fold_in(key_list[6], 1), 0, ROWS_DEV - 1).astype(jnp.int32),
        "send_count": draw_send_count(jax.random.fold_in(key_list[12], 71), 0),
        "tile_src": draw_tile_src(jax.random.fold_in(key_list[12], 71), 0),
        "tile_dst": set_ends(jax.random.randint(key_list[9], (FGROUPS, DGROUPS, TILES), 0, LOCAL_BLOCKS), jax.random.fold_in(key_list[9], 1), 0, LOCAL_BLOCKS - 1).astype(jnp.int32),
        "tile_count": draw_tile_count(jax.random.fold_in(key_list[12], 71), 0),
        "tile_vals": draw_tile_vals(jax.random.fold_in(key_list[12], 71), 0),
    }


epsilon = 1e-05
highest = lax.Precision.HIGHEST

def reference(features, w_self, w_neigh, gain, shift, d_hidden, send_rows, send_count, tile_src, tile_dst, tile_count, tile_vals):
    stacked = features.reshape(NODES, F)
    own = jnp.dot(stacked, w_self, preferred_element_type=jnp.float32)
    neigh = jnp.dot(stacked, w_neigh, preferred_element_type=jnp.float32).astype(jnp.bfloat16).reshape(PARTS_SIZE, ROWS_DEV, HID)
    targets = send_rows.reshape(PARTS_SIZE, PARTS_SIZE, SLOTS)
    counts = send_count.reshape(PARTS_SIZE, PARTS_SIZE)
    live_slot = jnp.arange(SLOTS, dtype=jnp.int32)[None, None, :] < counts[:, :, None]
    tile_from = tile_src.reshape(PARTS_SIZE, TILES)
    tile_into = tile_dst.reshape(PARTS_SIZE, TILES)
    live_tiles = tile_count.reshape(PARTS_SIZE)
    values = tile_vals.reshape(PARTS_SIZE, TILES, TILE, TILE)
    senders = jnp.arange(PARTS_SIZE, dtype=jnp.int32)

    def aggregate(target):
        picked = neigh[senders[:, None], targets[:, target, :]]
        halo = jnp.where(live_slot[:, target, :, None], picked, jnp.zeros((), jnp.bfloat16))
        source = jnp.concatenate([neigh[target], halo.reshape(HALO_ROWS, HID)], axis=0)
        source = source.reshape(SRC_BLOCKS, TILE, HID).astype(jnp.float32)
        tiles_here = values[target].astype(jnp.float32)
        active = jnp.arange(TILES, dtype=jnp.int32) < live_tiles[target]
        products = jnp.einsum('tij,tjh->tih', tiles_here, source[tile_from[target]], precision=highest)
        placing = ((tile_into[target][None, :] == jnp.arange(LOCAL_BLOCKS, dtype=jnp.int32)[:, None]) & active[None, :]).astype(jnp.float32)
        summed = jnp.einsum('bt,tih->bih', placing, products, precision=highest).reshape(ROWS_DEV, HID)
        degree = 1.0 + jnp.dot(placing, lax.optimization_barrier(jnp.sum(tiles_here, axis=2)), precision=highest).reshape(ROWS_DEV)
        return (summed, degree)
    summed_all, degree_all = lax.map(aggregate, senders)
    degree = degree_all.reshape(NODES)
    pre = own + summed_all.reshape(NODES, HID) / degree[:, None]
    mean_pre = lax.optimization_barrier(jnp.sum(pre, axis=0)) / NODES
    variance = lax.optimization_barrier(jnp.sum(pre * pre, axis=0)) / NODES - mean_pre * mean_pre
    inverse = 1.0 / jnp.sqrt(variance + epsilon)
    normed = (pre - mean_pre) * inverse
    act = gain * normed + shift
    logistic = jax.nn.sigmoid(act)
    hidden = (act * logistic).astype(jnp.bfloat16)
    slope = d_hidden.reshape(NODES, HID).astype(jnp.float32) * logistic * (1.0 + act * (1.0 - logistic))
    shift_grad = lax.optimization_barrier(jnp.sum(slope, axis=0)) / NODES
    gain_grad = lax.optimization_barrier(jnp.sum(slope * normed, axis=0)) / NODES
    dpre = gain * inverse * (slope - shift_grad - normed * gain_grad)
    message_grad = (dpre / degree[:, None]).astype(jnp.bfloat16).reshape(PARTS_SIZE, LOCAL_BLOCKS, TILE, HID)

    def spread(running, target):
        tiles_here = values[target].astype(jnp.float32)
        active = jnp.arange(TILES, dtype=jnp.int32) < live_tiles[target]
        picked = message_grad[target][tile_into[target]].astype(jnp.float32)
        products = jnp.einsum('tij,tih->tjh', tiles_here, picked, precision=highest)
        placing = ((tile_from[target][None, :] == jnp.arange(SRC_BLOCKS, dtype=jnp.int32)[:, None]) & active[None, :]).astype(jnp.float32)
        source_grad = jnp.einsum('st,tjh->sjh', placing, products, precision=highest).reshape(SRC_BLOCKS * TILE, HID)
        running = running.at[target].add(source_grad[:ROWS_DEV])
        halo_grad = source_grad[ROWS_DEV:].astype(jnp.bfloat16)
        halo_grad = lax.optimization_barrier(halo_grad).astype(jnp.float32).reshape(PARTS_SIZE, SLOTS, HID)
        halo_grad = jnp.where(live_slot[:, target, :, None], halo_grad, jnp.zeros((), jnp.float32))
        running = running.at[senders[:, None], targets[:, target, :]].add(halo_grad)
        return (running, None)
    neigh_grad, _ = lax.scan(spread, jnp.zeros((PARTS_SIZE, ROWS_DEV, HID), jnp.float32), senders)
    out_shape = (FGROUPS, DGROUPS, ROWS_DEV, HID)
    return (hidden.reshape(out_shape), dpre.astype(jnp.bfloat16).reshape(out_shape), neigh_grad.astype(jnp.bfloat16).reshape(out_shape), gain_grad, shift_grad)
```

```python
import functools

import jax
import jax.numpy as jnp
from jax import lax
from jax.experimental import pallas as pl
from jax.experimental.pallas import tpu as pltpu
from jax.sharding import PartitionSpec as P

epsilon = 1e-05
MESH = pl.DeviceIdType.MESH
VM = pl.BlockSpec(memory_space=pltpu.VMEM)
HB = pl.BlockSpec(memory_space=pltpu.HBM)
f32 = jnp.float32
bf16 = jnp.bfloat16


def selection(rows_ref, count_ref, node_rows):
    rows = rows_ref[0, 0]
    parts, slots = rows.shape
    counts = jnp.broadcast_to(count_ref[0], (slots, parts)).T
    live = lax.broadcasted_iota(jnp.int32, (parts, slots), 1) < counts
    wanted = jnp.where(live, rows, -1)
    nodes = lax.broadcasted_iota(jnp.int32, (parts, slots, node_rows), 2)
    picked = wanted[:, :, None] == nodes
    return jnp.where(picked, 1.0, 0.0).astype(bf16).reshape(parts * slots, node_rows)


def tile_tables(from_ref, into_ref, live_ref, from_blocks, cells):
    tiles = from_ref.shape[2]
    spare = cells

    def turned(row):
        return jnp.broadcast_to(row, (tiles, tiles)).T

    at = lax.broadcasted_iota(jnp.int32, (1, tiles), 1)
    key = jnp.where(at < live_ref[...], into_ref[0] * from_blocks + from_ref[0], spare)
    key_down = turned(key)
    down = lax.broadcasted_iota(jnp.int32, (tiles, tiles), 0)
    across = lax.broadcasted_iota(jnp.int32, (tiles, tiles), 1)
    before = (key_down < key) | ((key_down == key) & (down < across))
    rank = jnp.sum(jnp.where(before, 1, 0), axis=0, keepdims=True)
    lands = turned(rank) == across
    order = jnp.sum(jnp.where(lands, down, 0), axis=0, keepdims=True)
    ordered_key = jnp.sum(jnp.where(lands, key_down, 0), axis=0, keepdims=True)
    cell = lax.broadcasted_iota(jnp.int32, (tiles, cells), 1)
    key_cells = jnp.broadcast_to(key, (cells, tiles)).T
    last = jnp.sum(jnp.where(key_cells <= cell, 1, 0), axis=0, keepdims=True) - 1
    found = jnp.sum(jnp.where(key_cells == cell, 1, 0), axis=0, keepdims=True)
    return order, ordered_key, last, found


def layer_kernel(feat_size, dom_size, tile, chunks, x_ref, ws_ref, wn_ref, rows_ref, count_ref, from_ref, into_ref,
                 live_ref, vals_ref, gain_ref, shift_ref, dh_ref,
                 hidden_ref, dself_ref, dneigh_ref, ggrad_ref, sgrad_ref,
                 rows_v, count_v, from_v, into_v, live_v, gain_v, shift_v, dh_v,
                 xbuf, wnbuf, wsbuf, own, summed, neigh, halo, outgoing, pick, pick_t, ah, ah_t,
                 mg, back_out, returned, normed_buf, slope_buf, first, second, local_a, local_b,
                 scale_ref, vbuf, history, lists_v, lists_s,
                 local_sems, near_send, near_recv, pass_send, pass_recv, halo_recv, back_recv, stat_recv, out_send):
    me_f, me_d = lax.axis_index("feat"), lax.axis_index("dom")
    me = me_f * dom_size + me_d
    total = feat_size * dom_size
    node_rows = x_ref.shape[2]
    columns, width = wn_ref.shape
    slots = rows_ref.shape[3]
    group_rows = dom_size * slots
    halo_rows = total * slots
    nodes = node_rows * total
    tiles = vbuf.shape[0]
    from_blocks = (node_rows + halo_rows) // tile
    into_blocks = node_rows // tile
    cells = into_blocks * from_blocks
    chunk = width // chunks
    team = next(size for size in (4, 2, 1) if dom_size % size == 0)
    share = columns // team
    seat = lax.rem(me_d, team)
    team_base = me_d - seat
    nears = range(feat_size - 1, 0, -1)

    def peer_of(k):
        peer = lax.rem(me + k, total)
        return peer, (lax.div(peer, dom_size), lax.rem(peer, dom_size))

    def near_of(k):
        return jnp.bitwise_xor(me_f, k) if feat_size & (feat_size - 1) == 0 else lax.rem(me_f + k, feat_size)

    def share_of(owner):
        return pl.ds(pl.multiple_of(owner * share, share), share)

    def rows_of(peer, count):
        return pl.ds(pl.multiple_of(peer * count, count), count)

    def cols_of(c):
        return slice(c * chunk, (c + 1) * chunk)

    barrier = pltpu.get_barrier_semaphore()

    def greet(k, carry):
        _, where = peer_of(k)
        pl.semaphore_signal(barrier, inc=1, device_id=where, device_id_type=MESH)
        return carry

    lax.fori_loop(1, total, greet, 0)

    places = [
        (rows_ref, rows_v), (count_ref, count_v), (from_ref, from_v), (into_ref, into_v), (live_ref, live_v),
        (vals_ref.at[0, 0], vbuf), (wn_ref, wnbuf.at[me_f]), (x_ref.at[me_f, 0], xbuf.at[me_f]),
        (ws_ref, wsbuf.at[me_f]), (gain_ref, gain_v), (shift_ref, shift_v), (dh_ref.at[0, 0], dh_v),
    ]
    local_copies = [pltpu.make_async_copy(a, b, local_sems.at[i]) for i, (a, b) in enumerate(places)]
    for copy in local_copies:
        copy.start()
    with jax.named_scope("s_pick"):
        for copy in local_copies[0:2]:
            copy.wait()
        pick[...] = selection(rows_v, count_v, node_rows)
    with jax.named_scope("s_meet"):
        pl.semaphore_wait(barrier, total - 1)

    def near(kind, k, arriving):
        other = near_of(k)
        landing = other if arriving else me_f
        if kind == 2:
            source, target = x_ref.at[other, 0], xbuf.at[landing]
        else:
            source = (wn_ref, ws_ref)[kind].at[share_of(seat)]
            target = (wnbuf, wsbuf)[kind].at[landing, share_of(seat)]
        return pltpu.make_async_remote_copy(
            src_ref=source,
            dst_ref=target,
            send_sem=near_send.at[kind, other],
            recv_sem=near_recv.at[kind, landing],
            device_id=(other, me_d),
            device_id_type=MESH,
        )

    def passed(kind, k, step, arriving):
        other = near_of(k)
        mate = lax.rem(seat + step, team)
        owner = mate if arriving else seat
        buffer = (wnbuf, wsbuf)[kind]
        return pltpu.make_async_remote_copy(
            src_ref=buffer.at[other, share_of(seat)],
            dst_ref=buffer.at[other, share_of(owner)],
            send_sem=pass_send.at[kind, other, mate],
            recv_sem=pass_recv.at[kind, other, owner],
            device_id=(me_f, team_base + mate),
            device_id_type=MESH,
        )

    with jax.named_scope("s_near"):
        for kind in range(3):
            for k in nears:
                near(kind, k, False).start()

    with jax.named_scope("s_tables"):
        for copy in local_copies[2:5]:
            copy.wait()
        order, ordered_key, last, found = tile_tables(from_v, into_v, live_v, from_blocks, cells)
        lists_v[...] = jnp.zeros_like(lists_v)
        lists_v[0:1, 0:tiles] = order
        lists_v[1:2, 0:tiles] = ordered_key
        lists_v[2:3, 0:cells] = last
        lists_v[3:4, 0:cells] = found
        to_scalars = pltpu.make_async_copy(lists_v, lists_s, local_sems.at[len(places)])
        to_scalars.start()
    with jax.named_scope("s_pass"):
        for kind in range(2):
            for k in nears:
                near(kind, k, True).wait_recv()
                for step in range(1, team):
                    passed(kind, k, step, False).start()
    with jax.named_scope("s_lists"):
        to_scalars.wait()
        for copy in local_copies[5:]:
            copy.wait()

    def add_tile(r, running):
        earlier = lists_s[1, jnp.maximum(r - 1, 0)]
        running = jnp.where(lists_s[1, r] == earlier, running, 0.0) + vbuf[lists_s[0, r]].astype(f32)
        history[r] = running
        return running

    with jax.named_scope("s_addtile"):
        lax.fori_loop(0, tiles, add_tile, jnp.zeros((tile, tile), f32), unroll=2)
    with jax.named_scope("s_settle"):
        for b in range(into_blocks):
            span = slice(b * tile, (b + 1) * tile)

            def settle(s, weight):
                spot = b * from_blocks + s
                value = history[jnp.maximum(lists_s[2, spot], 0)]
                value = jnp.where(lists_s[3, spot] > 0, value, 0.0)
                high = value.astype(bf16)
                lanes = pl.ds(pl.multiple_of(s * tile, tile), tile)
                ah[span, lanes] = high
                ah_t[lanes, span] = high.T
                return weight + value

            weight = lax.fori_loop(0, from_blocks, settle, jnp.zeros((tile, tile), f32))
            inverse_degree = 1.0 / (1.0 + jnp.sum(weight, axis=1, keepdims=True))
            scale_ref[span] = jnp.broadcast_to(inverse_degree, (tile, 128))

    with jax.named_scope("s_neigh"):
        summed[...] = jnp.dot(xbuf[me_f], wnbuf[me_f], preferred_element_type=f32)
        for k in nears:
            for step in range(1, team):
                passed(0, k, step, True).wait_recv()
            near(2, k, True).wait_recv()
            summed[...] += jnp.dot(xbuf[near_of(k)], wnbuf[near_of(k)], preferred_element_type=f32)
        neigh[...] = summed[...].astype(bf16)

    def send_group(source, target, recv_sems, send_sem, c, group, first_spot):
        def start(k, carry):
            spot = lax.rem(me_d + k, dom_size)
            pltpu.make_async_remote_copy(
                src_ref=source.at[c, rows_of(group * dom_size + spot, slots)],
                dst_ref=target.at[c, rows_of(me, slots)],
                send_sem=send_sem,
                recv_sem=recv_sems.at[c, me_f],
                device_id=(group, spot),
                device_id_type=MESH,
            ).start()
            return carry

        lax.fori_loop(first_spot, dom_size, start, 0)

    def wait_group(buffer, recv_sems, send_sem, c, group, count):
        block = buffer.at[c, pl.ds(0, count * slots)]
        pltpu.make_async_remote_copy(
            src_ref=block, dst_ref=block, send_sem=send_sem, recv_sem=recv_sems.at[c, group],
            device_id=(me_f, me_d), device_id_type=MESH,
        ).wait_recv()

    def wait_sent(block, send_sem):
        pltpu.make_async_remote_copy(
            src_ref=block, dst_ref=block, send_sem=send_sem, recv_sem=stat_recv.at[0, 0],
            device_id=(me_f, me_d), device_id_type=MESH,
        ).wait_send()

    def send_stats(source, target, turn, c):
        def start(k, carry):
            _, where = peer_of(k)
            pltpu.make_async_remote_copy(
                src_ref=source.at[c],
                dst_ref=target.at[c, me],
                send_sem=out_send.at[2 + turn, c],
                recv_sem=stat_recv.at[turn, c],
                device_id=where,
                device_id_type=MESH,
            ).start()
            return carry

        lax.fori_loop(1, total, start, 0)

    def wait_stats(target, turn, c):
        block = target.at[c, pl.ds(0, total - 1)]
        pltpu.make_async_remote_copy(
            src_ref=block, dst_ref=block, send_sem=out_send.at[2 + turn, c], recv_sem=stat_recv.at[turn, c],
            device_id=(me_f, me_d), device_id_type=MESH,
        ).wait_recv()

    mine = rows_of(me, slots)
    with jax.named_scope("s_out"):
        for i in range(feat_size):
            group = lax.rem(me_f + i, feat_size)
            span = rows_of(group, group_rows)
            picked = jnp.dot(pick[span], neigh[...], preferred_element_type=f32).astype(bf16)
            for c in range(chunks):
                outgoing[c, span] = picked[:, cols_of(c)]
            send_group(outgoing, halo, halo_recv, out_send.at[0, 0], 0, group, 1 if i == 0 else 0)
        for c in range(1, chunks):
            for i in range(feat_size):
                group = lax.rem(me_f + i, feat_size)
                send_group(outgoing, halo, halo_recv, out_send.at[0, c], c, group, 1 if i == 0 else 0)
        for c in range(chunks):
            halo[c, mine] = outgoing[c, mine]
    with jax.named_scope("s_own"):
        summed[...] = jnp.dot(ah[:, 0:node_rows], neigh[...], preferred_element_type=f32)
        own[...] = jnp.dot(xbuf[me_f], wsbuf[me_f], preferred_element_type=f32)
        for k in nears:
            for step in range(1, team):
                passed(1, k, step, True).wait_recv()
            own[...] += jnp.dot(xbuf[near_of(k)], wsbuf[near_of(k)], preferred_element_type=f32)

    def turn_pick(s, carry):
        rows = rows_of(s, tile)
        pick_t[:, rows] = pick[rows, :].T
        return carry

    with jax.named_scope("s_turn"):
        lax.fori_loop(0, halo_rows // tile, turn_pick, 0)

    for c in range(chunks):
        cols = cols_of(c)
        with jax.named_scope("s_halo%d" % c):
            for i in range(feat_size):
                group = lax.rem(me_f + feat_size - i, feat_size)
                span = rows_of(group, group_rows)
                edges = pl.ds(pl.multiple_of(node_rows + group * group_rows, tile), group_rows)
                wait_group(halo, halo_recv, out_send.at[0, c], c, group, dom_size - 1 if i == 0 else dom_size)
                summed[:, cols] += jnp.dot(ah[:, edges], halo[c, span], preferred_element_type=f32)
        with jax.named_scope("s_pre%d" % c):
            col_sum = jnp.zeros((1, chunk), f32)
            col_square = jnp.zeros((1, chunk), f32)
            for b in range(into_blocks):
                span = slice(b * tile, (b + 1) * tile)
                pre = own[span, cols] + summed[span, cols] * scale_ref[span, 0:1]
                own[span, cols] = pre
                col_sum += jnp.sum(pre, axis=0, keepdims=True)
                col_square += jnp.sum(pre * pre, axis=0, keepdims=True)
            local_a[c, 0:1] = col_sum
            local_a[c, 1:2] = col_square
            first[c, me] = local_a[c]
            send_stats(local_a, first, 0, c)
    gain = gain_v[...].reshape(1, width)
    shift = shift_v[...].reshape(1, width)
    factors = []
    for c in range(chunks):
        cols = cols_of(c)
        with jax.named_scope("s_stat1_%d" % c):
            wait_stats(first, 0, c)
        with jax.named_scope("s_act%d" % c):
            sums = jnp.sum(first[c], axis=0)
            mean = sums[0:1] / nodes
            variance = sums[1:2] / nodes - mean * mean
            inverse = 1.0 / jnp.sqrt(variance + epsilon)
            factors.append(gain[:, cols] * inverse)
            slope_sum = jnp.zeros((1, chunk), f32)
            product_sum = jnp.zeros((1, chunk), f32)
            for b in range(into_blocks):
                span = slice(b * tile, (b + 1) * tile)
                normed = (own[span, cols] - mean) * inverse
                act = gain[:, cols] * normed + shift[:, cols]
                logistic = jax.nn.sigmoid(act)
                hidden_ref[span, cols] = (act * logistic).astype(bf16)
                slope = dh_v[span, cols].astype(f32) * logistic * (1.0 + act * (1.0 - logistic))
                normed_buf[span, cols] = normed
                slope_buf[span, cols] = slope
                slope_sum += jnp.sum(slope, axis=0, keepdims=True)
                product_sum += jnp.sum(slope * normed, axis=0, keepdims=True)
            local_b[c, 0:1] = slope_sum
            local_b[c, 1:2] = product_sum
            second[c, me] = local_b[c]
            send_stats(local_b, second, 1, c)
    for c in range(chunks):
        cols = cols_of(c)
        with jax.named_scope("s_stat2_%d" % c):
            wait_stats(second, 1, c)
        with jax.named_scope("s_dpre%d" % c):
            sums = jnp.sum(second[c], axis=0)
            shift_grad = sums[0:1] / nodes
            gain_grad = sums[1:2] / nodes
            sgrad_ref[:, cols] = shift_grad
            ggrad_ref[:, cols] = gain_grad
            for b in range(into_blocks):
                span = slice(b * tile, (b + 1) * tile)
                dpre = factors[c] * (slope_buf[span, cols] - shift_grad - normed_buf[span, cols] * gain_grad)
                dself_ref[span, cols] = dpre.astype(bf16)
                mg[span, cols] = (dpre * scale_ref[span, 0:1]).astype(bf16)
        with jax.named_scope("s_back%d" % c):
            for i in range(feat_size):
                group = lax.rem(me_f + i, feat_size)
                span = rows_of(group, group_rows)
                edges = pl.ds(pl.multiple_of(node_rows + group * group_rows, tile), group_rows)
                back_out[c, span] = jnp.dot(ah_t[edges], mg[:, cols], preferred_element_type=f32).astype(bf16)
                send_group(back_out, returned, back_recv, out_send.at[1, c], c, group, 1 if i == 0 else 0)
            returned[c, mine] = back_out[c, mine]
    with jax.named_scope("s_dlocal"):
        summed[...] = jnp.dot(ah_t[0:node_rows], mg[...], preferred_element_type=f32)
    with jax.named_scope("s_sendw"):
        for k in nears:
            for kind in range(3):
                near(kind, k, False).wait_send()
            for kind in range(2):
                for step in range(1, team):
                    passed(kind, k, step, False).wait_send()
        for c in range(chunks):
            wait_sent(outgoing.at[c, pl.ds(0, (total - 1) * slots)], out_send.at[0, c])
            for turn, block in ((0, first), (1, second)):
                wait_sent(block.at[c, pl.ds(0, total - 1)], out_send.at[2 + turn, c])
    for c in range(chunks):
        cols = cols_of(c)
        with jax.named_scope("s_gather%d" % c):
            for i in range(feat_size):
                group = lax.rem(me_f + feat_size - i, feat_size)
                span = rows_of(group, group_rows)
                wait_group(returned, back_recv, out_send.at[1, c], c, group, dom_size - 1 if i == 0 else dom_size)
                gathered = jnp.dot(pick_t[:, span], returned[c, span], preferred_element_type=f32)
                if i < feat_size - 1:
                    summed[:, cols] += gathered
                else:
                    dneigh_ref[:, cols] = (summed[:, cols] + gathered).astype(bf16)
    with jax.named_scope("s_sendw2"):
        for c in range(chunks):
            wait_sent(back_out.at[c, pl.ds(0, (total - 1) * slots)], out_send.at[1, c])


def finish_kernel(hidden, d_self, d_neigh, gain_grad, shift_grad,
                  hidden_out, dself_out, dneigh_out, ggrad_out, sgrad_out, sems):
    pairs = ((hidden, hidden_out), (d_self, dself_out), (d_neigh, dneigh_out))
    copies = [pltpu.make_async_copy(a, b.at[0, 0], sems.at[i]) for i, (a, b) in enumerate(pairs)]
    for copy in copies:
        copy.start()
    ggrad_out[...] = gain_grad[...].reshape(ggrad_out.shape)
    sgrad_out[...] = shift_grad[...].reshape(sgrad_out.shape)
    for copy in copies:
        copy.wait()


def shards(feat_size, dom_size, features, w_self, w_neigh, gain, shift, d_hidden, send_rows, send_count,
           tile_src, tile_dst, tile_count, tile_vals):
    node_rows, columns = features.shape[2], features.shape[3]
    width = w_self.shape[1]
    tiles, tile = tile_vals.shape[2], tile_vals.shape[3]
    parts, slots = send_rows.shape[2], send_rows.shape[3]
    own_blocks = node_rows // tile
    halo_rows = parts * slots
    all_rows = node_rows + halo_rows
    cells = own_blocks * (all_rows // tile)
    list_lanes = -(-max(tiles, cells) // 128) * 128
    chunks = 2 if width % 256 == 0 else 1
    chunk = width // chunks
    dma = pltpu.SemaphoreType.DMA
    shape = jax.ShapeDtypeStruct
    i32 = jnp.int32
    results = pl.pallas_call(
        functools.partial(layer_kernel, feat_size, dom_size, tile, chunks),
        out_shape=(
            pltpu.VMEM((node_rows, width), bf16),
            pltpu.VMEM((node_rows, width), bf16),
            pltpu.VMEM((node_rows, width), bf16),
            pltpu.VMEM((1, width), f32),
            pltpu.VMEM((1, width), f32),
        ),
        in_specs=[HB] * 12,
        out_specs=(VM,) * 5,
        scratch_shapes=[
            pltpu.VMEM(send_rows.shape, i32),
            pltpu.VMEM(send_count.shape, i32),
            pltpu.VMEM(tile_src.shape, i32),
            pltpu.VMEM(tile_dst.shape, i32),
            pltpu.VMEM(tile_count.shape, i32),
            pltpu.VMEM(gain.shape, f32),
            pltpu.VMEM(shift.shape, f32),
            pltpu.VMEM((node_rows, width), bf16),
            pltpu.VMEM((feat_size, node_rows, columns), bf16),
            pltpu.VMEM((feat_size, columns, width), bf16),
            pltpu.VMEM((feat_size, columns, width), bf16),
            pltpu.VMEM((node_rows, width), f32),
            pltpu.VMEM((node_rows, width), f32),
            pltpu.VMEM((node_rows, width), bf16),
            pltpu.VMEM((chunks, halo_rows, chunk), bf16),
            pltpu.VMEM((chunks, halo_rows, chunk), bf16),
            pltpu.VMEM((halo_rows, node_rows), bf16),
            pltpu.VMEM((node_rows, halo_rows), bf16),
            pltpu.VMEM((node_rows, all_rows), bf16),
            pltpu.VMEM((all_rows, node_rows), bf16),
            pltpu.VMEM((node_rows, width), bf16),
            pltpu.VMEM((chunks, halo_rows, chunk), bf16),
            pltpu.VMEM((chunks, halo_rows, chunk), bf16),
            pltpu.VMEM((node_rows, width), f32),
            pltpu.VMEM((node_rows, width), f32),
            pltpu.VMEM((chunks, parts, 2, chunk), f32),
            pltpu.VMEM((chunks, parts, 2, chunk), f32),
            pltpu.VMEM((chunks, 2, chunk), f32),
            pltpu.VMEM((chunks, 2, chunk), f32),
            pltpu.VMEM((node_rows, 128), f32),
            pltpu.VMEM((tiles, tile, tile), bf16),
            pltpu.VMEM((tiles, tile, tile), f32),
            pltpu.VMEM((8, list_lanes), i32),
            pltpu.SMEM((8, list_lanes), i32),
            dma((13,)), dma((3, feat_size)), dma((3, feat_size)), dma((2, feat_size, 4)), dma((2, feat_size, 4)),
            dma((chunks, feat_size)), dma((chunks, feat_size)), dma((2, chunks)), dma((4, chunks)),
        ],
        compiler_params=pltpu.CompilerParams(
            collective_id=0, has_side_effects=True, vmem_limit_bytes=58 * 1024 * 1024),
        name="layer",
    )(features, w_self, w_neigh, send_rows, send_count, tile_src, tile_dst, tile_count, tile_vals, gain, shift, d_hidden)
    kept = [pltpu.with_memory_space_constraint(result, pltpu.VMEM) for result in results]
    out_shape = (1, 1, node_rows, width)
    return pl.pallas_call(
        finish_kernel,
        out_shape=(shape(out_shape, bf16),) * 3 + (shape((width,), f32),) * 2,
        in_specs=[VM] * 5,
        out_specs=(HB,) * 3 + (VM,) * 2,
        scratch_shapes=[dma((3,))],
        name="finish",
    )(*kept)


def solution(mesh):
    in_specs = (
        P(None, "dom", None, "feat"),
        P("feat", None),
        P("feat", None),
        P(),
        P(),
        P("feat", "dom", None, None),
        P("feat", "dom", None, None),
        P("feat", "dom", None),
        P("feat", "dom", None),
        P("feat", "dom", None),
        P("feat", "dom"),
        P("feat", "dom", None, None, None),
    )
    out_specs = (
        P("feat", "dom", None, None),
        P("feat", "dom", None, None),
        P("feat", "dom", None, None),
        P(),
        P(),
    )
    body = functools.partial(shards, mesh.shape["feat"], mesh.shape["dom"])
    return jax.shard_map(body, mesh=mesh, in_specs=in_specs, out_specs=out_specs, check_vma=False)
```

```python
import functools

import jax
import jax.numpy as jnp
from jax import lax
from jax.experimental import pallas as pl
from jax.experimental.pallas import tpu as pltpu
from jax.sharding import PartitionSpec as P

epsilon = 1e-05
MESH = pl.DeviceIdType.MESH
VM = pl.BlockSpec(memory_space=pltpu.VMEM)
HB = pl.BlockSpec(memory_space=pltpu.HBM)
f32 = jnp.float32
bf16 = jnp.bfloat16


def selection(rows_ref, count_ref, node_rows):
    rows = rows_ref[0, 0]
    parts, slots = rows.shape
    counts = jnp.broadcast_to(count_ref[0], (slots, parts)).T
    live = lax.broadcasted_iota(jnp.int32, (parts, slots), 1) < counts
    wanted = jnp.where(live, rows, -1)
    nodes = lax.broadcasted_iota(jnp.int32, (parts, slots, node_rows), 2)
    picked = wanted[:, :, None] == nodes
    return jnp.where(picked, 1.0, 0.0).astype(bf16).reshape(parts * slots, node_rows)


def tile_tables(from_ref, into_ref, live_ref, from_blocks, cells):
    tiles = from_ref.shape[2]
    spare = cells

    def turned(row):
        return jnp.broadcast_to(row, (tiles, tiles)).T

    at = lax.broadcasted_iota(jnp.int32, (1, tiles), 1)
    key = jnp.where(at < live_ref[...], into_ref[0] * from_blocks + from_ref[0], spare)
    key_down = turned(key)
    down = lax.broadcasted_iota(jnp.int32, (tiles, tiles), 0)
    across = lax.broadcasted_iota(jnp.int32, (tiles, tiles), 1)
    before = (key_down < key) | ((key_down == key) & (down < across))
    rank = jnp.sum(jnp.where(before, 1, 0), axis=0, keepdims=True)
    lands = turned(rank) == across
    order = jnp.sum(jnp.where(lands, down, 0), axis=0, keepdims=True)
    ordered_key = jnp.sum(jnp.where(lands, key_down, 0), axis=0, keepdims=True)
    cell = lax.broadcasted_iota(jnp.int32, (tiles, cells), 1)
    key_cells = jnp.broadcast_to(key, (cells, tiles)).T
    last = jnp.sum(jnp.where(key_cells <= cell, 1, 0), axis=0, keepdims=True) - 1
    found = jnp.sum(jnp.where(key_cells == cell, 1, 0), axis=0, keepdims=True)
    return order, ordered_key, last, found


def layer_kernel(feat_size, dom_size, tile, chunks, x_ref, ws_ref, wn_ref, rows_ref, count_ref, from_ref, into_ref,
                 live_ref, vals_ref, gain_ref, shift_ref, dh_ref,
                 hidden_ref, dself_ref, dneigh_ref, ggrad_ref, sgrad_ref,
                 rows_v, count_v, from_v, into_v, live_v, gain_v, shift_v, dh_v,
                 xbuf, wnbuf, wsbuf, own, summed, neigh, halo, outgoing, pick, pick_t, ah, ah_t,
                 mg, back_out, returned, normed_buf, slope_buf, first, second, local_a, local_b,
                 scale_ref, vbuf, history, lists_v, lists_s,
                 local_sems, near_send, near_recv, pass_send, pass_recv, halo_recv, back_recv, stat_recv, out_send):
    me_f, me_d = lax.axis_index("feat"), lax.axis_index("dom")
    me = me_f * dom_size + me_d
    total = feat_size * dom_size
    node_rows = x_ref.shape[2]
    columns, width = wn_ref.shape
    slots = rows_ref.shape[3]
    group_rows = dom_size * slots
    halo_rows = total * slots
    nodes = node_rows * total
    tiles = vbuf.shape[0]
    from_blocks = (node_rows + halo_rows) // tile
    into_blocks = node_rows // tile
    cells = into_blocks * from_blocks
    chunk = width // chunks
    team = next(size for size in (8, 4, 2, 1) if dom_size % size == 0 and columns % (16 * size) == 0)
    share = columns // team
    seat = lax.rem(me_d, team)
    team_base = me_d - seat
    nears = range(1, feat_size)
    paired = total & (total - 1) == 0

    def near_of(k):
        return jnp.bitwise_xor(me_f, k) if paired else lax.rem(me_f + k, feat_size)

    def spot_of(k):
        return jnp.bitwise_xor(me_d, dom_size - 1 - k) if paired else lax.rem(me_d + 1 + k, dom_size)

    def group_to(i):
        return near_of(feat_size - 1 - i)

    def group_from(i):
        return near_of(feat_size - 1 - i) if paired else lax.rem(me_f + 1 + i, feat_size)

    def spots_of(i):
        return dom_size - 1 if i == feat_size - 1 else dom_size

    def each_peer(visit):
        for i in range(feat_size):
            def step(k, carry):
                visit(group_to(i), spot_of(k))
                return carry

            lax.fori_loop(0, spots_of(i), step, 0)

    def share_of(owner):
        return pl.ds(pl.multiple_of(owner * share, share), share)

    def rows_of(peer, count):
        return pl.ds(pl.multiple_of(peer * count, count), count)

    def cols_of(c):
        return slice(c * chunk, (c + 1) * chunk)

    barrier = pltpu.get_barrier_semaphore()

    def greet(group, spot):
        pl.semaphore_signal(barrier, inc=1, device_id=(group, spot), device_id_type=MESH)

    each_peer(greet)

    places = [
        (rows_ref, rows_v), (count_ref, count_v), (from_ref, from_v), (into_ref, into_v), (live_ref, live_v),
        (vals_ref.at[0, 0], vbuf), (wn_ref, wnbuf.at[me_f]), (x_ref.at[me_f, 0], xbuf.at[me_f]),
        (ws_ref, wsbuf.at[me_f]), (gain_ref, gain_v), (shift_ref, shift_v), (dh_ref.at[0, 0], dh_v),
    ]
    local_copies = [pltpu.make_async_copy(a, b, local_sems.at[i]) for i, (a, b) in enumerate(places)]
    for copy in local_copies:
        copy.start()
    with jax.named_scope("s_meet"):
        pl.semaphore_wait(barrier, total - 1)

    def near(kind, k, arriving):
        other = near_of(k)
        landing = other if arriving else me_f
        if kind == 2:
            source, target = x_ref.at[other, 0], xbuf.at[landing]
        else:
            source = (wn_ref, ws_ref)[kind].at[share_of(seat)]
            target = (wnbuf, wsbuf)[kind].at[landing, share_of(seat)]
        return pltpu.make_async_remote_copy(
            src_ref=source,
            dst_ref=target,
            send_sem=near_send.at[kind, other],
            recv_sem=near_recv.at[kind, landing],
            device_id=(other, me_d),
            device_id_type=MESH,
        )

    def passed(kind, k, shift, flip, arriving):
        other = near_of(k)
        owner = jnp.bitwise_xor(seat, shift ^ flip if arriving else shift)
        buffer = (wnbuf, wsbuf)[kind]
        return pltpu.make_async_remote_copy(
            src_ref=buffer.at[other, share_of(owner)],
            dst_ref=buffer.at[other, share_of(owner)],
            send_sem=pass_send.at[kind, other, shift ^ flip],
            recv_sem=pass_recv.at[kind, other, shift ^ flip],
            device_id=(me_f, team_base + jnp.bitwise_xor(seat, flip)),
            device_id_type=MESH,
        )

    evens = range(2, team, 2)
    own_flips = [*evens, 1] if team > 1 else []

    def pass_first(kind):
        for k in nears:
            near(kind, k, True).wait_recv()
            for flip in own_flips:
                passed(kind, k, 0, flip, False).start()

    def pass_second(kind):
        for k in nears:
            for shift in evens:
                passed(kind, k, 0, shift, True).wait_recv()
                passed(kind, k, shift, 1, False).start()

    def pass_done(kind, k):
        if team > 1:
            passed(kind, k, 0, 1, True).wait_recv()
        for shift in evens:
            passed(kind, k, shift, 1, True).wait_recv()

    def pass_sent(kind, k):
        for flip in own_flips:
            passed(kind, k, 0, flip, False).wait_send()
        for shift in evens:
            passed(kind, k, shift, 1, False).wait_send()

    with jax.named_scope("s_near"):
        for kind in range(2):
            for k in reversed(nears):
                near(kind, k, False).start()
        for k in nears:
            near(2, k, False).start()

    with jax.named_scope("s_pick"):
        for copy in local_copies[0:2]:
            copy.wait()
        pick[...] = selection(rows_v, count_v, node_rows)
    with jax.named_scope("s_tables"):
        for copy in local_copies[2:5]:
            copy.wait()
        order, ordered_key, last, found = tile_tables(from_v, into_v, live_v, from_blocks, cells)
        lists_v[...] = jnp.zeros_like(lists_v)
        lists_v[0:1, 0:tiles] = order
        lists_v[1:2, 0:tiles] = ordered_key
        lists_v[2:3, 0:cells] = last
        lists_v[3:4, 0:cells] = found
        to_scalars = pltpu.make_async_copy(lists_v, lists_s, local_sems.at[len(places)])
        to_scalars.start()
    with jax.named_scope("s_lists"):
        to_scalars.wait()
        for copy in local_copies[5:]:
            copy.wait()

    def add_tile(r, running):
        earlier = lists_s[1, jnp.maximum(r - 1, 0)]
        running = jnp.where(lists_s[1, r] == earlier, running, 0.0) + vbuf[lists_s[0, r]].astype(f32)
        history[r] = running
        return running

    with jax.named_scope("s_addtile"):
        lax.fori_loop(0, tiles, add_tile, jnp.zeros((tile, tile), f32), unroll=2)
    with jax.named_scope("s_pass1"):
        pass_first(0)
    with jax.named_scope("s_settle"):
        for b in range(into_blocks):
            span = slice(b * tile, (b + 1) * tile)

            def settle(s, weight):
                spot = b * from_blocks + s
                value = history[jnp.maximum(lists_s[2, spot], 0)]
                value = jnp.where(lists_s[3, spot] > 0, value, 0.0)
                high = value.astype(bf16)
                lanes = pl.ds(pl.multiple_of(s * tile, tile), tile)
                ah[span, lanes] = high
                ah_t[lanes, span] = high.T
                return weight + value

            weight = lax.fori_loop(0, from_blocks, settle, jnp.zeros((tile, tile), f32))
            inverse_degree = 1.0 / (1.0 + jnp.sum(weight, axis=1, keepdims=True))
            scale_ref[span] = jnp.broadcast_to(inverse_degree, (tile, 128))

    with jax.named_scope("s_pass2"):
        pass_second(0)
        pass_first(1)

    with jax.named_scope("s_neigh"):
        summed[...] = jnp.dot(xbuf[me_f], wnbuf[me_f], preferred_element_type=f32)
        for k in nears:
            pass_done(0, k)
            near(2, k, True).wait_recv()
            more = jnp.dot(xbuf[near_of(k)], wnbuf[near_of(k)], preferred_element_type=f32)
            if k < feat_size - 1:
                summed[...] += more
            else:
                neigh[...] = (summed[...] + more).astype(bf16)

    def send_group(source, target, recv_sems, send_sem, c, i):
        group = group_to(i)

        def start(k, carry):
            spot = spot_of(k)
            pltpu.make_async_remote_copy(
                src_ref=source.at[c, rows_of(group * dom_size + spot, slots)],
                dst_ref=target.at[c, rows_of(me, slots)],
                send_sem=send_sem,
                recv_sem=recv_sems.at[c, me_f],
                device_id=(group, spot),
                device_id_type=MESH,
            ).start()
            return carry

        lax.fori_loop(0, spots_of(i), start, 0)

    def wait_group(buffer, recv_sems, send_sem, c, i):
        group = group_from(i)
        block = buffer.at[c, pl.ds(0, spots_of(i) * slots)]
        pltpu.make_async_remote_copy(
            src_ref=block, dst_ref=block, send_sem=send_sem, recv_sem=recv_sems.at[c, group],
            device_id=(me_f, me_d), device_id_type=MESH,
        ).wait_recv()

    def wait_sent(block, send_sem):
        pltpu.make_async_remote_copy(
            src_ref=block, dst_ref=block, send_sem=send_sem, recv_sem=stat_recv.at[0, 0],
            device_id=(me_f, me_d), device_id_type=MESH,
        ).wait_send()

    def send_stats(source, target, turn, c):
        def start(group, spot):
            pltpu.make_async_remote_copy(
                src_ref=source.at[c],
                dst_ref=target.at[c, me],
                send_sem=out_send.at[2 + turn, c],
                recv_sem=stat_recv.at[turn, c],
                device_id=(group, spot),
                device_id_type=MESH,
            ).start()

        each_peer(start)

    def wait_stats(target, turn, c):
        block = target.at[c, pl.ds(0, total - 1)]
        pltpu.make_async_remote_copy(
            src_ref=block, dst_ref=block, send_sem=out_send.at[2 + turn, c], recv_sem=stat_recv.at[turn, c],
            device_id=(me_f, me_d), device_id_type=MESH,
        ).wait_recv()

    mine = rows_of(me, slots)
    with jax.named_scope("s_out"):
        for i in range(feat_size):
            span = rows_of(group_to(i), group_rows)
            picked = jnp.dot(pick[span], neigh[...], preferred_element_type=f32).astype(bf16)
            for c in range(chunks):
                outgoing[c, span] = picked[:, cols_of(c)]
            send_group(outgoing, halo, halo_recv, out_send.at[0, 0], 0, i)
        for c in range(chunks):
            halo[c, mine] = outgoing[c, mine]
    with jax.named_scope("s_own"):
        pass_second(1)
        summed[...] = jnp.dot(ah[:, 0:node_rows], neigh[...], preferred_element_type=f32)
        own[...] = jnp.dot(xbuf[me_f], wsbuf[me_f], preferred_element_type=f32)
        for k in nears:
            pass_done(1, k)
            own[...] += jnp.dot(xbuf[near_of(k)], wsbuf[near_of(k)], preferred_element_type=f32)

    def turn_pick(s, carry):
        rows = rows_of(s, tile)
        pick_t[:, rows] = pick[rows, :].T
        return carry

    with jax.named_scope("s_turn"):
        lax.fori_loop(0, halo_rows // tile, turn_pick, 0)

    for c in range(chunks):
        cols = cols_of(c)
        with jax.named_scope("s_halo%d" % c):
            for i in range(feat_size):
                group = group_from(i)
                span = rows_of(group, group_rows)
                edges = pl.ds(pl.multiple_of(node_rows + group * group_rows, tile), group_rows)
                if i == 1 and c + 1 < chunks:
                    for j in range(4):
                        send_group(outgoing, halo, halo_recv, out_send.at[0, c + 1], c + 1, j)
                wait_group(halo, halo_recv, out_send.at[0, c], c, i)
                summed[:, cols] += jnp.dot(ah[:, edges], halo[c, span], preferred_element_type=f32)
        with jax.named_scope("s_pre%d" % c):
            col_sum = jnp.zeros((1, chunk), f32)
            col_square = jnp.zeros((1, chunk), f32)
            for b in range(into_blocks):
                span = slice(b * tile, (b + 1) * tile)
                pre = own[span, cols] + summed[span, cols] * scale_ref[span, 0:1]
                own[span, cols] = pre
                col_sum += jnp.sum(pre, axis=0, keepdims=True)
                col_square += jnp.sum(pre * pre, axis=0, keepdims=True)
            local_a[c, 0:1] = col_sum
            local_a[c, 1:2] = col_square
            first[c, me] = local_a[c]
            send_stats(local_a, first, 0, c)
            if c + 1 < chunks:
                for j in range(4, feat_size):
                    send_group(outgoing, halo, halo_recv, out_send.at[0, c + 1], c + 1, j)
    gain = gain_v[...].reshape(1, width)
    shift = shift_v[...].reshape(1, width)
    factors = []
    for c in range(chunks):
        cols = cols_of(c)
        with jax.named_scope("s_stat1_%d" % c):
            wait_stats(first, 0, c)
        with jax.named_scope("s_act%d" % c):
            sums = jnp.sum(first[c], axis=0)
            mean = sums[0:1] / nodes
            variance = sums[1:2] / nodes - mean * mean
            inverse = 1.0 / jnp.sqrt(variance + epsilon)
            factors.append(gain[:, cols] * inverse)
            slope_sum = jnp.zeros((1, chunk), f32)
            product_sum = jnp.zeros((1, chunk), f32)
            for b in range(into_blocks):
                span = slice(b * tile, (b + 1) * tile)
                normed = (own[span, cols] - mean) * inverse
                act = gain[:, cols] * normed + shift[:, cols]
                logistic = jax.nn.sigmoid(act)
                hidden_ref[span, cols] = (act * logistic).astype(bf16)
                slope = dh_v[span, cols].astype(f32) * logistic * (1.0 + act * (1.0 - logistic))
                normed_buf[span, cols] = normed
                slope_buf[span, cols] = slope
                slope_sum += jnp.sum(slope, axis=0, keepdims=True)
                product_sum += jnp.sum(slope * normed, axis=0, keepdims=True)
            local_b[c, 0:1] = slope_sum
            local_b[c, 1:2] = product_sum
            second[c, me] = local_b[c]
            send_stats(local_b, second, 1, c)
    for c in range(chunks):
        cols = cols_of(c)
        with jax.named_scope("s_stat2_%d" % c):
            wait_stats(second, 1, c)
        with jax.named_scope("s_dpre%d" % c):
            sums = jnp.sum(second[c], axis=0)
            shift_grad = sums[0:1] / nodes
            gain_grad = sums[1:2] / nodes
            sgrad_ref[:, cols] = shift_grad
            ggrad_ref[:, cols] = gain_grad
            for b in range(into_blocks):
                span = slice(b * tile, (b + 1) * tile)
                dpre = factors[c] * (slope_buf[span, cols] - shift_grad - normed_buf[span, cols] * gain_grad)
                dself_ref[span, cols] = dpre.astype(bf16)
                mg[span, cols] = (dpre * scale_ref[span, 0:1]).astype(bf16)
        with jax.named_scope("s_back%d" % c):
            for i in range(feat_size):
                group = group_to(i)
                span = rows_of(group, group_rows)
                edges = pl.ds(pl.multiple_of(node_rows + group * group_rows, tile), group_rows)
                back_out[c, span] = jnp.dot(ah_t[edges], mg[:, cols], preferred_element_type=f32).astype(bf16)
                send_group(back_out, returned, back_recv, out_send.at[1, c], c, i)
            returned[c, mine] = back_out[c, mine]
    with jax.named_scope("s_dlocal"):
        summed[...] = jnp.dot(ah_t[0:node_rows], mg[...], preferred_element_type=f32)
    with jax.named_scope("s_sendw"):
        for k in nears:
            for kind in range(3):
                near(kind, k, False).wait_send()
            for kind in range(2):
                pass_sent(kind, k)
        for c in range(chunks):
            wait_sent(outgoing.at[c, pl.ds(0, (total - 1) * slots)], out_send.at[0, c])
            for turn, block in ((0, first), (1, second)):
                wait_sent(block.at[c, pl.ds(0, total - 1)], out_send.at[2 + turn, c])
    for c in range(chunks):
        cols = cols_of(c)
        with jax.named_scope("s_gather%d" % c):
            for i in range(feat_size):
                span = rows_of(group_from(i), group_rows)
                wait_group(returned, back_recv, out_send.at[1, c], c, i)
                gathered = jnp.dot(pick_t[:, span], returned[c, span], preferred_element_type=f32)
                if i < feat_size - 1:
                    summed[:, cols] += gathered
                else:
                    dneigh_ref[:, cols] = (summed[:, cols] + gathered).astype(bf16)
    with jax.named_scope("s_sendw2"):
        for c in range(chunks):
            wait_sent(back_out.at[c, pl.ds(0, (total - 1) * slots)], out_send.at[1, c])


def finish_kernel(hidden, d_self, d_neigh, gain_grad, shift_grad,
                  hidden_out, dself_out, dneigh_out, ggrad_out, sgrad_out, sems):
    pairs = ((hidden, hidden_out), (d_self, dself_out), (d_neigh, dneigh_out))
    copies = [pltpu.make_async_copy(a, b.at[0, 0], sems.at[i]) for i, (a, b) in enumerate(pairs)]
    for copy in copies:
        copy.start()
    ggrad_out[...] = gain_grad[...].reshape(ggrad_out.shape)
    sgrad_out[...] = shift_grad[...].reshape(sgrad_out.shape)
    for copy in copies:
        copy.wait()


def shards(feat_size, dom_size, features, w_self, w_neigh, gain, shift, d_hidden, send_rows, send_count,
           tile_src, tile_dst, tile_count, tile_vals):
    node_rows, columns = features.shape[2], features.shape[3]
    width = w_self.shape[1]
    tiles, tile = tile_vals.shape[2], tile_vals.shape[3]
    parts, slots = send_rows.shape[2], send_rows.shape[3]
    own_blocks = node_rows // tile
    halo_rows = parts * slots
    all_rows = node_rows + halo_rows
    cells = own_blocks * (all_rows // tile)
    list_lanes = -(-max(tiles, cells) // 128) * 128
    chunks = 2 if width % 256 == 0 else 1
    chunk = width // chunks
    dma = pltpu.SemaphoreType.DMA
    shape = jax.ShapeDtypeStruct
    i32 = jnp.int32
    results = pl.pallas_call(
        functools.partial(layer_kernel, feat_size, dom_size, tile, chunks),
        out_shape=(
            pltpu.VMEM((node_rows, width), bf16),
            pltpu.VMEM((node_rows, width), bf16),
            pltpu.VMEM((node_rows, width), bf16),
            pltpu.VMEM((1, width), f32),
            pltpu.VMEM((1, width), f32),
        ),
        in_specs=[HB] * 12,
        out_specs=(VM,) * 5,
        scratch_shapes=[
            pltpu.VMEM(send_rows.shape, i32),
            pltpu.VMEM(send_count.shape, i32),
            pltpu.VMEM(tile_src.shape, i32),
            pltpu.VMEM(tile_dst.shape, i32),
            pltpu.VMEM(tile_count.shape, i32),
            pltpu.VMEM(gain.shape, f32),
            pltpu.VMEM(shift.shape, f32),
            pltpu.VMEM((node_rows, width), bf16),
            pltpu.VMEM((feat_size, node_rows, columns), bf16),
            pltpu.VMEM((feat_size, columns, width), bf16),
            pltpu.VMEM((feat_size, columns, width), bf16),
            pltpu.VMEM((node_rows, width), f32),
            pltpu.VMEM((node_rows, width), f32),
            pltpu.VMEM((node_rows, width), bf16),
            pltpu.VMEM((chunks, halo_rows, chunk), bf16),
            pltpu.VMEM((chunks, halo_rows, chunk), bf16),
            pltpu.VMEM((halo_rows, node_rows), bf16),
            pltpu.VMEM((node_rows, halo_rows), bf16),
            pltpu.VMEM((node_rows, all_rows), bf16),
            pltpu.VMEM((all_rows, node_rows), bf16),
            pltpu.VMEM((node_rows, width), bf16),
            pltpu.VMEM((chunks, halo_rows, chunk), bf16),
            pltpu.VMEM((chunks, halo_rows, chunk), bf16),
            pltpu.VMEM((node_rows, width), f32),
            pltpu.VMEM((node_rows, width), f32),
            pltpu.VMEM((chunks, parts, 2, chunk), f32),
            pltpu.VMEM((chunks, parts, 2, chunk), f32),
            pltpu.VMEM((chunks, 2, chunk), f32),
            pltpu.VMEM((chunks, 2, chunk), f32),
            pltpu.VMEM((node_rows, 128), f32),
            pltpu.VMEM((tiles, tile, tile), bf16),
            pltpu.VMEM((tiles, tile, tile), f32),
            pltpu.VMEM((8, list_lanes), i32),
            pltpu.SMEM((8, list_lanes), i32),
            dma((13,)), dma((3, feat_size)), dma((3, feat_size)), dma((2, feat_size, 8)), dma((2, feat_size, 8)),
            dma((chunks, feat_size)), dma((chunks, feat_size)), dma((2, chunks)), dma((4, chunks)),
        ],
        compiler_params=pltpu.CompilerParams(
            collective_id=0, has_side_effects=True, vmem_limit_bytes=58 * 1024 * 1024),
        name="layer",
    )(features, w_self, w_neigh, send_rows, send_count, tile_src, tile_dst, tile_count, tile_vals, gain, shift, d_hidden)
    kept = [pltpu.with_memory_space_constraint(result, pltpu.VMEM) for result in results]
    out_shape = (1, 1, node_rows, width)
    return pl.pallas_call(
        finish_kernel,
        out_shape=(shape(out_shape, bf16),) * 3 + (shape((width,), f32),) * 2,
        in_specs=[VM] * 5,
        out_specs=(HB,) * 3 + (VM,) * 2,
        scratch_shapes=[dma((3,))],
        name="finish",
    )(*kept)


def solution(mesh):
    in_specs = (
        P(None, "dom", None, "feat"),
        P("feat", None),
        P("feat", None),
        P(),
        P(),
        P("feat", "dom", None, None),
        P("feat", "dom", None, None),
        P("feat", "dom", None),
        P("feat", "dom", None),
        P("feat", "dom", None),
        P("feat", "dom"),
        P("feat", "dom", None, None, None),
    )
    out_specs = (
        P("feat", "dom", None, None),
        P("feat", "dom", None, None),
        P("feat", "dom", None, None),
        P(),
        P(),
    )
    body = functools.partial(shards, mesh.shape["feat"], mesh.shape["dom"])
    return jax.shard_map(body, mesh=mesh, in_specs=in_specs, out_specs=out_specs, check_vma=False)
```

```python
import functools

import jax
import jax.numpy as jnp
from jax import lax
from jax.experimental import pallas as pl
from jax.experimental.pallas import tpu as pltpu
from jax.sharding import PartitionSpec as P

epsilon = 1e-05
MESH = pl.DeviceIdType.MESH
VM = pl.BlockSpec(memory_space=pltpu.VMEM)
HB = pl.BlockSpec(memory_space=pltpu.HBM)
f32 = jnp.float32
bf16 = jnp.bfloat16


def selection(rows_ref, count_ref, node_rows):
    rows = rows_ref[0, 0]
    parts, slots = rows.shape
    counts = jnp.broadcast_to(count_ref[0], (slots, parts)).T
    live = lax.broadcasted_iota(jnp.int32, (parts, slots), 1) < counts
    wanted = jnp.where(live, rows, -1)
    nodes = lax.broadcasted_iota(jnp.int32, (parts, slots, node_rows), 2)
    picked = wanted[:, :, None] == nodes
    return jnp.where(picked, 1.0, 0.0).astype(bf16).reshape(parts * slots, node_rows)


def tile_tables(from_ref, into_ref, live_ref, from_blocks, cells):
    tiles = from_ref.shape[2]
    spare = cells

    def turned(row):
        return jnp.broadcast_to(row, (tiles, tiles)).T

    at = lax.broadcasted_iota(jnp.int32, (1, tiles), 1)
    key = jnp.where(at < live_ref[...], into_ref[0] * from_blocks + from_ref[0], spare)
    key_down = turned(key)
    down = lax.broadcasted_iota(jnp.int32, (tiles, tiles), 0)
    across = lax.broadcasted_iota(jnp.int32, (tiles, tiles), 1)
    before = (key_down < key) | ((key_down == key) & (down < across))
    rank = jnp.sum(jnp.where(before, 1, 0), axis=0, keepdims=True)
    lands = turned(rank) == across
    order = jnp.sum(jnp.where(lands, down, 0), axis=0, keepdims=True)
    ordered_key = jnp.sum(jnp.where(lands, key_down, 0), axis=0, keepdims=True)
    cell = lax.broadcasted_iota(jnp.int32, (tiles, cells), 1)
    key_cells = jnp.broadcast_to(key, (cells, tiles)).T
    last = jnp.sum(jnp.where(key_cells <= cell, 1, 0), axis=0, keepdims=True) - 1
    found = jnp.sum(jnp.where(key_cells == cell, 1, 0), axis=0, keepdims=True)
    return order, ordered_key, last, found


def layer_kernel(feat_size, dom_size, tile, chunks, x_ref, ws_ref, wn_ref, rows_ref, count_ref, from_ref, into_ref,
                 live_ref, vals_ref, gain_ref, shift_ref, dh_ref,
                 hidden_ref, dself_ref, dneigh_ref, ggrad_ref, sgrad_ref,
                 rows_v, count_v, from_v, into_v, live_v, gain_v, shift_v, dh_v,
                 xbuf, wnbuf, wsbuf, own, summed, neigh, halo, outgoing, pick, pick_t, ah, ah_t,
                 mg, back_out, returned, normed_buf, slope_buf, first, second, local_a, local_b,
                 scale_ref, vbuf, history, lists_v, lists_s,
                 local_sems, near_send, near_recv, pass_send, pass_recv, halo_recv, back_recv, stat_recv, out_send, met):
    me_f, me_d = lax.axis_index("feat"), lax.axis_index("dom")
    me = me_f * dom_size + me_d
    total = feat_size * dom_size
    node_rows = x_ref.shape[2]
    columns, width = wn_ref.shape
    slots = rows_ref.shape[3]
    group_rows = dom_size * slots
    halo_rows = total * slots
    nodes = node_rows * total
    tiles = vbuf.shape[0]
    from_blocks = (node_rows + halo_rows) // tile
    into_blocks = node_rows // tile
    cells = into_blocks * from_blocks
    chunk = width // chunks
    team = next(size for size in (8, 4, 2, 1) if dom_size % size == 0 and columns % (16 * size) == 0)
    share = columns // team
    seat = lax.rem(me_d, team)
    team_base = me_d - seat
    nears = range(1, feat_size)
    paired = total & (total - 1) == 0

    def near_of(k):
        return jnp.bitwise_xor(me_f, k) if paired else lax.rem(me_f + k, feat_size)

    def spot_of(k):
        return jnp.bitwise_xor(me_d, dom_size - 1 - k) if paired else lax.rem(me_d + 1 + k, dom_size)

    def group_to(i):
        return near_of(feat_size - 1 - i)

    def group_from(i):
        return near_of(feat_size - 1 - i) if paired else lax.rem(me_f + 1 + i, feat_size)

    def spots_of(i):
        return dom_size - 1 if i == feat_size - 1 else dom_size

    def each_peer(visit):
        for i in range(feat_size):
            def step(k, carry):
                visit(group_to(i), spot_of(k))
                return carry

            lax.fori_loop(0, spots_of(i), step, 0)

    def share_of(owner):
        return pl.ds(pl.multiple_of(owner * share, share), share)

    def rows_of(peer, count):
        return pl.ds(pl.multiple_of(peer * count, count), count)

    def cols_of(c):
        return slice(c * chunk, (c + 1) * chunk)

    barrier = pltpu.get_barrier_semaphore()
    split = dom_size % 2 == 0 and dom_size > 2
    side = lax.rem(me_d, 2)
    sibling = me_d + 1 - 2 * side
    near_count = 2 * feat_size - 1
    far_count = total - 2 * feat_size

    def hail(where):
        pl.semaphore_signal(barrier, inc=1, device_id=where, device_id_type=MESH)

    def hail_far(k, carry):
        pair = lax.rem(lax.div(me_d, 2) + 1 + lax.rem(k, dom_size // 2 - 1), dom_size // 2)
        hail((lax.div(k, dom_size // 2 - 1), 2 * pair + 1))
        return carry

    if split:
        for k in nears:
            hail((near_of(k), me_d - side))

        @pl.when(side == 1)
        def _():
            hail((me_f, sibling))

        lax.fori_loop(0, feat_size * (dom_size // 2 - 1), hail_far, 0)
    else:
        each_peer(lambda group, spot: hail((group, spot)))

    def meet_near():
        if not split:
            pl.semaphore_wait(barrier, total - 1)
            return

        @pl.when(side == 0)
        def _():
            pl.semaphore_wait(barrier, near_count)
            pl.semaphore_signal(met.at[0], inc=1, device_id=(me_f, sibling), device_id_type=MESH)

        @pl.when(side == 1)
        def _():
            pl.semaphore_wait(met.at[0], 1)

    def meet_far():
        if not split:
            return

        @pl.when(side == 1)
        def _():
            pl.semaphore_wait(barrier, far_count)
            pl.semaphore_signal(met.at[1], inc=1, device_id=(me_f, sibling), device_id_type=MESH)

        @pl.when(side == 0)
        def _():
            pl.semaphore_wait(met.at[1], 1)

    places = [
        (rows_ref, rows_v), (count_ref, count_v), (from_ref, from_v), (into_ref, into_v), (live_ref, live_v),
        (vals_ref.at[0, 0], vbuf), (wn_ref, wnbuf.at[me_f]), (x_ref.at[me_f, 0], xbuf.at[me_f]),
        (ws_ref, wsbuf.at[me_f]), (gain_ref, gain_v), (shift_ref, shift_v), (dh_ref.at[0, 0], dh_v),
    ]
    local_copies = [pltpu.make_async_copy(a, b, local_sems.at[i]) for i, (a, b) in enumerate(places)]
    for copy in local_copies:
        copy.start()
    with jax.named_scope("s_meet"):
        meet_near()

    def near(kind, k, arriving):
        other = near_of(k)
        landing = other if arriving else me_f
        if kind == 2:
            source, target = x_ref.at[other, 0], xbuf.at[landing]
        else:
            source = (wn_ref, ws_ref)[kind].at[share_of(seat)]
            target = (wnbuf, wsbuf)[kind].at[landing, share_of(seat)]
        return pltpu.make_async_remote_copy(
            src_ref=source,
            dst_ref=target,
            send_sem=near_send.at[kind, other],
            recv_sem=near_recv.at[kind, landing],
            device_id=(other, me_d),
            device_id_type=MESH,
        )

    def passed(kind, k, shift, flip, arriving):
        other = near_of(k)
        owner = jnp.bitwise_xor(seat, shift ^ flip if arriving else shift)
        buffer = (wnbuf, wsbuf)[kind]
        return pltpu.make_async_remote_copy(
            src_ref=buffer.at[other, share_of(owner)],
            dst_ref=buffer.at[other, share_of(owner)],
            send_sem=pass_send.at[kind, other, shift ^ flip],
            recv_sem=pass_recv.at[kind, other, shift ^ flip],
            device_id=(me_f, team_base + jnp.bitwise_xor(seat, flip)),
            device_id_type=MESH,
        )

    evens = range(2, team, 2)
    own_flips = [*evens, 1] if team > 1 else []

    def pass_first(kind):
        for k in nears:
            near(kind, k, True).wait_recv()
            for flip in own_flips:
                passed(kind, k, 0, flip, False).start()

    def pass_second(kind):
        for k in nears:
            for shift in evens:
                passed(kind, k, 0, shift, True).wait_recv()
                passed(kind, k, shift, 1, False).start()

    def pass_done(kind, k):
        if team > 1:
            passed(kind, k, 0, 1, True).wait_recv()
        for shift in evens:
            passed(kind, k, shift, 1, True).wait_recv()

    def pass_sent(kind, k):
        for flip in own_flips:
            passed(kind, k, 0, flip, False).wait_send()
        for shift in evens:
            passed(kind, k, shift, 1, False).wait_send()

    with jax.named_scope("s_near"):
        for kind in range(2):
            for k in reversed(nears):
                near(kind, k, False).start()
        for k in nears:
            near(2, k, False).start()

    with jax.named_scope("s_pick"):
        for copy in local_copies[0:2]:
            copy.wait()
        pick[...] = selection(rows_v, count_v, node_rows)
    with jax.named_scope("s_tables"):
        for copy in local_copies[2:5]:
            copy.wait()
        order, ordered_key, last, found = tile_tables(from_v, into_v, live_v, from_blocks, cells)
        lists_v[...] = jnp.zeros_like(lists_v)
        lists_v[0:1, 0:tiles] = order
        lists_v[1:2, 0:tiles] = ordered_key
        lists_v[2:3, 0:cells] = last
        lists_v[3:4, 0:cells] = found
        to_scalars = pltpu.make_async_copy(lists_v, lists_s, local_sems.at[len(places)])
        to_scalars.start()
    with jax.named_scope("s_lists"):
        to_scalars.wait()
        for copy in local_copies[5:]:
            copy.wait()

    def add_tile(r, running):
        earlier = lists_s[1, jnp.maximum(r - 1, 0)]
        running = jnp.where(lists_s[1, r] == earlier, running, 0.0) + vbuf[lists_s[0, r]].astype(f32)
        history[r] = running
        return running

    with jax.named_scope("s_addtile"):
        lax.fori_loop(0, tiles, add_tile, jnp.zeros((tile, tile), f32), unroll=2)
    with jax.named_scope("s_far"):
        meet_far()
    with jax.named_scope("s_pass1"):
        pass_first(0)
    with jax.named_scope("s_settle"):
        for b in range(into_blocks):
            span = slice(b * tile, (b + 1) * tile)

            def settle(s, weight):
                spot = b * from_blocks + s
                value = history[jnp.maximum(lists_s[2, spot], 0)]
                value = jnp.where(lists_s[3, spot] > 0, value, 0.0)
                high = value.astype(bf16)
                lanes = pl.ds(pl.multiple_of(s * tile, tile), tile)
                ah[span, lanes] = high
                ah_t[lanes, span] = high.T
                return weight + value

            weight = lax.fori_loop(0, from_blocks, settle, jnp.zeros((tile, tile), f32))
            inverse_degree = 1.0 / (1.0 + jnp.sum(weight, axis=1, keepdims=True))
            scale_ref[span] = jnp.broadcast_to(inverse_degree, (tile, 128))

    with jax.named_scope("s_pass2"):
        pass_second(0)
        pass_first(1)

    with jax.named_scope("s_neigh"):
        summed[...] = jnp.dot(xbuf[me_f], wnbuf[me_f], preferred_element_type=f32)
        for k in nears:
            pass_done(0, k)
            near(2, k, True).wait_recv()
            more = jnp.dot(xbuf[near_of(k)], wnbuf[near_of(k)], preferred_element_type=f32)
            if k < feat_size - 1:
                summed[...] += more
            else:
                neigh[...] = (summed[...] + more).astype(bf16)

    def send_group(source, target, recv_sems, send_sem, c, i):
        group = group_to(i)

        def start(k, carry):
            spot = spot_of(k)
            pltpu.make_async_remote_copy(
                src_ref=source.at[c, rows_of(group * dom_size + spot, slots)],
                dst_ref=target.at[c, rows_of(me, slots)],
                send_sem=send_sem,
                recv_sem=recv_sems.at[c, me_f],
                device_id=(group, spot),
                device_id_type=MESH,
            ).start()
            return carry

        lax.fori_loop(0, spots_of(i), start, 0)

    def wait_group(buffer, recv_sems, send_sem, c, i):
        group = group_from(i)
        block = buffer.at[c, pl.ds(0, spots_of(i) * slots)]
        pltpu.make_async_remote_copy(
            src_ref=block, dst_ref=block, send_sem=send_sem, recv_sem=recv_sems.at[c, group],
            device_id=(me_f, me_d), device_id_type=MESH,
        ).wait_recv()

    def wait_sent(block, send_sem):
        pltpu.make_async_remote_copy(
            src_ref=block, dst_ref=block, send_sem=send_sem, recv_sem=stat_recv.at[0, 0],
            device_id=(me_f, me_d), device_id_type=MESH,
        ).wait_send()

    def send_stats(source, target, turn, c):
        def start(group, spot):
            pltpu.make_async_remote_copy(
                src_ref=source.at[c],
                dst_ref=target.at[c, me],
                send_sem=out_send.at[2 + turn, c],
                recv_sem=stat_recv.at[turn, c],
                device_id=(group, spot),
                device_id_type=MESH,
            ).start()

        each_peer(start)

    def wait_stats(target, turn, c):
        block = target.at[c, pl.ds(0, total - 1)]
        pltpu.make_async_remote_copy(
            src_ref=block, dst_ref=block, send_sem=out_send.at[2 + turn, c], recv_sem=stat_recv.at[turn, c],
            device_id=(me_f, me_d), device_id_type=MESH,
        ).wait_recv()

    mine = rows_of(me, slots)
    with jax.named_scope("s_out"):
        for i in range(feat_size):
            span = rows_of(group_to(i), group_rows)
            picked = jnp.dot(pick[span], neigh[...], preferred_element_type=f32).astype(bf16)
            for c in range(chunks):
                outgoing[c, span] = picked[:, cols_of(c)]
            send_group(outgoing, halo, halo_recv, out_send.at[0, 0], 0, i)
        for c in range(chunks):
            halo[c, mine] = outgoing[c, mine]
    with jax.named_scope("s_own"):
        pass_second(1)
        summed[...] = jnp.dot(ah[:, 0:node_rows], neigh[...], preferred_element_type=f32)
        own[...] = jnp.dot(xbuf[me_f], wsbuf[me_f], preferred_element_type=f32)
        for k in nears:
            pass_done(1, k)
            own[...] += jnp.dot(xbuf[near_of(k)], wsbuf[near_of(k)], preferred_element_type=f32)

    def turn_pick(s, carry):
        rows = rows_of(s, tile)
        pick_t[:, rows] = pick[rows, :].T
        return carry

    with jax.named_scope("s_turn"):
        lax.fori_loop(0, halo_rows // tile, turn_pick, 0)

    gain = gain_v[...].reshape(1, width)
    shift = shift_v[...].reshape(1, width)
    inverses = {}

    def send_rows(c, i):
        send_group(outgoing, halo, halo_recv, out_send.at[0, c], c, i)

    def take_rows(c, i):
        with jax.named_scope("s_halo%d%d" % (c, i)):
            group = group_from(i)
            edges = pl.ds(pl.multiple_of(node_rows + group * group_rows, tile), group_rows)
            wait_group(halo, halo_recv, out_send.at[0, c], c, i)
            summed[:, cols_of(c)] += jnp.dot(
                ah[:, edges], halo[c, rows_of(group, group_rows)], preferred_element_type=f32)

    def sum_pre(c):
        cols = cols_of(c)
        with jax.named_scope("s_pre%d" % c):
            col_sum = jnp.zeros((1, chunk), f32)
            col_square = jnp.zeros((1, chunk), f32)
            for b in range(into_blocks):
                span = slice(b * tile, (b + 1) * tile)
                pre = own[span, cols] + summed[span, cols] * scale_ref[span, 0:1]
                own[span, cols] = pre
                col_sum += jnp.sum(pre, axis=0, keepdims=True)
                col_square += jnp.sum(pre * pre, axis=0, keepdims=True)
            local_a[c, 0:1] = col_sum
            local_a[c, 1:2] = col_square
            first[c, me] = local_a[c]
            send_stats(local_a, first, 0, c)

    def activate(c):
        cols = cols_of(c)
        with jax.named_scope("s_stat1_%d" % c):
            wait_stats(first, 0, c)
        with jax.named_scope("s_act%d" % c):
            sums = jnp.sum(first[c], axis=0)
            mean = sums[0:1] / nodes
            variance = sums[1:2] / nodes - mean * mean
            inverse = 1.0 / jnp.sqrt(variance + epsilon)
            inverses[c] = inverse
            slope_sum = jnp.zeros((1, chunk), f32)
            product_sum = jnp.zeros((1, chunk), f32)
            for b in range(into_blocks):
                span = slice(b * tile, (b + 1) * tile)
                normed = (own[span, cols] - mean) * inverse
                act = gain[:, cols] * normed + shift[:, cols]
                logistic = jax.nn.sigmoid(act)
                hidden_ref[span, cols] = (act * logistic).astype(bf16)
                slope = dh_v[span, cols].astype(f32) * logistic * (1.0 + act * (1.0 - logistic))
                normed_buf[span, cols] = normed
                slope_buf[span, cols] = slope
                slope_sum += jnp.sum(slope, axis=0, keepdims=True)
                product_sum += jnp.sum(slope * normed, axis=0, keepdims=True)
            local_b[c, 0:1] = slope_sum
            local_b[c, 1:2] = product_sum
            second[c, me] = local_b[c]
            send_stats(local_b, second, 1, c)

    def send_back(c):
        cols = cols_of(c)
        with jax.named_scope("s_stat2_%d" % c):
            wait_stats(second, 1, c)
        with jax.named_scope("s_dpre%d" % c):
            sums = jnp.sum(second[c], axis=0)
            shift_grad = sums[0:1] / nodes
            gain_grad = sums[1:2] / nodes
            sgrad_ref[:, cols] = shift_grad
            ggrad_ref[:, cols] = gain_grad
            factor = gain[:, cols] * inverses[c]
            for b in range(into_blocks):
                span = slice(b * tile, (b + 1) * tile)
                dpre = factor * (slope_buf[span, cols] - shift_grad - normed_buf[span, cols] * gain_grad)
                dself_ref[span, cols] = dpre.astype(bf16)
                mg[span, cols] = (dpre * scale_ref[span, 0:1]).astype(bf16)
        with jax.named_scope("s_back%d" % c):
            for i in range(feat_size):
                group = group_to(i)
                span = rows_of(group, group_rows)
                edges = pl.ds(pl.multiple_of(node_rows + group * group_rows, tile), group_rows)
                back_out[c, span] = jnp.dot(ah_t[edges], mg[:, cols], preferred_element_type=f32).astype(bf16)
                send_group(back_out, returned, back_recv, out_send.at[1, c], c, i)
            returned[c, mine] = back_out[c, mine]

    steps = {"S": send_rows, "H": take_rows, "P": sum_pre, "A": activate, "B": send_back}
    for step in "S10 S11 S12 S13 H00 H01 H02 H03 P0 H10 H11 H12 H13 P1 A0 A1 B0 B1".split():
        steps[step[0]](*(int(digit) for digit in step[1:]))
    with jax.named_scope("s_dlocal"):
        summed[...] = jnp.dot(ah_t[0:node_rows], mg[...], preferred_element_type=f32)
    with jax.named_scope("s_sendw"):
        for k in nears:
            for kind in range(3):
                near(kind, k, False).wait_send()
            for kind in range(2):
                pass_sent(kind, k)
        for c in range(chunks):
            wait_sent(outgoing.at[c, pl.ds(0, (total - 1) * slots)], out_send.at[0, c])
            for turn, block in ((0, first), (1, second)):
                wait_sent(block.at[c, pl.ds(0, total - 1)], out_send.at[2 + turn, c])
    for c in range(chunks):
        cols = cols_of(c)
        with jax.named_scope("s_gather%d" % c):
            for i in range(feat_size):
                span = rows_of(group_from(i), group_rows)
                wait_group(returned, back_recv, out_send.at[1, c], c, i)
                gathered = jnp.dot(pick_t[:, span], returned[c, span], preferred_element_type=f32)
                if i < feat_size - 1:
                    summed[:, cols] += gathered
                else:
                    dneigh_ref[:, cols] = (summed[:, cols] + gathered).astype(bf16)
    with jax.named_scope("s_sendw2"):
        for c in range(chunks):
            wait_sent(back_out.at[c, pl.ds(0, (total - 1) * slots)], out_send.at[1, c])


def finish_kernel(hidden, d_self, d_neigh, gain_grad, shift_grad,
                  hidden_out, dself_out, dneigh_out, ggrad_out, sgrad_out, sems):
    pairs = ((hidden, hidden_out), (d_self, dself_out), (d_neigh, dneigh_out))
    copies = [pltpu.make_async_copy(a, b.at[0, 0], sems.at[i]) for i, (a, b) in enumerate(pairs)]
    for copy in copies:
        copy.start()
    ggrad_out[...] = gain_grad[...].reshape(ggrad_out.shape)
    sgrad_out[...] = shift_grad[...].reshape(sgrad_out.shape)
    for copy in copies:
        copy.wait()


def shards(feat_size, dom_size, features, w_self, w_neigh, gain, shift, d_hidden, send_rows, send_count,
           tile_src, tile_dst, tile_count, tile_vals):
    node_rows, columns = features.shape[2], features.shape[3]
    width = w_self.shape[1]
    tiles, tile = tile_vals.shape[2], tile_vals.shape[3]
    parts, slots = send_rows.shape[2], send_rows.shape[3]
    own_blocks = node_rows // tile
    halo_rows = parts * slots
    all_rows = node_rows + halo_rows
    cells = own_blocks * (all_rows // tile)
    list_lanes = -(-max(tiles, cells) // 128) * 128
    chunks = 2 if width % 256 == 0 else 1
    chunk = width // chunks
    dma = pltpu.SemaphoreType.DMA
    shape = jax.ShapeDtypeStruct
    i32 = jnp.int32
    results = pl.pallas_call(
        functools.partial(layer_kernel, feat_size, dom_size, tile, chunks),
        out_shape=(
            pltpu.VMEM((node_rows, width), bf16),
            pltpu.VMEM((node_rows, width), bf16),
            pltpu.VMEM((node_rows, width), bf16),
            pltpu.VMEM((1, width), f32),
            pltpu.VMEM((1, width), f32),
        ),
        in_specs=[HB] * 12,
        out_specs=(VM,) * 5,
        scratch_shapes=[
            pltpu.VMEM(send_rows.shape, i32),
            pltpu.VMEM(send_count.shape, i32),
            pltpu.VMEM(tile_src.shape, i32),
            pltpu.VMEM(tile_dst.shape, i32),
            pltpu.VMEM(tile_count.shape, i32),
            pltpu.VMEM(gain.shape, f32),
            pltpu.VMEM(shift.shape, f32),
            pltpu.VMEM((node_rows, width), bf16),
            pltpu.VMEM((feat_size, node_rows, columns), bf16),
            pltpu.VMEM((feat_size, columns, width), bf16),
            pltpu.VMEM((feat_size, columns, width), bf16),
            pltpu.VMEM((node_rows, width), f32),
            pltpu.VMEM((node_rows, width), f32),
            pltpu.VMEM((node_rows, width), bf16),
            pltpu.VMEM((chunks, halo_rows, chunk), bf16),
            pltpu.VMEM((chunks, halo_rows, chunk), bf16),
            pltpu.VMEM((halo_rows, node_rows), bf16),
            pltpu.VMEM((node_rows, halo_rows), bf16),
            pltpu.VMEM((node_rows, all_rows), bf16),
            pltpu.VMEM((all_rows, node_rows), bf16),
            pltpu.VMEM((node_rows, width), bf16),
            pltpu.VMEM((chunks, halo_rows, chunk), bf16),
            pltpu.VMEM((chunks, halo_rows, chunk), bf16),
            pltpu.VMEM((node_rows, width), f32),
            pltpu.VMEM((node_rows, width), f32),
            pltpu.VMEM((chunks, parts, 2, chunk), f32),
            pltpu.VMEM((chunks, parts, 2, chunk), f32),
            pltpu.VMEM((chunks, 2, chunk), f32),
            pltpu.VMEM((chunks, 2, chunk), f32),
            pltpu.VMEM((node_rows, 128), f32),
            pltpu.VMEM((tiles, tile, tile), bf16),
            pltpu.VMEM((tiles, tile, tile), f32),
            pltpu.VMEM((8, list_lanes), i32),
            pltpu.SMEM((8, list_lanes), i32),
            dma((13,)), dma((3, feat_size)), dma((3, feat_size)), dma((2, feat_size, 8)), dma((2, feat_size, 8)),
            dma((chunks, feat_size)), dma((chunks, feat_size)), dma((2, chunks)), dma((4, chunks)), pltpu.SemaphoreType.REGULAR((2,)),
        ],
        compiler_params=pltpu.CompilerParams(
            collective_id=0, has_side_effects=True, vmem_limit_bytes=58 * 1024 * 1024),
        name="layer",
    )(features, w_self, w_neigh, send_rows, send_count, tile_src, tile_dst, tile_count, tile_vals, gain, shift, d_hidden)
    kept = [pltpu.with_memory_space_constraint(result, pltpu.VMEM) for result in results]
    out_shape = (1, 1, node_rows, width)
    return pl.pallas_call(
        finish_kernel,
        out_shape=(shape(out_shape, bf16),) * 3 + (shape((width,), f32),) * 2,
        in_specs=[VM] * 5,
        out_specs=(HB,) * 3 + (VM,) * 2,
        scratch_shapes=[dma((3,))],
        name="finish",
    )(*kept)


def solution(mesh):
    in_specs = (
        P(None, "dom", None, "feat"),
        P("feat", None),
        P("feat", None),
        P(),
        P(),
        P("feat", "dom", None, None),
        P("feat", "dom", None, None),
        P("feat", "dom", None),
        P("feat", "dom", None),
        P("feat", "dom", None),
        P("feat", "dom"),
        P("feat", "dom", None, None, None),
    )
    out_specs = (
        P("feat", "dom", None, None),
        P("feat", "dom", None, None),
        P("feat", "dom", None, None),
        P(),
        P(),
    )
    body = functools.partial(shards, mesh.shape["feat"], mesh.shape["dom"])
    return jax.shard_map(body, mesh=mesh, in_specs=in_specs, out_specs=out_specs, check_vma=False)
```

```python
import functools

import jax
import jax.numpy as jnp
from jax import lax
from jax.experimental import pallas as pl
from jax.experimental.pallas import tpu as pltpu
from jax.sharding import PartitionSpec as P

epsilon = 1e-05
MESH = pl.DeviceIdType.MESH
VM = pl.BlockSpec(memory_space=pltpu.VMEM)
HB = pl.BlockSpec(memory_space=pltpu.HBM)
f32 = jnp.float32
bf16 = jnp.bfloat16


def selection(rows_ref, count_ref, node_rows):
    rows = rows_ref[0, 0]
    parts, slots = rows.shape
    counts = jnp.broadcast_to(count_ref[0], (slots, parts)).T
    live = lax.broadcasted_iota(jnp.int32, (parts, slots), 1) < counts
    wanted = jnp.where(live, rows, -1)
    nodes = lax.broadcasted_iota(jnp.int32, (parts, slots, node_rows), 2)
    picked = wanted[:, :, None] == nodes
    return jnp.where(picked, 1.0, 0.0).astype(bf16).reshape(parts * slots, node_rows)


def tile_tables(from_ref, into_ref, live_ref, from_blocks, cells):
    tiles = from_ref.shape[2]
    spare = cells

    def turned(row):
        return jnp.broadcast_to(row, (tiles, tiles)).T

    at = lax.broadcasted_iota(jnp.int32, (1, tiles), 1)
    key = jnp.where(at < live_ref[...], into_ref[0] * from_blocks + from_ref[0], spare)
    key_down = turned(key)
    down = lax.broadcasted_iota(jnp.int32, (tiles, tiles), 0)
    across = lax.broadcasted_iota(jnp.int32, (tiles, tiles), 1)
    before = (key_down < key) | ((key_down == key) & (down < across))
    rank = jnp.sum(jnp.where(before, 1, 0), axis=0, keepdims=True)
    lands = turned(rank) == across
    order = jnp.sum(jnp.where(lands, down, 0), axis=0, keepdims=True)
    ordered_key = jnp.sum(jnp.where(lands, key_down, 0), axis=0, keepdims=True)
    cell = lax.broadcasted_iota(jnp.int32, (tiles, cells), 1)
    key_cells = jnp.broadcast_to(key, (cells, tiles)).T
    last = jnp.sum(jnp.where(key_cells <= cell, 1, 0), axis=0, keepdims=True) - 1
    found = jnp.sum(jnp.where(key_cells == cell, 1, 0), axis=0, keepdims=True)
    return order, ordered_key, last, found


def layer_kernel(feat_size, dom_size, tile, chunks, x_ref, ws_ref, wn_ref, rows_ref, count_ref, from_ref, into_ref,
                 live_ref, vals_ref, gain_ref, shift_ref, dh_ref,
                 hidden_ref, dself_ref, dneigh_ref, ggrad_ref, sgrad_ref,
                 rows_v, count_v, from_v, into_v, live_v, gain_v, shift_v, dh_v,
                 xbuf, wnbuf, wsbuf, own, summed, neigh, halo, outgoing, pick, pick_t, ah, ah_t,
                 mg, back_out, returned, normed_buf, slope_buf, first, second, local_a, local_b,
                 scale_ref, vbuf, history, lists_v, lists_s,
                 local_sems, near_send, near_recv, pass_send, pass_recv, halo_recv, stat_recv, out_send, met):
    me_f, me_d = lax.axis_index("feat"), lax.axis_index("dom")
    me = me_f * dom_size + me_d
    total = feat_size * dom_size
    node_rows = x_ref.shape[2]
    columns, width = wn_ref.shape
    slots = rows_ref.shape[3]
    group_rows = dom_size * slots
    halo_rows = total * slots
    nodes = node_rows * total
    tiles = vbuf.shape[0]
    from_blocks = (node_rows + halo_rows) // tile
    into_blocks = node_rows // tile
    cells = into_blocks * from_blocks
    chunk = width // chunks
    team = next(size for size in (8, 4, 2, 1) if dom_size % size == 0 and columns % (16 * size) == 0)
    share = columns // team
    seat = lax.rem(me_d, team)
    team_base = me_d - seat
    nears = range(1, feat_size)
    paired = total & (total - 1) == 0

    def near_of(k):
        return jnp.bitwise_xor(me_f, k) if paired else lax.rem(me_f + k, feat_size)

    def spot_of(k):
        return jnp.bitwise_xor(me_d, dom_size - 1 - k) if paired else lax.rem(me_d + 1 + k, dom_size)

    def group_to(i):
        return near_of(feat_size - 1 - i)

    def group_from(i):
        return near_of(feat_size - 1 - i) if paired else lax.rem(me_f + 1 + i, feat_size)

    def spots_of(i):
        return dom_size - 1 if i == feat_size - 1 else dom_size

    def each_peer(visit):
        for i in range(feat_size):
            def step(k, carry):
                visit(group_to(i), spot_of(k))
                return carry

            lax.fori_loop(0, spots_of(i), step, 0)

    def share_of(owner):
        return pl.ds(pl.multiple_of(owner * share, share), share)

    def slab_of(origin):
        return pl.ds(pl.multiple_of(origin * columns, columns), columns)

    def share_in(origin, owner):
        return pl.ds(pl.multiple_of(origin * columns + owner * share, share), share)

    def rows_of(peer, count):
        return pl.ds(pl.multiple_of(peer * count, count), count)

    def cols_of(c):
        return slice(c * chunk, (c + 1) * chunk)

    barrier = pltpu.get_barrier_semaphore()
    split = dom_size % 2 == 0 and dom_size > 2
    side = lax.rem(me_d, 2)
    sibling = me_d + 1 - 2 * side
    near_count = 2 * feat_size - 1
    far_count = total - 2 * feat_size

    def hail(where):
        pl.semaphore_signal(barrier, inc=1, device_id=where, device_id_type=MESH)

    def hail_far(k, carry):
        pair = lax.rem(lax.div(me_d, 2) + 1 + lax.rem(k, dom_size // 2 - 1), dom_size // 2)
        hail((lax.div(k, dom_size // 2 - 1), 2 * pair + 1))
        return carry

    if split:
        for k in nears:
            hail((near_of(k), me_d - side))

        @pl.when(side == 1)
        def _():
            hail((me_f, sibling))

        lax.fori_loop(0, feat_size * (dom_size // 2 - 1), hail_far, 0)
    else:
        each_peer(lambda group, spot: hail((group, spot)))

    def meet_near():
        if not split:
            pl.semaphore_wait(barrier, total - 1)
            return

        @pl.when(side == 0)
        def _():
            pl.semaphore_wait(barrier, near_count)
            pl.semaphore_signal(met.at[0], inc=1, device_id=(me_f, sibling), device_id_type=MESH)

        @pl.when(side == 1)
        def _():
            pl.semaphore_wait(met.at[0], 1)

    def meet_far():
        if not split:
            return

        @pl.when(side == 1)
        def _():
            pl.semaphore_wait(barrier, far_count)
            pl.semaphore_signal(met.at[1], inc=1, device_id=(me_f, sibling), device_id_type=MESH)

        @pl.when(side == 0)
        def _():
            pl.semaphore_wait(met.at[1], 1)

    places = [
        (rows_ref, rows_v), (count_ref, count_v), (from_ref, from_v), (into_ref, into_v), (live_ref, live_v),
        (vals_ref.at[0, 0], vbuf), (wn_ref, wnbuf.at[slab_of(me_f)]), (x_ref.at[me_f, 0], xbuf.at[me_f]),
        (ws_ref, wsbuf.at[slab_of(me_f)]), (gain_ref, gain_v), (shift_ref, shift_v), (dh_ref.at[0, 0], dh_v),
    ]
    local_copies = [pltpu.make_async_copy(a, b, local_sems.at[i]) for i, (a, b) in enumerate(places)]
    for copy in local_copies:
        copy.start()
    with jax.named_scope("s_meet"):
        meet_near()

    def near(kind, k, arriving):
        other = near_of(k)
        landing = other if arriving else me_f
        if kind == 2:
            source, target = x_ref.at[other, 0], xbuf.at[landing]
        else:
            source = (wn_ref, ws_ref)[kind].at[share_of(seat)]
            target = (wnbuf, wsbuf)[kind].at[share_in(landing, seat)]
        return pltpu.make_async_remote_copy(
            src_ref=source,
            dst_ref=target,
            send_sem=near_send.at[kind],
            recv_sem=near_recv.at[kind + k - 1 if kind == 2 else kind],
            device_id=(other, me_d),
            device_id_type=MESH,
        )

    def settled(block, sem):
        pltpu.make_async_copy(block, block, sem).wait()

    evens = range(2, team, 2)
    weights = (wnbuf, wsbuf)

    def shares(kind, count):
        return weights[kind].at[pl.ds(0, (feat_size - 1) * count * share)]

    def hand_on(kind, k, shift, flip):
        place = weights[kind].at[share_in(near_of(k), jnp.bitwise_xor(seat, shift))]
        pltpu.make_async_remote_copy(
            src_ref=place,
            dst_ref=place,
            send_sem=pass_send.at[kind],
            recv_sem=pass_recv.at[kind, 1 if flip == 1 else 0],
            device_id=(me_f, team_base + jnp.bitwise_xor(seat, flip)),
            device_id_type=MESH,
        ).start()

    def pass_first(kind):
        settled(shares(kind, 1), near_recv.at[kind])
        if team > 1:
            for k in nears:
                for flip in (*evens, 1):
                    hand_on(kind, k, 0, flip)

    def pass_second(kind):
        if team > 2:
            settled(shares(kind, team // 2 - 1), pass_recv.at[kind, 0])
            for k in nears:
                for shift in evens:
                    hand_on(kind, k, shift, 1)

    def pass_done(kind):
        if team > 1:
            settled(shares(kind, team // 2), pass_recv.at[kind, 1])

    def pass_sent(kind):
        settled(shares(kind, 1), near_send.at[kind])
        if team > 1:
            settled(shares(kind, team - 1), pass_send.at[kind])

    with jax.named_scope("s_near"):
        for kind in range(2):
            for k in reversed(nears):
                near(kind, k, False).start()
        for k in nears:
            near(2, k, False).start()

    with jax.named_scope("s_pick"):
        for copy in local_copies[0:2]:
            copy.wait()
        pick[...] = selection(rows_v, count_v, node_rows)
    with jax.named_scope("s_tables"):
        for copy in local_copies[2:5]:
            copy.wait()
        order, ordered_key, last, found = tile_tables(from_v, into_v, live_v, from_blocks, cells)
        lists_v[...] = jnp.zeros_like(lists_v)
        lists_v[0:1, 0:tiles] = order
        lists_v[1:2, 0:tiles] = ordered_key
        lists_v[2:3, 0:cells] = last
        lists_v[3:4, 0:cells] = found
        to_scalars = pltpu.make_async_copy(lists_v, lists_s, local_sems.at[0])
        to_scalars.start()
    with jax.named_scope("s_lists"):
        to_scalars.wait()
        for copy in local_copies[5:]:
            copy.wait()

    def add_tile(r, running):
        earlier = lists_s[1, jnp.maximum(r - 1, 0)]
        running = jnp.where(lists_s[1, r] == earlier, running, 0.0) + vbuf[lists_s[0, r]].astype(f32)
        history[r] = running
        return running

    with jax.named_scope("s_addtile"):
        lax.fori_loop(0, tiles, add_tile, jnp.zeros((tile, tile), f32), unroll=2)
    with jax.named_scope("s_far"):
        meet_far()
    with jax.named_scope("s_pass1"):
        pass_first(0)
    with jax.named_scope("s_settle"):
        for b in range(into_blocks):
            span = slice(b * tile, (b + 1) * tile)

            def settle(s, weight):
                spot = b * from_blocks + s
                value = history[jnp.maximum(lists_s[2, spot], 0)]
                value = jnp.where(lists_s[3, spot] > 0, value, 0.0)
                high = value.astype(bf16)
                lanes = pl.ds(pl.multiple_of(s * tile, tile), tile)
                ah[span, lanes] = high
                ah_t[lanes, span] = high.T
                return weight + value

            weight = lax.fori_loop(0, from_blocks, settle, jnp.zeros((tile, tile), f32))
            inverse_degree = 1.0 / (1.0 + jnp.sum(weight, axis=1, keepdims=True))
            scale_ref[span] = jnp.broadcast_to(inverse_degree, (tile, 128))

    with jax.named_scope("s_pass2"):
        pass_second(0)
        pass_first(1)

    with jax.named_scope("s_neigh"):
        summed[...] = jnp.dot(xbuf[me_f], wnbuf[slab_of(me_f)], preferred_element_type=f32)
        pass_done(0)
        for k in nears:
            near(2, k, True).wait_recv()
            more = jnp.dot(xbuf[near_of(k)], wnbuf[slab_of(near_of(k))], preferred_element_type=f32)
            if k < feat_size - 1:
                summed[...] += more
            else:
                neigh[...] = (summed[...] + more).astype(bf16)

    def send_group(source, target, recv_sems, send_sem, c, i):
        group = group_to(i)

        def start(k, carry):
            spot = spot_of(k)
            pltpu.make_async_remote_copy(
                src_ref=source.at[c, rows_of(group * dom_size + spot, slots)],
                dst_ref=target.at[c, rows_of(me, slots)],
                send_sem=send_sem,
                recv_sem=recv_sems.at[c, me_f],
                device_id=(group, spot),
                device_id_type=MESH,
            ).start()
            return carry

        lax.fori_loop(0, spots_of(i), start, 0)

    def wait_group(buffer, recv_sems, c, i):
        settled(buffer.at[c, pl.ds(0, spots_of(i) * slots)], recv_sems.at[c, group_from(i)])

    def send_stats(source, target, turn, c):
        def start(group, spot):
            pltpu.make_async_remote_copy(
                src_ref=source.at[c],
                dst_ref=target.at[c, me],
                send_sem=out_send.at[2 + turn],
                recv_sem=stat_recv.at[turn, c],
                device_id=(group, spot),
                device_id_type=MESH,
            ).start()

        each_peer(start)

    def wait_stats(target, turn, c):
        settled(target.at[c, pl.ds(0, total - 1)], stat_recv.at[turn, c])

    mine = rows_of(me, slots)
    with jax.named_scope("s_out"):
        for i in range(feat_size):
            span = rows_of(group_to(i), group_rows)
            picked = jnp.dot(pick[span], neigh[...], preferred_element_type=f32).astype(bf16)
            for c in range(chunks):
                outgoing[c, span] = picked[:, cols_of(c)]
            send_group(outgoing, halo, halo_recv, out_send.at[0], 0, i)
        for c in range(chunks):
            halo[c, mine] = outgoing[c, mine]
    with jax.named_scope("s_own"):
        pass_second(1)
        summed[...] = jnp.dot(ah[:, 0:node_rows], neigh[...], preferred_element_type=f32)
        own[...] = jnp.dot(xbuf[me_f], wsbuf[slab_of(me_f)], preferred_element_type=f32)
        pass_done(1)
        for k in nears:
            own[...] += jnp.dot(xbuf[near_of(k)], wsbuf[slab_of(near_of(k))], preferred_element_type=f32)

    def turn_pick(s, carry):
        rows = rows_of(s, tile)
        pick_t[:, rows] = pick[rows, :].T
        return carry

    with jax.named_scope("s_turn"):
        lax.fori_loop(0, halo_rows // tile, turn_pick, 0)

    gain = gain_v[...].reshape(1, width)
    shift = shift_v[...].reshape(1, width)
    inverses = {}

    def send_rows(c, i):
        send_group(outgoing, halo, halo_recv, out_send.at[0], c, i)

    def take_rows(c, i):
        with jax.named_scope("s_halo%d%d" % (c, i)):
            group = group_from(i)
            edges = pl.ds(pl.multiple_of(node_rows + group * group_rows, tile), group_rows)
            wait_group(halo, halo_recv, c, i)
            summed[:, cols_of(c)] += jnp.dot(
                ah[:, edges], halo[c, rows_of(group, group_rows)], preferred_element_type=f32)

    def sum_pre(c):
        cols = cols_of(c)
        with jax.named_scope("s_pre%d" % c):
            col_sum = jnp.zeros((1, chunk), f32)
            col_square = jnp.zeros((1, chunk), f32)
            for b in range(into_blocks):
                span = slice(b * tile, (b + 1) * tile)
                pre = own[span, cols] + summed[span, cols] * scale_ref[span, 0:1]
                own[span, cols] = pre
                col_sum += jnp.sum(pre, axis=0, keepdims=True)
                col_square += jnp.sum(pre * pre, axis=0, keepdims=True)
            local_a[c, 0:1] = col_sum
            local_a[c, 1:2] = col_square
            first[c, me] = local_a[c]
            send_stats(local_a, first, 0, c)

    def activate(c):
        cols = cols_of(c)
        with jax.named_scope("s_stat1_%d" % c):
            wait_stats(first, 0, c)
        with jax.named_scope("s_act%d" % c):
            sums = jnp.sum(first[c], axis=0)
            mean = sums[0:1] / nodes
            variance = sums[1:2] / nodes - mean * mean
            inverse = 1.0 / jnp.sqrt(variance + epsilon)
            inverses[c] = inverse
            slope_sum = jnp.zeros((1, chunk), f32)
            product_sum = jnp.zeros((1, chunk), f32)
            for b in range(into_blocks):
                span = slice(b * tile, (b + 1) * tile)
                normed = (own[span, cols] - mean) * inverse
                act = gain[:, cols] * normed + shift[:, cols]
                logistic = jax.nn.sigmoid(act)
                hidden_ref[span, cols] = (act * logistic).astype(bf16)
                slope = dh_v[span, cols].astype(f32) * logistic * (1.0 + act * (1.0 - logistic))
                normed_buf[span, cols] = normed
                slope_buf[span, cols] = slope
                slope_sum += jnp.sum(slope, axis=0, keepdims=True)
                product_sum += jnp.sum(slope * normed, axis=0, keepdims=True)
            local_b[c, 0:1] = slope_sum
            local_b[c, 1:2] = product_sum
            second[c, me] = local_b[c]
            send_stats(local_b, second, 1, c)

    def send_back(c):
        cols = cols_of(c)
        with jax.named_scope("s_stat2_%d" % c):
            wait_stats(second, 1, c)
        with jax.named_scope("s_dpre%d" % c):
            sums = jnp.sum(second[c], axis=0)
            shift_grad = sums[0:1] / nodes
            gain_grad = sums[1:2] / nodes
            sgrad_ref[:, cols] = shift_grad
            ggrad_ref[:, cols] = gain_grad
            factor = gain[:, cols] * inverses[c]
            for b in range(into_blocks):
                span = slice(b * tile, (b + 1) * tile)
                dpre = factor * (slope_buf[span, cols] - shift_grad - normed_buf[span, cols] * gain_grad)
                dself_ref[span, cols] = dpre.astype(bf16)
                mg[span, cols] = (dpre * scale_ref[span, 0:1]).astype(bf16)
        with jax.named_scope("s_back%d" % c):
            for i in range(feat_size):
                group = group_to(i)
                span = rows_of(group, group_rows)
                edges = pl.ds(pl.multiple_of(node_rows + group * group_rows, tile), group_rows)
                back_out[c, span] = jnp.dot(ah_t[edges], mg[:, cols], preferred_element_type=f32).astype(bf16)
                send_group(back_out, returned, halo_recv, out_send.at[1], c, i)
            returned[c, mine] = back_out[c, mine]

    steps = {"S": send_rows, "H": take_rows, "P": sum_pre, "A": activate, "B": send_back}
    for step in "S10 S11 S12 S13 H00 H01 H02 H03 P0 H10 H11 H12 H13 P1 A0 A1 B0 B1".split():
        steps[step[0]](*(int(digit) for digit in step[1:]))
    with jax.named_scope("s_dlocal"):
        summed[...] = jnp.dot(ah_t[0:node_rows], mg[...], preferred_element_type=f32)
    peers_rows = pl.ds(0, (total - 1) * slots)
    with jax.named_scope("s_sendw"):
        for kind in range(2):
            pass_sent(kind)
        settled(xbuf.at[pl.ds(0, feat_size - 1)], near_send.at[2])
        settled(outgoing.at[:, peers_rows], out_send.at[0])
        settled(first.at[:, pl.ds(0, total - 1)], out_send.at[2])
        settled(second.at[:, pl.ds(0, total - 1)], out_send.at[3])
    for c in range(chunks):
        cols = cols_of(c)
        with jax.named_scope("s_gather%d" % c):
            for i in range(feat_size):
                span = rows_of(group_from(i), group_rows)
                wait_group(returned, halo_recv, c, i)
                gathered = jnp.dot(pick_t[:, span], returned[c, span], preferred_element_type=f32)
                if i < feat_size - 1:
                    summed[:, cols] += gathered
                else:
                    dneigh_ref[:, cols] = (summed[:, cols] + gathered).astype(bf16)
    settled(back_out.at[:, peers_rows], out_send.at[1])


def finish_kernel(hidden, d_self, d_neigh, gain_grad, shift_grad,
                  hidden_out, dself_out, dneigh_out, ggrad_out, sgrad_out, sems):
    pairs = ((hidden, hidden_out), (d_self, dself_out), (d_neigh, dneigh_out))
    copies = [pltpu.make_async_copy(a, b.at[0, 0], sems.at[i]) for i, (a, b) in enumerate(pairs)]
    for copy in copies:
        copy.start()
    ggrad_out[...] = gain_grad[...].reshape(ggrad_out.shape)
    sgrad_out[...] = shift_grad[...].reshape(sgrad_out.shape)
    for copy in copies:
        copy.wait()


def shards(feat_size, dom_size, features, w_self, w_neigh, gain, shift, d_hidden, send_rows, send_count,
           tile_src, tile_dst, tile_count, tile_vals):
    node_rows, columns = features.shape[2], features.shape[3]
    width = w_self.shape[1]
    tiles, tile = tile_vals.shape[2], tile_vals.shape[3]
    parts, slots = send_rows.shape[2], send_rows.shape[3]
    own_blocks = node_rows // tile
    halo_rows = parts * slots
    all_rows = node_rows + halo_rows
    cells = own_blocks * (all_rows // tile)
    list_lanes = -(-max(tiles, cells) // 128) * 128
    chunks = 2 if width % 256 == 0 else 1
    chunk = width // chunks
    dma = pltpu.SemaphoreType.DMA
    shape = jax.ShapeDtypeStruct
    i32 = jnp.int32
    results = pl.pallas_call(
        functools.partial(layer_kernel, feat_size, dom_size, tile, chunks),
        out_shape=(
            pltpu.VMEM((node_rows, width), bf16),
            pltpu.VMEM((node_rows, width), bf16),
            pltpu.VMEM((node_rows, width), bf16),
            pltpu.VMEM((1, width), f32),
            pltpu.VMEM((1, width), f32),
        ),
        in_specs=[HB] * 12,
        out_specs=(VM,) * 5,
        scratch_shapes=[
            pltpu.VMEM(send_rows.shape, i32),
            pltpu.VMEM(send_count.shape, i32),
            pltpu.VMEM(tile_src.shape, i32),
            pltpu.VMEM(tile_dst.shape, i32),
            pltpu.VMEM(tile_count.shape, i32),
            pltpu.VMEM(gain.shape, f32),
            pltpu.VMEM(shift.shape, f32),
            pltpu.VMEM((node_rows, width), bf16),
            pltpu.VMEM((feat_size, node_rows, columns), bf16),
            pltpu.VMEM((feat_size * columns, width), bf16),
            pltpu.VMEM((feat_size * columns, width), bf16),
            pltpu.VMEM((node_rows, width), f32),
            pltpu.VMEM((node_rows, width), f32),
            pltpu.VMEM((node_rows, width), bf16),
            pltpu.VMEM((chunks, halo_rows, chunk), bf16),
            pltpu.VMEM((chunks, halo_rows, chunk), bf16),
            pltpu.VMEM((halo_rows, node_rows), bf16),
            pltpu.VMEM((node_rows, halo_rows), bf16),
            pltpu.VMEM((node_rows, all_rows), bf16),
            pltpu.VMEM((all_rows, node_rows), bf16),
            pltpu.VMEM((node_rows, width), bf16),
            pltpu.VMEM((chunks, halo_rows, chunk), bf16),
            pltpu.VMEM((chunks, halo_rows, chunk), bf16),
            pltpu.VMEM((node_rows, width), f32),
            pltpu.VMEM((node_rows, width), f32),
            pltpu.VMEM((chunks, parts, 2, chunk), f32),
            pltpu.VMEM((chunks, parts, 2, chunk), f32),
            pltpu.VMEM((chunks, 2, chunk), f32),
            pltpu.VMEM((chunks, 2, chunk), f32),
            pltpu.VMEM((node_rows, 128), f32),
            pltpu.VMEM((tiles, tile, tile), bf16),
            pltpu.VMEM((tiles, tile, tile), f32),
            pltpu.VMEM((8, list_lanes), i32),
            pltpu.SMEM((8, list_lanes), i32),
            dma((12,)), dma((3,)), dma((1 + feat_size,)), dma((2,)), dma((2, 2)),
            dma((chunks, feat_size)), dma((2, chunks)), dma((4,)), pltpu.SemaphoreType.REGULAR((2,)),
        ],
        compiler_params=pltpu.CompilerParams(
            collective_id=0, has_side_effects=True, vmem_limit_bytes=58 * 1024 * 1024),
        name="layer",
    )(features, w_self, w_neigh, send_rows, send_count, tile_src, tile_dst, tile_count, tile_vals, gain, shift, d_hidden)
    kept = [pltpu.with_memory_space_constraint(result, pltpu.VMEM) for result in results]
    out_shape = (1, 1, node_rows, width)
    return pl.pallas_call(
        finish_kernel,
        out_shape=(shape(out_shape, bf16),) * 3 + (shape((width,), f32),) * 2,
        in_specs=[VM] * 5,
        out_specs=(HB,) * 3 + (VM,) * 2,
        scratch_shapes=[dma((3,))],
        name="finish",
    )(*kept)


def solution(mesh):
    in_specs = (
        P(None, "dom", None, "feat"),
        P("feat", None),
        P("feat", None),
        P(),
        P(),
        P("feat", "dom", None, None),
        P("feat", "dom", None, None),
        P("feat", "dom", None),
        P("feat", "dom", None),
        P("feat", "dom", None),
        P("feat", "dom"),
        P("feat", "dom", None, None, None),
    )
    out_specs = (
        P("feat", "dom", None, None),
        P("feat", "dom", None, None),
        P("feat", "dom", None, None),
        P(),
        P(),
    )
    body = functools.partial(shards, mesh.shape["feat"], mesh.shape["dom"])
    return jax.shard_map(body, mesh=mesh, in_specs=in_specs, out_specs=out_specs, check_vma=False)
```

```python
import functools

import jax
import jax.numpy as jnp
from jax import lax
from jax.experimental import pallas as pl
from jax.experimental.pallas import tpu as pltpu
from jax.sharding import PartitionSpec as P

epsilon = 1e-05
MESH = pl.DeviceIdType.MESH
VM = pl.BlockSpec(memory_space=pltpu.VMEM)
HB = pl.BlockSpec(memory_space=pltpu.HBM)
f32 = jnp.float32
bf16 = jnp.bfloat16


def selection(rows_ref, count_ref, node_rows):
    rows = rows_ref[0, 0]
    parts, slots = rows.shape
    counts = jnp.broadcast_to(count_ref[0], (slots, parts)).T
    live = lax.broadcasted_iota(jnp.int32, (parts, slots), 1) < counts
    wanted = jnp.where(live, rows, -1)
    nodes = lax.broadcasted_iota(jnp.int32, (parts, slots, node_rows), 2)
    picked = wanted[:, :, None] == nodes
    return jnp.where(picked, 1.0, 0.0).astype(bf16).reshape(parts * slots, node_rows)


def tile_tables(from_ref, into_ref, live_ref, from_blocks, cells):
    tiles = from_ref.shape[2]
    spare = cells

    def turned(row):
        return jnp.broadcast_to(row, (tiles, tiles)).T

    at = lax.broadcasted_iota(jnp.int32, (1, tiles), 1)
    key = jnp.where(at < live_ref[...], into_ref[0] * from_blocks + from_ref[0], spare)
    key_down = turned(key)
    down = lax.broadcasted_iota(jnp.int32, (tiles, tiles), 0)
    across = lax.broadcasted_iota(jnp.int32, (tiles, tiles), 1)
    before = (key_down < key) | ((key_down == key) & (down < across))
    rank = jnp.sum(jnp.where(before, 1, 0), axis=0, keepdims=True)
    lands = turned(rank) == across
    order = jnp.sum(jnp.where(lands, down, 0), axis=0, keepdims=True)
    ordered_key = jnp.sum(jnp.where(lands, key_down, 0), axis=0, keepdims=True)
    cell = lax.broadcasted_iota(jnp.int32, (tiles, cells), 1)
    key_cells = jnp.broadcast_to(key, (cells, tiles)).T
    last = jnp.sum(jnp.where(key_cells <= cell, 1, 0), axis=0, keepdims=True) - 1
    found = jnp.sum(jnp.where(key_cells == cell, 1, 0), axis=0, keepdims=True)
    return order, ordered_key, last, found


def layer_kernel(feat_size, dom_size, tile, chunks, x_ref, ws_ref, wn_ref, rows_ref, count_ref, from_ref, into_ref,
                 live_ref, vals_ref, gain_ref, shift_ref, dh_ref,
                 hidden_ref, dself_ref, dneigh_ref, ggrad_ref, sgrad_ref,
                 rows_v, count_v, from_v, into_v, live_v, gain_v, shift_v, dh_v,
                 xown, xside, xin, wnbuf, wsbuf, part_out, part_in, own, summed, neigh, halo, outgoing, pick, pick_t, ah, ah_t,
                 mg, back_out, returned, normed_buf, slope_buf, first, second, local_a, local_b,
                 scale_ref, vbuf, history, lists_v, lists_s,
                 local_sems, near_send, near_recv, pass_send, pass_recv, part_sems, halo_recv, stat_recv, out_send, met):
    me_f, me_d = lax.axis_index("feat"), lax.axis_index("dom")
    me = me_f * dom_size + me_d
    total = feat_size * dom_size
    node_rows = x_ref.shape[2]
    columns, width = wn_ref.shape
    slots = rows_ref.shape[3]
    group_rows = dom_size * slots
    halo_rows = total * slots
    nodes = node_rows * total
    tiles = vbuf.shape[0]
    from_blocks = (node_rows + halo_rows) // tile
    into_blocks = node_rows // tile
    cells = into_blocks * from_blocks
    chunk = width // chunks
    half = node_rows // 2
    across, beside = jnp.bitwise_xor(me_f, 1), jnp.bitwise_xor(me_f, 2)
    facing = jnp.bitwise_xor(me_f, 3)
    sides = (across, beside)
    halves = (pl.ds(0, half), pl.ds(half, half))

    def team_of(limit):
        return next(size for size in (8, 4, 2, 1) if size <= limit and dom_size % size == 0 and columns % (16 * size) == 0)

    teams = (team_of(2), team_of(8))
    share_rows = tuple(columns // size for size in teams)
    seats = tuple(lax.rem(me_d, size) for size in teams)
    nears = range(1, feat_size)
    paired = total & (total - 1) == 0

    def near_of(k):
        return jnp.bitwise_xor(me_f, k) if paired else lax.rem(me_f + k, feat_size)

    def spot_of(k):
        return jnp.bitwise_xor(me_d, dom_size - 1 - k) if paired else lax.rem(me_d + 1 + k, dom_size)

    def group_to(i):
        return near_of(feat_size - 1 - i)

    def group_from(i):
        return near_of(feat_size - 1 - i) if paired else lax.rem(me_f + 1 + i, feat_size)

    def spots_of(i):
        return dom_size - 1 if i == feat_size - 1 else dom_size

    def each_peer(visit):
        for i in range(feat_size):
            def step(k, carry):
                visit(group_to(i), spot_of(k))
                return carry

            lax.fori_loop(0, spots_of(i), step, 0)

    def slab_of(slab):
        return slice(slab * columns, (slab + 1) * columns)

    def share_in(kind, slab, owner):
        rows = share_rows[kind]
        return pl.ds(pl.multiple_of(slab * columns + owner * rows, rows), rows)

    def rows_of(peer, count):
        return pl.ds(pl.multiple_of(peer * count, count), count)

    def cols_of(c):
        return slice(c * chunk, (c + 1) * chunk)

    barrier = pltpu.get_barrier_semaphore()
    split = dom_size % 2 == 0 and dom_size > 2
    side = lax.rem(me_d, 2)
    sibling = me_d + 1 - 2 * side
    near_count = 2 * feat_size - 1
    far_count = total - 2 * feat_size

    def hail(where):
        pl.semaphore_signal(barrier, inc=1, device_id=where, device_id_type=MESH)

    def hail_far(k, carry):
        pair = lax.rem(lax.div(me_d, 2) + 1 + lax.rem(k, dom_size // 2 - 1), dom_size // 2)
        hail((lax.div(k, dom_size // 2 - 1), 2 * pair + 1))
        return carry

    if split:
        for k in nears:
            hail((near_of(k), me_d - side))

        @pl.when(side == 1)
        def _():
            hail((me_f, sibling))

        lax.fori_loop(0, feat_size * (dom_size // 2 - 1), hail_far, 0)
    else:
        each_peer(lambda group, spot: hail((group, spot)))

    def meet_near():
        if not split:
            pl.semaphore_wait(barrier, total - 1)
            return

        @pl.when(side == 0)
        def _():
            pl.semaphore_wait(barrier, near_count)
            pl.semaphore_signal(met.at[0], inc=1, device_id=(me_f, sibling), device_id_type=MESH)

        @pl.when(side == 1)
        def _():
            pl.semaphore_wait(met.at[0], 1)

    def meet_far():
        if not split:
            return

        @pl.when(side == 1)
        def _():
            pl.semaphore_wait(barrier, far_count)
            pl.semaphore_signal(met.at[1], inc=1, device_id=(me_f, sibling), device_id_type=MESH)

        @pl.when(side == 0)
        def _():
            pl.semaphore_wait(met.at[1], 1)

    places = [
        (rows_ref, rows_v), (count_ref, count_v), (from_ref, from_v), (into_ref, into_v), (live_ref, live_v),
        (vals_ref.at[0, 0], vbuf), (wn_ref, wnbuf.at[slab_of(0)]), (x_ref.at[me_f, 0], xown),
        (ws_ref, wsbuf.at[slab_of(0)]), (gain_ref, gain_v), (shift_ref, shift_v), (dh_ref.at[0, 0], dh_v),
        (x_ref.at[beside, 0, halves[0]], xside.at[0]), (x_ref.at[across, 0, halves[1]], xside.at[1]),
    ]
    local_copies = [pltpu.make_async_copy(a, b, local_sems.at[i]) for i, (a, b) in enumerate(places)]
    for copy in local_copies:
        copy.start()
    with jax.named_scope("s_meet"):
        meet_near()

    def settled(block, sem):
        pltpu.make_async_copy(block, block, sem).wait()

    def push(source, target, send_sem, recv_sem, where):
        pltpu.make_async_remote_copy(
            src_ref=source,
            dst_ref=target,
            send_sem=send_sem,
            recv_sem=recv_sem,
            device_id=where,
            device_id_type=MESH,
        ).start()

    weights = (wnbuf, wsbuf)

    def evens(kind):
        return range(2, teams[kind], 2)

    def shares(kind, count):
        return weights[kind].at[pl.ds(0, 2 * count * share_rows[kind])]

    def hand_on(kind, slab, shift, flip):
        place = weights[kind].at[share_in(kind, slab, jnp.bitwise_xor(seats[kind], shift))]
        mate = me_d - seats[kind] + jnp.bitwise_xor(seats[kind], flip)
        push(place, place, pass_send.at[kind], pass_recv.at[kind, 1 if flip == 1 else 0], (me_f, mate))

    def pass_first(kind):
        settled(shares(kind, 1), near_recv.at[kind])
        if teams[kind] > 1:
            for slab in (1, 2):
                for flip in (*evens(kind), 1):
                    hand_on(kind, slab, 0, flip)

    def pass_second(kind):
        if teams[kind] > 2:
            settled(shares(kind, teams[kind] // 2 - 1), pass_recv.at[kind, 0])
            for slab in (1, 2):
                for shift in evens(kind):
                    hand_on(kind, slab, shift, 1)

    def pass_done(kind):
        if teams[kind] > 1:
            settled(shares(kind, teams[kind] // 2), pass_recv.at[kind, 1])

    def pass_sent(kind):
        settled(shares(kind, 1), near_send.at[kind])
        if teams[kind] > 1:
            settled(shares(kind, teams[kind] - 1), pass_send.at[kind])

    def side_part(kind, h):
        weight = weights[kind]
        return (
            jnp.dot(xside[h], weight[slab_of(0)], preferred_element_type=f32)
            + jnp.dot(xin[h], weight[slab_of(1 + h)], preferred_element_type=f32)
        )

    def own_part(kind, h):
        weight = weights[kind]
        return (
            jnp.dot(xown[halves[h]], weight[slab_of(0)], preferred_element_type=f32)
            + jnp.dot(xin[2 + h], weight[slab_of(1 + h)], preferred_element_type=f32)
        )

    def send_part(kind, h):
        part_out[kind, halves[h]] = side_part(kind, h).astype(bf16)
        push(part_out.at[kind, halves[h]], part_in.at[kind, halves[h]],
             part_sems.at[0, kind], part_sems.at[1, kind], (sides[1 - h], me_d))

    with jax.named_scope("s_near"):
        for kind, source in enumerate((wn_ref, ws_ref)):
            for h in range(2):
                push(source.at[share_in(kind, 0, seats[kind])], weights[kind].at[share_in(kind, 1 + h, seats[kind])],
                     near_send.at[kind], near_recv.at[kind], (sides[h], me_d))
        for h in range(2):
            push(x_ref.at[facing, 0, halves[h]], xin.at[h], near_send.at[2], near_recv.at[2 + h], (sides[h], me_d))
        for h in range(2):
            push(x_ref.at[sides[h], 0, halves[h]], xin.at[2 + h], near_send.at[2], near_recv.at[4 + h], (sides[h], me_d))

    with jax.named_scope("s_pick"):
        for copy in local_copies[0:2]:
            copy.wait()
        pick[...] = selection(rows_v, count_v, node_rows)
    with jax.named_scope("s_tables"):
        for copy in local_copies[2:5]:
            copy.wait()
        order, ordered_key, last, found = tile_tables(from_v, into_v, live_v, from_blocks, cells)
        lists_v[...] = jnp.zeros_like(lists_v)
        lists_v[0:1, 0:tiles] = order
        lists_v[1:2, 0:tiles] = ordered_key
        lists_v[2:3, 0:cells] = last
        lists_v[3:4, 0:cells] = found
        to_scalars = pltpu.make_async_copy(lists_v, lists_s, local_sems.at[0])
        to_scalars.start()
    with jax.named_scope("s_lists"):
        to_scalars.wait()
        for copy in local_copies[5:]:
            copy.wait()

    def add_tile(r, running):
        earlier = lists_s[1, jnp.maximum(r - 1, 0)]
        running = jnp.where(lists_s[1, r] == earlier, running, 0.0) + vbuf[lists_s[0, r]].astype(f32)
        history[r] = running
        return running

    with jax.named_scope("s_addtile"):
        lax.fori_loop(0, tiles, add_tile, jnp.zeros((tile, tile), f32), unroll=2)
    with jax.named_scope("s_pass1"):
        pass_first(0)
    with jax.named_scope("s_far"):
        meet_far()
        pass_first(1)

    def settle_block(b):
        span = slice(b * tile, (b + 1) * tile)

        def settle(s, weight):
            spot = b * from_blocks + s
            value = history[jnp.maximum(lists_s[2, spot], 0)]
            value = jnp.where(lists_s[3, spot] > 0, value, 0.0)
            high = value.astype(bf16)
            lanes = pl.ds(pl.multiple_of(s * tile, tile), tile)
            ah[span, lanes] = high
            ah_t[lanes, span] = high.T
            return weight + value

        weight = lax.fori_loop(0, from_blocks, settle, jnp.zeros((tile, tile), f32))
        inverse_degree = 1.0 / (1.0 + jnp.sum(weight, axis=1, keepdims=True))
        scale_ref[span] = jnp.broadcast_to(inverse_degree, (tile, 128))

    for b in range(into_blocks):
        if b == into_blocks - 1:
            with jax.named_scope("s_wpart"):
                pass_done(0)
                for h in range(2):
                    settled(xin.at[h], near_recv.at[2 + h])
            with jax.named_scope("s_part"):
                for h in range(2):
                    send_part(0, h)
        with jax.named_scope("s_settle%d" % b):
            settle_block(b)
    with jax.named_scope("s_pass2"):
        pass_second(1)
    with jax.named_scope("s_wown"):
        for h in range(2):
            settled(xin.at[2 + h], near_recv.at[4 + h])
    with jax.named_scope("s_neigh"):
        for h in range(2):
            summed[halves[h]] = own_part(0, h)
    with jax.named_scope("s_wneigh"):
        settled(part_in.at[0], part_sems.at[1, 0])
    with jax.named_scope("s_round"):
        neigh[...] = (summed[...] + part_in[0].astype(f32)).astype(bf16)

    def send_group(source, target, recv_sems, send_sem, c, i):
        group = group_to(i)

        def start(k, carry):
            spot = spot_of(k)
            pltpu.make_async_remote_copy(
                src_ref=source.at[c, rows_of(group * dom_size + spot, slots)],
                dst_ref=target.at[c, rows_of(me, slots)],
                send_sem=send_sem,
                recv_sem=recv_sems.at[c, me_f],
                device_id=(group, spot),
                device_id_type=MESH,
            ).start()
            return carry

        lax.fori_loop(0, spots_of(i), start, 0)

    def wait_group(buffer, recv_sems, c, i):
        settled(buffer.at[c, pl.ds(0, spots_of(i) * slots)], recv_sems.at[c, group_from(i)])

    def send_stats(source, target, turn, c):
        def start(group, spot):
            pltpu.make_async_remote_copy(
                src_ref=source.at[c],
                dst_ref=target.at[c, me],
                send_sem=out_send.at[2 + turn],
                recv_sem=stat_recv.at[turn, c],
                device_id=(group, spot),
                device_id_type=MESH,
            ).start()

        each_peer(start)

    def wait_stats(target, turn, c):
        settled(target.at[c, pl.ds(0, total - 1)], stat_recv.at[turn, c])

    mine = rows_of(me, slots)
    with jax.named_scope("s_out"):
        for i in range(feat_size):
            span = rows_of(group_to(i), group_rows)
            picked = jnp.dot(pick[span], neigh[...], preferred_element_type=f32).astype(bf16)
            for c in range(chunks):
                outgoing[c, span] = picked[:, cols_of(c)]
            send_group(outgoing, halo, halo_recv, out_send.at[0], 0, i)
        for c in range(chunks):
            halo[c, mine] = outgoing[c, mine]
    with jax.named_scope("s_own"):
        pass_done(1)
        for h in range(2):
            send_part(1, h)
        summed[...] = jnp.dot(ah[:, 0:node_rows], neigh[...], preferred_element_type=f32)
        for h in range(2):
            own[halves[h]] = own_part(1, h)

    def turn_pick(s, carry):
        rows = rows_of(s, tile)
        pick_t[:, rows] = pick[rows, :].T
        return carry

    with jax.named_scope("s_turn"):
        lax.fori_loop(0, halo_rows // tile, turn_pick, 0)

    gain = gain_v[...].reshape(1, width)
    shift = shift_v[...].reshape(1, width)
    inverses = {}

    def send_rows(c, i):
        send_group(outgoing, halo, halo_recv, out_send.at[0], c, i)

    def take_rows(c, i):
        with jax.named_scope("s_halo%d%d" % (c, i)):
            group = group_from(i)
            edges = pl.ds(pl.multiple_of(node_rows + group * group_rows, tile), group_rows)
            wait_group(halo, halo_recv, c, i)
            summed[:, cols_of(c)] += jnp.dot(
                ah[:, edges], halo[c, rows_of(group, group_rows)], preferred_element_type=f32)

    def sum_pre(c):
        cols = cols_of(c)
        with jax.named_scope("s_wpre%d" % c):
            if c == 0:
                settled(part_in.at[1], part_sems.at[1, 1])
        with jax.named_scope("s_pre%d" % c):
            col_sum = jnp.zeros((1, chunk), f32)
            col_square = jnp.zeros((1, chunk), f32)
            for b in range(into_blocks):
                span = slice(b * tile, (b + 1) * tile)
                pre = own[span, cols] + part_in[1, span, cols].astype(f32) + summed[span, cols] * scale_ref[span]
                own[span, cols] = pre
                col_sum += jnp.sum(pre, axis=0, keepdims=True)
                col_square += jnp.sum(pre * pre, axis=0, keepdims=True)
            local_a[c, 0:1] = col_sum
            local_a[c, 1:2] = col_square
            first[c, me] = local_a[c]
            send_stats(local_a, first, 0, c)

    def activate(c):
        cols = cols_of(c)
        with jax.named_scope("s_stat1_%d" % c):
            wait_stats(first, 0, c)
        with jax.named_scope("s_act%d" % c):
            sums = jnp.sum(first[c], axis=0)
            mean = sums[0:1] / nodes
            variance = sums[1:2] / nodes - mean * mean
            inverse = 1.0 / jnp.sqrt(variance + epsilon)
            inverses[c] = inverse
            slope_sum = jnp.zeros((1, chunk), f32)
            product_sum = jnp.zeros((1, chunk), f32)
            for b in range(into_blocks):
                span = slice(b * tile, (b + 1) * tile)
                normed = (own[span, cols] - mean) * inverse
                act = gain[:, cols] * normed + shift[:, cols]
                logistic = jax.nn.sigmoid(act)
                hidden_ref[span, cols] = (act * logistic).astype(bf16)
                slope = dh_v[span, cols].astype(f32) * logistic * (1.0 + act * (1.0 - logistic))
                normed_buf[span, cols] = normed
                slope_buf[span, cols] = slope
                slope_sum += jnp.sum(slope, axis=0, keepdims=True)
                product_sum += jnp.sum(slope * normed, axis=0, keepdims=True)
            local_b[c, 0:1] = slope_sum
            local_b[c, 1:2] = product_sum
            second[c, me] = local_b[c]
            send_stats(local_b, second, 1, c)

    def send_back(c):
        cols = cols_of(c)
        with jax.named_scope("s_stat2_%d" % c):
            wait_stats(second, 1, c)
        with jax.named_scope("s_dpre%d" % c):
            sums = jnp.sum(second[c], axis=0)
            shift_grad = sums[0:1] / nodes
            gain_grad = sums[1:2] / nodes
            sgrad_ref[:, cols] = shift_grad
            ggrad_ref[:, cols] = gain_grad
            factor = gain[:, cols] * inverses[c]
            for b in range(into_blocks):
                span = slice(b * tile, (b + 1) * tile)
                dpre = factor * (slope_buf[span, cols] - shift_grad - normed_buf[span, cols] * gain_grad)
                dself_ref[span, cols] = dpre.astype(bf16)
                mg[span, cols] = (dpre * scale_ref[span]).astype(bf16)
        with jax.named_scope("s_back%d" % c):
            for i in range(feat_size):
                group = group_to(i)
                span = rows_of(group, group_rows)
                edges = pl.ds(pl.multiple_of(node_rows + group * group_rows, tile), group_rows)
                back_out[c, span] = jnp.dot(ah_t[edges], mg[:, cols], preferred_element_type=f32).astype(bf16)
                send_group(back_out, returned, halo_recv, out_send.at[1], c, i)
            returned[c, mine] = back_out[c, mine]

    steps = {"S": send_rows, "H": take_rows, "P": sum_pre, "A": activate, "B": send_back}
    for step in "S10 S11 S12 S13 H00 H01 H02 H03 P0 H10 H11 H12 H13 P1 A0 A1 B0 B1".split():
        steps[step[0]](*(int(digit) for digit in step[1:]))
    with jax.named_scope("s_dlocal"):
        summed[...] = jnp.dot(ah_t[0:node_rows], mg[...], preferred_element_type=f32)
    peers_rows = pl.ds(0, (total - 1) * slots)
    with jax.named_scope("s_sendw"):
        for kind in range(2):
            pass_sent(kind)
        settled(xin, near_send.at[2])
        for kind in range(2):
            settled(part_out.at[kind], part_sems.at[0, kind])
        settled(outgoing.at[:, peers_rows], out_send.at[0])
        settled(first.at[:, pl.ds(0, total - 1)], out_send.at[2])
        settled(second.at[:, pl.ds(0, total - 1)], out_send.at[3])
    for c in range(chunks):
        cols = cols_of(c)
        with jax.named_scope("s_gather%d" % c):
            for i in range(feat_size):
                span = rows_of(group_from(i), group_rows)
                wait_group(returned, halo_recv, c, i)
                gathered = jnp.dot(pick_t[:, span], returned[c, span], preferred_element_type=f32)
                if i < feat_size - 1:
                    summed[:, cols] += gathered
                else:
                    dneigh_ref[:, cols] = (summed[:, cols] + gathered).astype(bf16)
    settled(back_out.at[:, peers_rows], out_send.at[1])


def finish_kernel(hidden, d_self, d_neigh, gain_grad, shift_grad,
                  hidden_out, dself_out, dneigh_out, ggrad_out, sgrad_out, sems):
    pairs = ((hidden, hidden_out), (d_self, dself_out), (d_neigh, dneigh_out))
    copies = [pltpu.make_async_copy(a, b.at[0, 0], sems.at[i]) for i, (a, b) in enumerate(pairs)]
    for copy in copies:
        copy.start()
    ggrad_out[...] = gain_grad[...].reshape(ggrad_out.shape)
    sgrad_out[...] = shift_grad[...].reshape(sgrad_out.shape)
    for copy in copies:
        copy.wait()


def shards(feat_size, dom_size, features, w_self, w_neigh, gain, shift, d_hidden, send_rows, send_count,
           tile_src, tile_dst, tile_count, tile_vals):
    node_rows, columns = features.shape[2], features.shape[3]
    width = w_self.shape[1]
    tiles, tile = tile_vals.shape[2], tile_vals.shape[3]
    parts, slots = send_rows.shape[2], send_rows.shape[3]
    own_blocks = node_rows // tile
    halo_rows = parts * slots
    all_rows = node_rows + halo_rows
    cells = own_blocks * (all_rows // tile)
    list_lanes = -(-max(tiles, cells) // 128) * 128
    chunks = width // 128
    chunk = width // chunks
    dma = pltpu.SemaphoreType.DMA
    shape = jax.ShapeDtypeStruct
    i32 = jnp.int32
    results = pl.pallas_call(
        functools.partial(layer_kernel, feat_size, dom_size, tile, chunks),
        out_shape=(
            pltpu.VMEM((node_rows, width), bf16),
            pltpu.VMEM((node_rows, width), bf16),
            pltpu.VMEM((node_rows, width), bf16),
            pltpu.VMEM((1, width), f32),
            pltpu.VMEM((1, width), f32),
        ),
        in_specs=[HB] * 12,
        out_specs=(VM,) * 5,
        scratch_shapes=[
            pltpu.VMEM(send_rows.shape, i32),
            pltpu.VMEM(send_count.shape, i32),
            pltpu.VMEM(tile_src.shape, i32),
            pltpu.VMEM(tile_dst.shape, i32),
            pltpu.VMEM(tile_count.shape, i32),
            pltpu.VMEM(gain.shape, f32),
            pltpu.VMEM(shift.shape, f32),
            pltpu.VMEM((node_rows, width), bf16),
            pltpu.VMEM((node_rows, columns), bf16),
            pltpu.VMEM((2, node_rows // 2, columns), bf16),
            pltpu.VMEM((4, node_rows // 2, columns), bf16),
            pltpu.VMEM((3 * columns, width), bf16),
            pltpu.VMEM((3 * columns, width), bf16),
            pltpu.VMEM((2, node_rows, width), bf16),
            pltpu.VMEM((2, node_rows, width), bf16),
            pltpu.VMEM((node_rows, width), f32),
            pltpu.VMEM((node_rows, width), f32),
            pltpu.VMEM((node_rows, width), bf16),
            pltpu.VMEM((chunks, halo_rows, chunk), bf16),
            pltpu.VMEM((chunks, halo_rows, chunk), bf16),
            pltpu.VMEM((halo_rows, node_rows), bf16),
            pltpu.VMEM((node_rows, halo_rows), bf16),
            pltpu.VMEM((node_rows, all_rows), bf16),
            pltpu.VMEM((all_rows, node_rows), bf16),
            pltpu.VMEM((node_rows, width), bf16),
            pltpu.VMEM((chunks, halo_rows, chunk), bf16),
            pltpu.VMEM((chunks, halo_rows, chunk), bf16),
            pltpu.VMEM((node_rows, width), f32),
            pltpu.VMEM((node_rows, width), f32),
            pltpu.VMEM((chunks, parts, 2, chunk), f32),
            pltpu.VMEM((chunks, parts, 2, chunk), f32),
            pltpu.VMEM((chunks, 2, chunk), f32),
            pltpu.VMEM((chunks, 2, chunk), f32),
            pltpu.VMEM((node_rows, 128), f32),
            pltpu.VMEM((tiles, tile, tile), bf16),
            pltpu.VMEM((tiles, tile, tile), f32),
            pltpu.VMEM((8, list_lanes), i32),
            pltpu.SMEM((8, list_lanes), i32),
            dma((14,)), dma((3,)), dma((6,)), dma((2,)), dma((2, 2)), dma((2, 2)),
            dma((chunks, feat_size)), dma((2, chunks)), dma((4,)), pltpu.SemaphoreType.REGULAR((2,)),
        ],
        compiler_params=pltpu.CompilerParams(
            collective_id=0, has_side_effects=True, vmem_limit_bytes=58 * 1024 * 1024),
        name="layer",
    )(features, w_self, w_neigh, send_rows, send_count, tile_src, tile_dst, tile_count, tile_vals, gain, shift, d_hidden)
    kept = [pltpu.with_memory_space_constraint(result, pltpu.VMEM) for result in results]
    out_shape = (1, 1, node_rows, width)
    return pl.pallas_call(
        finish_kernel,
        out_shape=(shape(out_shape, bf16),) * 3 + (shape((width,), f32),) * 2,
        in_specs=[VM] * 5,
        out_specs=(HB,) * 3 + (VM,) * 2,
        scratch_shapes=[dma((3,))],
        name="finish",
    )(*kept)


def solution(mesh):
    in_specs = (
        P(None, "dom", None, "feat"),
        P("feat", None),
        P("feat", None),
        P(),
        P(),
        P("feat", "dom", None, None),
        P("feat", "dom", None, None),
        P("feat", "dom", None),
        P("feat", "dom", None),
        P("feat", "dom", None),
        P("feat", "dom"),
        P("feat", "dom", None, None, None),
    )
    out_specs = (
        P("feat", "dom", None, None),
        P("feat", "dom", None, None),
        P("feat", "dom", None, None),
        P(),
        P(),
    )
    body = functools.partial(shards, mesh.shape["feat"], mesh.shape["dom"])
    return jax.shard_map(body, mesh=mesh, in_specs=in_specs, out_specs=out_specs, check_vma=False)
```

```python
import functools

import jax
import jax.numpy as jnp
from jax import lax
from jax.experimental import pallas as pl
from jax.experimental.pallas import tpu as pltpu
from jax.sharding import PartitionSpec as P

epsilon = 1e-05
MESH = pl.DeviceIdType.MESH
VM = pl.BlockSpec(memory_space=pltpu.VMEM)
HB = pl.BlockSpec(memory_space=pltpu.HBM)
f32 = jnp.float32
bf16 = jnp.bfloat16


def selection(rows_ref, count_ref, node_rows):
    rows = rows_ref[0, 0]
    parts, slots = rows.shape
    counts = jnp.broadcast_to(count_ref[0], (slots, parts)).T
    live = lax.broadcasted_iota(jnp.int32, (parts, slots), 1) < counts
    wanted = jnp.where(live, rows, -1)
    nodes = lax.broadcasted_iota(jnp.int32, (parts, slots, node_rows), 2)
    picked = wanted[:, :, None] == nodes
    return jnp.where(picked, 1.0, 0.0).astype(bf16).reshape(parts * slots, node_rows)


def tile_tables(from_ref, into_ref, live_ref, from_blocks, cells):
    tiles = from_ref.shape[2]
    spare = cells

    def turned(row):
        return jnp.broadcast_to(row, (tiles, tiles)).T

    at = lax.broadcasted_iota(jnp.int32, (1, tiles), 1)
    key = jnp.where(at < live_ref[...], into_ref[0] * from_blocks + from_ref[0], spare)
    key_down = turned(key)
    down = lax.broadcasted_iota(jnp.int32, (tiles, tiles), 0)
    across = lax.broadcasted_iota(jnp.int32, (tiles, tiles), 1)
    before = (key_down < key) | ((key_down == key) & (down < across))
    rank = jnp.sum(jnp.where(before, 1, 0), axis=0, keepdims=True)
    lands = turned(rank) == across
    order = jnp.sum(jnp.where(lands, down, 0), axis=0, keepdims=True)
    ordered_key = jnp.sum(jnp.where(lands, key_down, 0), axis=0, keepdims=True)
    cell = lax.broadcasted_iota(jnp.int32, (tiles, cells), 1)
    key_cells = jnp.broadcast_to(key, (cells, tiles)).T
    last = jnp.sum(jnp.where(key_cells <= cell, 1, 0), axis=0, keepdims=True) - 1
    found = jnp.sum(jnp.where(key_cells == cell, 1, 0), axis=0, keepdims=True)
    return order, ordered_key, last, found


def layer_kernel(feat_size, dom_size, tile, chunks, x_ref, ws_ref, wn_ref, rows_ref, count_ref, from_ref, into_ref,
                 live_ref, vals_ref, gain_ref, shift_ref, dh_ref,
                 hidden_ref, dself_ref, dneigh_ref, ggrad_ref, sgrad_ref,
                 rows_v, count_v, from_v, into_v, live_v, gain_v, shift_v, dh_v,
                 xown, xside, xin, wnbuf, wsbuf, part_out, part_in, own, summed, neigh, halo, outgoing, pick, pick_t, ah, ah_t,
                 mg, back_out, returned, normed_buf, slope_buf, first, second, local_a, local_b,
                 scale_ref, vbuf, history, lists_v, lists_s,
                 local_sems, near_send, near_recv, pass_send, pass_recv, part_sems, halo_recv, stat_recv, out_send, met):
    me_f, me_d = lax.axis_index("feat"), lax.axis_index("dom")
    me = me_f * dom_size + me_d
    total = feat_size * dom_size
    node_rows = x_ref.shape[2]
    columns, width = wn_ref.shape
    slots = rows_ref.shape[3]
    group_rows = dom_size * slots
    halo_rows = total * slots
    nodes = node_rows * total
    tiles = vbuf.shape[0]
    from_blocks = (node_rows + halo_rows) // tile
    into_blocks = node_rows // tile
    cells = into_blocks * from_blocks
    chunk = width // chunks
    half = node_rows // 2
    across, beside = jnp.bitwise_xor(me_f, 1), jnp.bitwise_xor(me_f, 2)
    facing = jnp.bitwise_xor(me_f, 3)
    sides = (across, beside)
    halves = (pl.ds(0, half), pl.ds(half, half))

    def team_of(limit):
        return next(size for size in (8, 4, 2, 1) if size <= limit and dom_size % size == 0 and columns % (16 * size) == 0)

    teams = (team_of(2), team_of(8))
    share_rows = tuple(columns // size for size in teams)
    seats = tuple(lax.rem(me_d, size) for size in teams)
    nears = range(1, feat_size)
    paired = total & (total - 1) == 0

    def near_of(k):
        return jnp.bitwise_xor(me_f, k) if paired else lax.rem(me_f + k, feat_size)

    def spot_of(k):
        return jnp.bitwise_xor(me_d, dom_size - 1 - k) if paired else lax.rem(me_d + 1 + k, dom_size)

    def group_to(i):
        return near_of(feat_size - 1 - i)

    def group_from(i):
        return near_of(feat_size - 1 - i) if paired else lax.rem(me_f + 1 + i, feat_size)

    def spots_of(i):
        return dom_size - 1 if i == feat_size - 1 else dom_size

    def each_peer(visit):
        for i in range(feat_size):
            def step(k, carry):
                visit(group_to(i), spot_of(k))
                return carry

            lax.fori_loop(0, spots_of(i), step, 0)

    def slab_of(slab):
        return slice(slab * columns, (slab + 1) * columns)

    def share_in(kind, slab, owner):
        rows = share_rows[kind]
        return pl.ds(pl.multiple_of(slab * columns + owner * rows, rows), rows)

    def rows_of(peer, count):
        return pl.ds(pl.multiple_of(peer * count, count), count)

    def cols_of(c):
        return slice(c * chunk, (c + 1) * chunk)

    barrier = pltpu.get_barrier_semaphore()
    split = dom_size % 2 == 0 and dom_size > 2
    side = lax.rem(me_d, 2)
    sibling = me_d + 1 - 2 * side
    near_count = 2 * feat_size - 1
    far_count = total - 2 * feat_size

    def hail(where):
        pl.semaphore_signal(barrier, inc=1, device_id=where, device_id_type=MESH)

    def hail_far(k, carry):
        pair = lax.rem(lax.div(me_d, 2) + 1 + lax.rem(k, dom_size // 2 - 1), dom_size // 2)
        hail((lax.div(k, dom_size // 2 - 1), 2 * pair + 1))
        return carry

    if split:
        for k in nears:
            hail((near_of(k), me_d - side))

        @pl.when(side == 1)
        def _():
            hail((me_f, sibling))

        lax.fori_loop(0, feat_size * (dom_size // 2 - 1), hail_far, 0)
    else:
        each_peer(lambda group, spot: hail((group, spot)))

    def meet_near():
        if not split:
            pl.semaphore_wait(barrier, total - 1)
            return

        @pl.when(side == 0)
        def _():
            pl.semaphore_wait(barrier, near_count)
            pl.semaphore_signal(met.at[0], inc=1, device_id=(me_f, sibling), device_id_type=MESH)

        @pl.when(side == 1)
        def _():
            pl.semaphore_wait(met.at[0], 1)

    def meet_far():
        if not split:
            return

        @pl.when(side == 1)
        def _():
            pl.semaphore_wait(barrier, far_count)
            pl.semaphore_signal(met.at[1], inc=1, device_id=(me_f, sibling), device_id_type=MESH)

        @pl.when(side == 0)
        def _():
            pl.semaphore_wait(met.at[1], 1)

    places = [
        (rows_ref, rows_v, 0), (count_ref, count_v, 1), (from_ref, from_v, 2), (into_ref, into_v, 3), (live_ref, live_v, 4),
        (vals_ref.at[0, 0], vbuf, 5), (wn_ref, wnbuf.at[slab_of(0)], 6), (ws_ref, wsbuf.at[slab_of(0)], 6),
        (x_ref.at[me_f, 0], xown, 7), (x_ref.at[beside, 0, halves[0]], xside.at[0], 7),
        (x_ref.at[across, 0, halves[1]], xside.at[1], 7), (gain_ref, gain_v, 8), (shift_ref, shift_v, 9),
        (dh_ref.at[0, 0], dh_v, 10),
    ]
    for source, target, i in places:
        pltpu.make_async_copy(source, target, local_sems.at[i]).start()

    def settled(block, sem):
        pltpu.make_async_copy(block, block, sem).wait()

    with jax.named_scope("s_meet"):
        meet_near()

    def push(source, target, send_sem, recv_sem, where):
        pltpu.make_async_remote_copy(
            src_ref=source,
            dst_ref=target,
            send_sem=send_sem,
            recv_sem=recv_sem,
            device_id=where,
            device_id_type=MESH,
        ).start()

    weights = (wnbuf, wsbuf)

    def evens(kind):
        return range(2, teams[kind], 2)

    def shares(kind, count):
        return weights[kind].at[pl.ds(0, 2 * count * share_rows[kind])]

    def hand_on(kind, slab, shift, flip):
        place = weights[kind].at[share_in(kind, slab, jnp.bitwise_xor(seats[kind], shift))]
        mate = me_d - seats[kind] + jnp.bitwise_xor(seats[kind], flip)
        push(place, place, pass_send.at[kind], pass_recv.at[kind, 1 if flip == 1 else 0], (me_f, mate))

    def pass_first(kind):
        settled(shares(kind, 1), near_recv.at[kind])
        if teams[kind] > 1:
            for slab in (1, 2):
                for flip in (*evens(kind), 1):
                    hand_on(kind, slab, 0, flip)

    def pass_second(kind):
        if teams[kind] > 2:
            settled(shares(kind, teams[kind] // 2 - 1), pass_recv.at[kind, 0])
            for slab in (1, 2):
                for shift in evens(kind):
                    hand_on(kind, slab, shift, 1)

    def pass_done(kind):
        if teams[kind] > 1:
            settled(shares(kind, teams[kind] // 2), pass_recv.at[kind, 1])

    def pass_sent(kind):
        settled(shares(kind, 1), near_send.at[kind])
        if teams[kind] > 1:
            settled(shares(kind, teams[kind] - 1), pass_send.at[kind])

    def side_part(kind, h):
        weight = weights[kind]
        return (
            jnp.dot(xside[h], weight[slab_of(0)], preferred_element_type=f32)
            + jnp.dot(xin[h], weight[slab_of(1 + h)], preferred_element_type=f32)
        )

    def own_part(kind, h):
        weight = weights[kind]
        return (
            jnp.dot(xown[halves[h]], weight[slab_of(0)], preferred_element_type=f32)
            + jnp.dot(xin[2 + h], weight[slab_of(1 + h)], preferred_element_type=f32)
        )

    def send_part(kind, h):
        part_out[kind, halves[h]] = side_part(kind, h).astype(bf16)
        push(part_out.at[kind, halves[h]], part_in.at[kind, halves[h]],
             part_sems.at[0, kind], part_sems.at[1, kind], (sides[1 - h], me_d))

    with jax.named_scope("s_near"):
        for kind, source in enumerate((wn_ref, ws_ref)):
            for h in range(2):
                push(source.at[share_in(kind, 0, seats[kind])], weights[kind].at[share_in(kind, 1 + h, seats[kind])],
                     near_send.at[kind], near_recv.at[kind], (sides[h], me_d))
        for h in range(2):
            push(x_ref.at[facing, 0, halves[h]], xin.at[h], near_send.at[2], near_recv.at[2], (sides[h], me_d))
        for h in range(2):
            push(x_ref.at[sides[h], 0, halves[h]], xin.at[2 + h], near_send.at[2], near_recv.at[3], (sides[h], me_d))

    with jax.named_scope("s_pick"):
        settled(rows_v, local_sems.at[0])
        settled(count_v, local_sems.at[1])
        pick[...] = selection(rows_v, count_v, node_rows)
    with jax.named_scope("s_tables"):
        for i, block in ((2, from_v), (3, into_v), (4, live_v)):
            settled(block, local_sems.at[i])
        order, ordered_key, last, found = tile_tables(from_v, into_v, live_v, from_blocks, cells)
        lists_v[...] = jnp.zeros_like(lists_v)
        lists_v[0:1, 0:tiles] = order
        lists_v[1:2, 0:tiles] = ordered_key
        lists_v[2:3, 0:cells] = last
        lists_v[3:4, 0:cells] = found
        to_scalars = pltpu.make_async_copy(lists_v, lists_s, local_sems.at[0])
        to_scalars.start()
    with jax.named_scope("s_lists"):
        to_scalars.wait()
        both_slabs = wnbuf.at[pl.ds(0, 2 * columns)]
        for i, block in ((5, vbuf), (6, both_slabs), (7, xin), (8, gain_v), (9, shift_v), (10, dh_v)):
            settled(block, local_sems.at[i])

    def add_tile(r, running):
        earlier = lists_s[1, jnp.maximum(r - 1, 0)]
        running = jnp.where(lists_s[1, r] == earlier, running, 0.0) + vbuf[lists_s[0, r]].astype(f32)
        history[r] = running
        return running

    with jax.named_scope("s_addtile"):
        lax.fori_loop(0, tiles, add_tile, jnp.zeros((tile, tile), f32), unroll=2)
    with jax.named_scope("s_pass1"):
        pass_first(0)
    with jax.named_scope("s_far"):
        meet_far()
        pass_first(1)

    def settle_block(b):
        span = slice(b * tile, (b + 1) * tile)

        def settle(s, weight):
            spot = b * from_blocks + s
            value = history[jnp.maximum(lists_s[2, spot], 0)]
            value = jnp.where(lists_s[3, spot] > 0, value, 0.0)
            high = value.astype(bf16)
            lanes = pl.ds(pl.multiple_of(s * tile, tile), tile)
            ah[span, lanes] = high
            ah_t[lanes, span] = high.T
            return weight + value

        weight = lax.fori_loop(0, from_blocks, settle, jnp.zeros((tile, tile), f32))
        inverse_degree = 1.0 / (1.0 + jnp.sum(weight, axis=1, keepdims=True))
        scale_ref[span] = jnp.broadcast_to(inverse_degree, (tile, 128))

    for b in range(into_blocks):
        if b == into_blocks - 1:
            with jax.named_scope("s_wpart"):
                pass_done(0)
                settled(xin.at[pl.ds(0, 2)], near_recv.at[2])
            with jax.named_scope("s_part"):
                for h in range(2):
                    send_part(0, h)
        with jax.named_scope("s_settle%d" % b):
            settle_block(b)
    with jax.named_scope("s_pass2"):
        pass_second(1)
    with jax.named_scope("s_wown"):
        settled(xin.at[pl.ds(2, 2)], near_recv.at[3])
    with jax.named_scope("s_neigh"):
        for h in range(2):
            summed[halves[h]] = own_part(0, h)
    with jax.named_scope("s_wneigh"):
        settled(part_in.at[0], part_sems.at[1, 0])
    with jax.named_scope("s_round"):
        neigh[...] = (summed[...] + part_in[0].astype(f32)).astype(bf16)

    def send_group(source, target, recv_sems, send_sem, c, i):
        group = group_to(i)

        def start(k, carry):
            spot = spot_of(k)
            pltpu.make_async_remote_copy(
                src_ref=source.at[c, rows_of(group * dom_size + spot, slots)],
                dst_ref=target.at[c, rows_of(me, slots)],
                send_sem=send_sem,
                recv_sem=recv_sems.at[c, me_f],
                device_id=(group, spot),
                device_id_type=MESH,
            ).start()
            return carry

        lax.fori_loop(0, spots_of(i), start, 0)

    def wait_group(buffer, recv_sems, c, i):
        settled(buffer.at[c, pl.ds(0, spots_of(i) * slots)], recv_sems.at[c, group_from(i)])

    def send_stats(source, target, turn, c):
        def start(group, spot):
            pltpu.make_async_remote_copy(
                src_ref=source.at[c],
                dst_ref=target.at[c, me],
                send_sem=out_send.at[2 + turn],
                recv_sem=stat_recv.at[turn, c],
                device_id=(group, spot),
                device_id_type=MESH,
            ).start()

        each_peer(start)

    def wait_stats(target, turn, c):
        settled(target.at[c, pl.ds(0, total - 1)], stat_recv.at[turn, c])

    mine = rows_of(me, slots)
    with jax.named_scope("s_out"):
        for i in range(feat_size):
            span = rows_of(group_to(i), group_rows)
            picked = jnp.dot(pick[span], neigh[...], preferred_element_type=f32).astype(bf16)
            for c in range(chunks):
                outgoing[c, span] = picked[:, cols_of(c)]
            send_group(outgoing, halo, halo_recv, out_send.at[0], 0, i)
        for c in range(chunks):
            halo[c, mine] = outgoing[c, mine]
    with jax.named_scope("s_own"):
        pass_done(1)
        for h in range(2):
            send_part(1, h)
        summed[...] = jnp.dot(ah[:, 0:node_rows], neigh[...], preferred_element_type=f32)
        for h in range(2):
            own[halves[h]] = own_part(1, h)

    def turn_pick(s, carry):
        rows = rows_of(s, tile)
        pick_t[:, rows] = pick[rows, :].T
        return carry

    with jax.named_scope("s_turn"):
        lax.fori_loop(0, halo_rows // tile, turn_pick, 0)

    gain = gain_v[...].reshape(1, width)
    shift = shift_v[...].reshape(1, width)
    inverses = {}

    def send_rows(c, i):
        send_group(outgoing, halo, halo_recv, out_send.at[0], c, i)

    def take_rows(c, i):
        with jax.named_scope("s_halo%d%d" % (c, i)):
            group = group_from(i)
            edges = pl.ds(pl.multiple_of(node_rows + group * group_rows, tile), group_rows)
            wait_group(halo, halo_recv, c, i)
            summed[:, cols_of(c)] += jnp.dot(
                ah[:, edges], halo[c, rows_of(group, group_rows)], preferred_element_type=f32)

    def sum_pre(c):
        cols = cols_of(c)
        with jax.named_scope("s_wpre%d" % c):
            if c == 0:
                settled(part_in.at[1], part_sems.at[1, 1])
        with jax.named_scope("s_pre%d" % c):
            col_sum = jnp.zeros((1, chunk), f32)
            col_square = jnp.zeros((1, chunk), f32)
            for b in range(into_blocks):
                span = slice(b * tile, (b + 1) * tile)
                pre = own[span, cols] + part_in[1, span, cols].astype(f32) + summed[span, cols] * scale_ref[span]
                own[span, cols] = pre
                col_sum += jnp.sum(pre, axis=0, keepdims=True)
                col_square += jnp.sum(pre * pre, axis=0, keepdims=True)
            local_a[c, 0:1] = col_sum
            local_a[c, 1:2] = col_square
            first[c, me] = local_a[c]
            send_stats(local_a, first, 0, c)

    def activate(c):
        cols = cols_of(c)
        with jax.named_scope("s_stat1_%d" % c):
            wait_stats(first, 0, c)
        with jax.named_scope("s_act%d" % c):
            sums = jnp.sum(first[c], axis=0)
            mean = sums[0:1] / nodes
            variance = sums[1:2] / nodes - mean * mean
            inverse = 1.0 / jnp.sqrt(variance + epsilon)
            inverses[c] = inverse
            slope_sum = jnp.zeros((1, chunk), f32)
            product_sum = jnp.zeros((1, chunk), f32)
            for b in range(into_blocks):
                span = slice(b * tile, (b + 1) * tile)
                normed = (own[span, cols] - mean) * inverse
                act = gain[:, cols] * normed + shift[:, cols]
                logistic = jax.nn.sigmoid(act)
                hidden_ref[span, cols] = (act * logistic).astype(bf16)
                slope = dh_v[span, cols].astype(f32) * logistic * (1.0 + act * (1.0 - logistic))
                normed_buf[span, cols] = normed
                slope_buf[span, cols] = slope
                slope_sum += jnp.sum(slope, axis=0, keepdims=True)
                product_sum += jnp.sum(slope * normed, axis=0, keepdims=True)
            local_b[c, 0:1] = slope_sum
            local_b[c, 1:2] = product_sum
            second[c, me] = local_b[c]
            send_stats(local_b, second, 1, c)

    def send_back(c):
        cols = cols_of(c)
        with jax.named_scope("s_stat2_%d" % c):
            wait_stats(second, 1, c)
        with jax.named_scope("s_dpre%d" % c):
            sums = jnp.sum(second[c], axis=0)
            shift_grad = sums[0:1] / nodes
            gain_grad = sums[1:2] / nodes
            sgrad_ref[:, cols] = shift_grad
            ggrad_ref[:, cols] = gain_grad
            factor = gain[:, cols] * inverses[c]
            for b in range(into_blocks):
                span = slice(b * tile, (b + 1) * tile)
                dpre = factor * (slope_buf[span, cols] - shift_grad - normed_buf[span, cols] * gain_grad)
                dself_ref[span, cols] = dpre.astype(bf16)
                mg[span, cols] = (dpre * scale_ref[span]).astype(bf16)
        with jax.named_scope("s_back%d" % c):
            for i in range(feat_size):
                group = group_to(i)
                span = rows_of(group, group_rows)
                edges = pl.ds(pl.multiple_of(node_rows + group * group_rows, tile), group_rows)
                back_out[c, span] = jnp.dot(ah_t[edges], mg[:, cols], preferred_element_type=f32).astype(bf16)
                send_group(back_out, returned, halo_recv, out_send.at[1], c, i)
            returned[c, mine] = back_out[c, mine]

    steps = {"S": send_rows, "H": take_rows, "P": sum_pre, "A": activate, "B": send_back}
    for step in "S10 S11 S12 S13 H00 H01 H02 H03 P0 H10 H11 H12 H13 P1 A0 A1 B0 B1".split():
        steps[step[0]](*(int(digit) for digit in step[1:]))
    with jax.named_scope("s_dlocal"):
        summed[...] = jnp.dot(ah_t[0:node_rows], mg[...], preferred_element_type=f32)
    peers_rows = pl.ds(0, (total - 1) * slots)
    with jax.named_scope("s_sendw"):
        for kind in range(2):
            pass_sent(kind)
        settled(xin, near_send.at[2])
        for kind in range(2):
            settled(part_out.at[kind], part_sems.at[0, kind])
        settled(outgoing.at[:, peers_rows], out_send.at[0])
        settled(first.at[:, pl.ds(0, total - 1)], out_send.at[2])
        settled(second.at[:, pl.ds(0, total - 1)], out_send.at[3])
    for c in range(chunks):
        cols = cols_of(c)
        with jax.named_scope("s_gather%d" % c):
            for i in range(feat_size):
                span = rows_of(group_from(i), group_rows)
                wait_group(returned, halo_recv, c, i)
                gathered = jnp.dot(pick_t[:, span], returned[c, span], preferred_element_type=f32)
                if i < feat_size - 1:
                    summed[:, cols] += gathered
                else:
                    dneigh_ref[:, cols] = (summed[:, cols] + gathered).astype(bf16)
    settled(back_out.at[:, peers_rows], out_send.at[1])


def finish_kernel(hidden, d_self, d_neigh, gain_grad, shift_grad,
                  hidden_out, dself_out, dneigh_out, ggrad_out, sgrad_out, flat_gain, flat_shift, sems):
    blocks = ((hidden, hidden_out.at[0, 0]), (d_self, dself_out.at[0, 0]), (d_neigh, dneigh_out.at[0, 0]))
    rows = ((flat_gain, ggrad_out), (flat_shift, sgrad_out))
    copies = [pltpu.make_async_copy(a, b, sems.at[i]) for i, (a, b) in enumerate(blocks + rows)]
    for copy in copies[:3]:
        copy.start()
    flat_gain[...] = gain_grad[...].reshape(flat_gain.shape)
    flat_shift[...] = shift_grad[...].reshape(flat_shift.shape)
    for copy in copies[3:]:
        copy.start()
    for copy in copies:
        copy.wait()


def shards(feat_size, dom_size, features, w_self, w_neigh, gain, shift, d_hidden, send_rows, send_count,
           tile_src, tile_dst, tile_count, tile_vals):
    node_rows, columns = features.shape[2], features.shape[3]
    width = w_self.shape[1]
    tiles, tile = tile_vals.shape[2], tile_vals.shape[3]
    parts, slots = send_rows.shape[2], send_rows.shape[3]
    own_blocks = node_rows // tile
    halo_rows = parts * slots
    all_rows = node_rows + halo_rows
    cells = own_blocks * (all_rows // tile)
    list_lanes = -(-max(tiles, cells) // 128) * 128
    chunks = width // 128
    chunk = width // chunks
    dma = pltpu.SemaphoreType.DMA
    shape = jax.ShapeDtypeStruct
    i32 = jnp.int32
    results = pl.pallas_call(
        functools.partial(layer_kernel, feat_size, dom_size, tile, chunks),
        out_shape=(
            pltpu.VMEM((node_rows, width), bf16),
            pltpu.VMEM((node_rows, width), bf16),
            pltpu.VMEM((node_rows, width), bf16),
            pltpu.VMEM((1, width), f32),
            pltpu.VMEM((1, width), f32),
        ),
        in_specs=[HB] * 12,
        out_specs=(VM,) * 5,
        scratch_shapes=[
            pltpu.VMEM(send_rows.shape, i32),
            pltpu.VMEM(send_count.shape, i32),
            pltpu.VMEM(tile_src.shape, i32),
            pltpu.VMEM(tile_dst.shape, i32),
            pltpu.VMEM(tile_count.shape, i32),
            pltpu.VMEM(gain.shape, f32),
            pltpu.VMEM(shift.shape, f32),
            pltpu.VMEM((node_rows, width), bf16),
            pltpu.VMEM((node_rows, columns), bf16),
            pltpu.VMEM((2, node_rows // 2, columns), bf16),
            pltpu.VMEM((4, node_rows // 2, columns), bf16),
            pltpu.VMEM((3 * columns, width), bf16),
            pltpu.VMEM((3 * columns, width), bf16),
            pltpu.VMEM((2, node_rows, width), bf16),
            pltpu.VMEM((2, node_rows, width), bf16),
            pltpu.VMEM((node_rows, width), f32),
            pltpu.VMEM((node_rows, width), f32),
            pltpu.VMEM((node_rows, width), bf16),
            pltpu.VMEM((chunks, halo_rows, chunk), bf16),
            pltpu.VMEM((chunks, halo_rows, chunk), bf16),
            pltpu.VMEM((halo_rows, node_rows), bf16),
            pltpu.VMEM((node_rows, halo_rows), bf16),
            pltpu.VMEM((node_rows, all_rows), bf16),
            pltpu.VMEM((all_rows, node_rows), bf16),
            pltpu.VMEM((node_rows, width), bf16),
            pltpu.VMEM((chunks, halo_rows, chunk), bf16),
            pltpu.VMEM((chunks, halo_rows, chunk), bf16),
            pltpu.VMEM((node_rows, width), f32),
            pltpu.VMEM((node_rows, width), f32),
            pltpu.VMEM((chunks, parts, 2, chunk), f32),
            pltpu.VMEM((chunks, parts, 2, chunk), f32),
            pltpu.VMEM((chunks, 2, chunk), f32),
            pltpu.VMEM((chunks, 2, chunk), f32),
            pltpu.VMEM((node_rows, 128), f32),
            pltpu.VMEM((tiles, tile, tile), bf16),
            pltpu.VMEM((tiles, tile, tile), f32),
            pltpu.VMEM((8, list_lanes), i32),
            pltpu.SMEM((8, list_lanes), i32),
            dma((11,)), dma((3,)), dma((4,)), dma((2,)), dma((2, 2)), dma((2, 2)),
            dma((chunks, feat_size)), dma((2, chunks)), dma((4,)), pltpu.SemaphoreType.REGULAR((2,)),
        ],
        compiler_params=pltpu.CompilerParams(
            collective_id=0, has_side_effects=True, vmem_limit_bytes=58 * 1024 * 1024),
        name="layer",
    )(features, w_self, w_neigh, send_rows, send_count, tile_src, tile_dst, tile_count, tile_vals, gain, shift, d_hidden)
    kept = [pltpu.with_memory_space_constraint(result, pltpu.VMEM) for result in results]
    out_shape = (1, 1, node_rows, width)
    return pl.pallas_call(
        finish_kernel,
        out_shape=(shape(out_shape, bf16),) * 3 + (shape((width,), f32),) * 2,
        in_specs=[VM] * 5,
        out_specs=(HB,) * 5,
        scratch_shapes=[pltpu.VMEM((width,), f32), pltpu.VMEM((width,), f32), dma((5,))],
        name="finish",
    )(*kept)


def solution(mesh):
    in_specs = (
        P(None, "dom", None, "feat"),
        P("feat", None),
        P("feat", None),
        P(),
        P(),
        P("feat", "dom", None, None),
        P("feat", "dom", None, None),
        P("feat", "dom", None),
        P("feat", "dom", None),
        P("feat", "dom", None),
        P("feat", "dom"),
        P("feat", "dom", None, None, None),
    )
    out_specs = (
        P("feat", "dom", None, None),
        P("feat", "dom", None, None),
        P("feat", "dom", None, None),
        P(),
        P(),
    )
    body = functools.partial(shards, mesh.shape["feat"], mesh.shape["dom"])
    return jax.shard_map(body, mesh=mesh, in_specs=in_specs, out_specs=out_specs, check_vma=False)
```

```python
import functools

import jax
import jax.numpy as jnp
from jax import lax
from jax.experimental import pallas as pl
from jax.experimental.pallas import tpu as pltpu
from jax.sharding import PartitionSpec as P

epsilon = 1e-05
MESH = pl.DeviceIdType.MESH
VM = pl.BlockSpec(memory_space=pltpu.VMEM)
HB = pl.BlockSpec(memory_space=pltpu.HBM)
f32 = jnp.float32
bf16 = jnp.bfloat16


def selection(rows_ref, count_ref, node_rows):
    rows = rows_ref[0, 0]
    parts, slots = rows.shape
    counts = jnp.broadcast_to(count_ref[0], (slots, parts)).T
    live = lax.broadcasted_iota(jnp.int32, (parts, slots), 1) < counts
    wanted = jnp.where(live, rows, -1)
    nodes = lax.broadcasted_iota(jnp.int32, (parts, slots, node_rows), 2)
    picked = wanted[:, :, None] == nodes
    return jnp.where(picked, 1.0, 0.0).astype(bf16).reshape(parts * slots, node_rows)


def tile_tables(from_ref, into_ref, live_ref, from_blocks, cells):
    tiles = from_ref.shape[2]
    spare = cells

    def turned(row):
        return jnp.broadcast_to(row, (tiles, tiles)).T

    at = lax.broadcasted_iota(jnp.int32, (1, tiles), 1)
    key = jnp.where(at < live_ref[...], into_ref[0] * from_blocks + from_ref[0], spare)
    key_down = turned(key)
    down = lax.broadcasted_iota(jnp.int32, (tiles, tiles), 0)
    across = lax.broadcasted_iota(jnp.int32, (tiles, tiles), 1)
    before = (key_down < key) | ((key_down == key) & (down < across))
    rank = jnp.sum(jnp.where(before, 1, 0), axis=0, keepdims=True)
    lands = turned(rank) == across
    order = jnp.sum(jnp.where(lands, down, 0), axis=0, keepdims=True)
    ordered_key = jnp.sum(jnp.where(lands, key_down, 0), axis=0, keepdims=True)
    cell = lax.broadcasted_iota(jnp.int32, (tiles, cells), 1)
    key_cells = jnp.broadcast_to(key, (cells, tiles)).T
    last = jnp.sum(jnp.where(key_cells <= cell, 1, 0), axis=0, keepdims=True) - 1
    found = jnp.sum(jnp.where(key_cells == cell, 1, 0), axis=0, keepdims=True)
    return order, ordered_key, last, found


def layer_kernel(feat_size, dom_size, tile, chunks, x_ref, ws_ref, wn_ref, rows_ref, count_ref, from_ref, into_ref,
                 live_ref, vals_ref, gain_ref, shift_ref, dh_ref,
                 hidden_ref, dself_ref, dneigh_ref, ggrad_ref, sgrad_ref,
                 rows_v, count_v, from_v, into_v, live_v, gain_v, shift_v, dh_v,
                 xown, xside, xin, wnbuf, wsbuf, part_out, part_in, own, summed, neigh, halo, outgoing, pick, pick_t, ah, ah_t,
                 mg, back_out, returned, normed_buf, slope_buf, first, second, local_a, local_b,
                 scale_ref, vbuf, history, lists_v, lists_s,
                 local_sems, near_send, near_recv, pass_send, pass_recv, part_sems, halo_recv, stat_recv, out_send, met):
    me_f, me_d = lax.axis_index("feat"), lax.axis_index("dom")
    me = me_f * dom_size + me_d
    total = feat_size * dom_size
    node_rows = x_ref.shape[2]
    columns, width = wn_ref.shape
    slots = rows_ref.shape[3]
    group_rows = dom_size * slots
    halo_rows = total * slots
    nodes = node_rows * total
    tiles = vbuf.shape[0]
    from_blocks = (node_rows + halo_rows) // tile
    into_blocks = node_rows // tile
    cells = into_blocks * from_blocks
    chunk = width // chunks
    half = node_rows // 2
    across, beside = jnp.bitwise_xor(me_f, 1), jnp.bitwise_xor(me_f, 2)
    facing = jnp.bitwise_xor(me_f, 3)
    sides = (across, beside)
    halves = (pl.ds(0, half), pl.ds(half, half))

    def team_of(limit):
        return next(size for size in (8, 4, 2, 1) if size <= limit and dom_size % size == 0 and columns % (16 * size) == 0)

    teams = (team_of(2), team_of(8))
    share_rows = tuple(columns // size for size in teams)
    seats = tuple(lax.rem(me_d, size) for size in teams)
    nears = range(1, feat_size)
    paired = total & (total - 1) == 0

    def near_of(k):
        return jnp.bitwise_xor(me_f, k) if paired else lax.rem(me_f + k, feat_size)

    def spot_of(k):
        return jnp.bitwise_xor(me_d, dom_size - 1 - k) if paired else lax.rem(me_d + 1 + k, dom_size)

    def group_to(i):
        return near_of(feat_size - 1 - i)

    def group_from(i):
        return near_of(feat_size - 1 - i) if paired else lax.rem(me_f + 1 + i, feat_size)

    def spots_of(i):
        return dom_size - 1 if i == feat_size - 1 else dom_size

    def each_peer(visit):
        for i in range(feat_size):
            def step(k, carry):
                visit(group_to(i), spot_of(k))
                return carry

            lax.fori_loop(0, spots_of(i), step, 0)

    def slab_of(slab):
        return slice(slab * columns, (slab + 1) * columns)

    def share_in(kind, slab, owner):
        rows = share_rows[kind]
        return pl.ds(pl.multiple_of(slab * columns + owner * rows, rows), rows)

    def rows_of(peer, count):
        return pl.ds(pl.multiple_of(peer * count, count), count)

    def cols_of(c):
        return slice(c * chunk, (c + 1) * chunk)

    barrier = pltpu.get_barrier_semaphore()
    split = dom_size % 2 == 0
    side = lax.rem(me_d, 2)
    sibling = me_d + 1 - 2 * side
    pairs = dom_size // 2
    role = 2 * me_f + side
    proxy, keeper = 0, 1

    def hail(where):
        pl.semaphore_signal(barrier, inc=1, device_id=where, device_id_type=MESH)

    def hail_keeper(k, carry):
        hail((0, 2 * lax.rem(lax.div(me_d, 2) + 1 + k, pairs) + 1))
        return carry

    if split:
        for other in sides:
            hail((other, me_d - side * (1 - jnp.minimum(other, 1))))

        @pl.when(role != proxy)
        def _():
            hail((me_f, sibling))

        lax.fori_loop(0, pairs - 1, hail_keeper, 0)

        @pl.when(role != keeper)
        def _():
            hail((0, me_d - side + 1))
    else:
        each_peer(lambda group, spot: hail((group, spot)))

    def meet_near():
        if not split:
            pl.semaphore_wait(barrier, total - 1)
            return

        @pl.when(role > keeper)
        def _():
            pl.semaphore_wait(barrier, 3)

        @pl.when(role == proxy)
        def _():
            pl.semaphore_wait(barrier, 5)
            pl.semaphore_signal(met.at[0], inc=1, device_id=(me_f, sibling), device_id_type=MESH)

        @pl.when(role == keeper)
        def _():
            pl.semaphore_wait(met.at[0], 1)

    def meet_far():
        if not split:
            return

        @pl.when(role == keeper)
        def _():
            pl.semaphore_wait(barrier, total - 1)
            for group in range(feat_size):
                for core in range(2):
                    if (group, core) != (0, 1):
                        where = (group, me_d - side + core)
                        pl.semaphore_signal(met.at[1], inc=1, device_id=where, device_id_type=MESH)

        @pl.when(role != keeper)
        def _():
            pl.semaphore_wait(met.at[1], 1)

    places = [
        (rows_ref, rows_v, 0), (count_ref, count_v, 1), (from_ref, from_v, 2), (into_ref, into_v, 3), (live_ref, live_v, 4),
        (vals_ref.at[0, 0], vbuf, 5), (wn_ref, wnbuf.at[slab_of(0)], 6), (ws_ref, wsbuf.at[slab_of(0)], 6),
        (x_ref.at[me_f, 0], xown, 7), (x_ref.at[beside, 0, halves[0]], xside.at[0], 7),
        (x_ref.at[across, 0, halves[1]], xside.at[1], 7), (gain_ref, gain_v, 8), (shift_ref, shift_v, 9),
        (dh_ref.at[0, 0], dh_v, 10),
    ]
    for source, target, i in places:
        pltpu.make_async_copy(source, target, local_sems.at[i]).start()

    def settled(block, sem):
        pltpu.make_async_copy(block, block, sem).wait()

    with jax.named_scope("s_meet"):
        meet_near()

    def push(source, target, send_sem, recv_sem, where):
        pltpu.make_async_remote_copy(
            src_ref=source,
            dst_ref=target,
            send_sem=send_sem,
            recv_sem=recv_sem,
            device_id=where,
            device_id_type=MESH,
        ).start()

    weights = (wnbuf, wsbuf)

    def evens(kind):
        return range(2, teams[kind], 2)

    def shares(kind, count):
        return weights[kind].at[pl.ds(0, 2 * count * share_rows[kind])]

    def hand_on(kind, slab, shift, flip):
        place = weights[kind].at[share_in(kind, slab, jnp.bitwise_xor(seats[kind], shift))]
        mate = me_d - seats[kind] + jnp.bitwise_xor(seats[kind], flip)
        push(place, place, pass_send.at[kind], pass_recv.at[kind, 1 if flip == 1 else 0], (me_f, mate))

    def pass_first(kind):
        settled(shares(kind, 1), near_recv.at[kind])
        if teams[kind] > 1:
            for slab in (1, 2):
                for flip in (*evens(kind), 1):
                    hand_on(kind, slab, 0, flip)

    def pass_second(kind):
        if teams[kind] > 2:
            settled(shares(kind, teams[kind] // 2 - 1), pass_recv.at[kind, 0])
            for slab in (1, 2):
                for shift in evens(kind):
                    hand_on(kind, slab, shift, 1)

    def pass_done(kind):
        if teams[kind] > 1:
            settled(shares(kind, teams[kind] // 2), pass_recv.at[kind, 1])

    def pass_sent(kind):
        settled(shares(kind, 1), near_send.at[kind])
        if teams[kind] > 1:
            settled(shares(kind, teams[kind] - 1), pass_send.at[kind])

    def side_part(kind, h):
        weight = weights[kind]
        return (
            jnp.dot(xside[h], weight[slab_of(0)], preferred_element_type=f32)
            + jnp.dot(xin[h], weight[slab_of(1 + h)], preferred_element_type=f32)
        )

    def own_part(kind, h):
        weight = weights[kind]
        return (
            jnp.dot(xown[halves[h]], weight[slab_of(0)], preferred_element_type=f32)
            + jnp.dot(xin[2 + h], weight[slab_of(1 + h)], preferred_element_type=f32)
        )

    def send_part(kind, h):
        part_out[kind, halves[h]] = side_part(kind, h).astype(bf16)
        push(part_out.at[kind, halves[h]], part_in.at[kind, halves[h]],
             part_sems.at[0, kind], part_sems.at[1, kind], (sides[1 - h], me_d))

    with jax.named_scope("s_near"):
        for kind, source in enumerate((wn_ref, ws_ref)):
            for h in range(2):
                push(source.at[share_in(kind, 0, seats[kind])], weights[kind].at[share_in(kind, 1 + h, seats[kind])],
                     near_send.at[kind], near_recv.at[kind], (sides[h], me_d))
        for h in range(2):
            push(x_ref.at[facing, 0, halves[h]], xin.at[h], near_send.at[2], near_recv.at[2], (sides[h], me_d))
        for h in range(2):
            push(x_ref.at[sides[h], 0, halves[h]], xin.at[2 + h], near_send.at[2], near_recv.at[3], (sides[h], me_d))

    with jax.named_scope("s_pick"):
        settled(rows_v, local_sems.at[0])
        settled(count_v, local_sems.at[1])
        pick[...] = selection(rows_v, count_v, node_rows)
    with jax.named_scope("s_tables"):
        for i, block in ((2, from_v), (3, into_v), (4, live_v)):
            settled(block, local_sems.at[i])
        order, ordered_key, last, found = tile_tables(from_v, into_v, live_v, from_blocks, cells)
        lists_v[...] = jnp.zeros_like(lists_v)
        lists_v[0:1, 0:tiles] = order
        lists_v[1:2, 0:tiles] = ordered_key
        lists_v[2:3, 0:cells] = last
        lists_v[3:4, 0:cells] = found
        to_scalars = pltpu.make_async_copy(lists_v, lists_s, local_sems.at[0])
        to_scalars.start()
    with jax.named_scope("s_lists"):
        to_scalars.wait()
        both_slabs = wnbuf.at[pl.ds(0, 2 * columns)]
        for i, block in ((5, vbuf), (6, both_slabs), (7, xin), (8, gain_v), (9, shift_v), (10, dh_v)):
            settled(block, local_sems.at[i])

    def add_tile(r, running):
        earlier = lists_s[1, jnp.maximum(r - 1, 0)]
        running = jnp.where(lists_s[1, r] == earlier, running, 0.0) + vbuf[lists_s[0, r]].astype(f32)
        history[r] = running
        return running

    with jax.named_scope("s_addtile"):
        lax.fori_loop(0, tiles, add_tile, jnp.zeros((tile, tile), f32), unroll=2)
    with jax.named_scope("s_pass1"):
        pass_first(0)
    with jax.named_scope("s_far"):
        meet_far()
        pass_first(1)

    def settle_block(b):
        span = slice(b * tile, (b + 1) * tile)

        def settle(s, weight):
            spot = b * from_blocks + s
            value = history[jnp.maximum(lists_s[2, spot], 0)]
            value = jnp.where(lists_s[3, spot] > 0, value, 0.0)
            high = value.astype(bf16)
            lanes = pl.ds(pl.multiple_of(s * tile, tile), tile)
            ah[span, lanes] = high
            ah_t[lanes, span] = high.T
            return weight + value

        weight = lax.fori_loop(0, from_blocks, settle, jnp.zeros((tile, tile), f32))
        inverse_degree = 1.0 / (1.0 + jnp.sum(weight, axis=1, keepdims=True))
        scale_ref[span] = jnp.broadcast_to(inverse_degree, (tile, 128))

    for b in range(into_blocks):
        if b == into_blocks - 1:
            with jax.named_scope("s_wpart"):
                pass_done(0)
                settled(xin.at[pl.ds(0, 2)], near_recv.at[2])
            with jax.named_scope("s_part"):
                for h in range(2):
                    send_part(0, h)
        with jax.named_scope("s_settle%d" % b):
            settle_block(b)
    with jax.named_scope("s_pass2"):
        pass_second(1)
    with jax.named_scope("s_wown"):
        settled(xin.at[pl.ds(2, 2)], near_recv.at[3])
    with jax.named_scope("s_neigh"):
        for h in range(2):
            summed[halves[h]] = own_part(0, h)
    with jax.named_scope("s_wneigh"):
        settled(part_in.at[0], part_sems.at[1, 0])
    with jax.named_scope("s_round"):
        neigh[...] = (summed[...] + part_in[0].astype(f32)).astype(bf16)

    def send_group(source, target, recv_sems, send_sem, c, i):
        group = group_to(i)

        def start(k, carry):
            spot = spot_of(k)
            pltpu.make_async_remote_copy(
                src_ref=source.at[c, rows_of(group * dom_size + spot, slots)],
                dst_ref=target.at[c, rows_of(me, slots)],
                send_sem=send_sem,
                recv_sem=recv_sems.at[c, me_f],
                device_id=(group, spot),
                device_id_type=MESH,
            ).start()
            return carry

        lax.fori_loop(0, spots_of(i), start, 0)

    def wait_group(buffer, recv_sems, c, i):
        settled(buffer.at[c, pl.ds(0, spots_of(i) * slots)], recv_sems.at[c, group_from(i)])

    def send_stats(source, target, turn, c):
        def start(group, spot):
            pltpu.make_async_remote_copy(
                src_ref=source.at[c],
                dst_ref=target.at[c, me],
                send_sem=out_send.at[2 + turn],
                recv_sem=stat_recv.at[turn, c],
                device_id=(group, spot),
                device_id_type=MESH,
            ).start()

        each_peer(start)

    def wait_stats(target, turn, c):
        settled(target.at[c, pl.ds(0, total - 1)], stat_recv.at[turn, c])

    mine = rows_of(me, slots)
    with jax.named_scope("s_out"):
        for i in range(feat_size):
            span = rows_of(group_to(i), group_rows)
            picked = jnp.dot(pick[span], neigh[...], preferred_element_type=f32).astype(bf16)
            for c in range(chunks):
                outgoing[c, span] = picked[:, cols_of(c)]
            send_group(outgoing, halo, halo_recv, out_send.at[0], 0, i)
        for c in range(chunks):
            halo[c, mine] = outgoing[c, mine]
    with jax.named_scope("s_own"):
        pass_done(1)
        for h in range(2):
            send_part(1, h)
        summed[...] = jnp.dot(ah[:, 0:node_rows], neigh[...], preferred_element_type=f32)
        for h in range(2):
            own[halves[h]] = own_part(1, h)

    def turn_pick(s, carry):
        rows = rows_of(s, tile)
        pick_t[:, rows] = pick[rows, :].T
        return carry

    with jax.named_scope("s_turn"):
        lax.fori_loop(0, halo_rows // tile, turn_pick, 0)

    gain = gain_v[...].reshape(1, width)
    shift = shift_v[...].reshape(1, width)
    inverses = {}

    def send_rows(c, i):
        send_group(outgoing, halo, halo_recv, out_send.at[0], c, i)

    def take_rows(c, i):
        with jax.named_scope("s_halo%d%d" % (c, i)):
            group = group_from(i)
            edges = pl.ds(pl.multiple_of(node_rows + group * group_rows, tile), group_rows)
            wait_group(halo, halo_recv, c, i)
            summed[:, cols_of(c)] += jnp.dot(
                ah[:, edges], halo[c, rows_of(group, group_rows)], preferred_element_type=f32)

    def sum_pre(c):
        cols = cols_of(c)
        with jax.named_scope("s_wpre%d" % c):
            if c == 0:
                settled(part_in.at[1], part_sems.at[1, 1])
        with jax.named_scope("s_pre%d" % c):
            col_sum = jnp.zeros((1, chunk), f32)
            col_square = jnp.zeros((1, chunk), f32)
            for b in range(into_blocks):
                span = slice(b * tile, (b + 1) * tile)
                pre = own[span, cols] + part_in[1, span, cols].astype(f32) + summed[span, cols] * scale_ref[span]
                own[span, cols] = pre
                col_sum += jnp.sum(pre, axis=0, keepdims=True)
                col_square += jnp.sum(pre * pre, axis=0, keepdims=True)
            local_a[c, 0:1] = col_sum
            local_a[c, 1:2] = col_square
            first[c, me] = local_a[c]
            send_stats(local_a, first, 0, c)

    def activate(c):
        cols = cols_of(c)
        with jax.named_scope("s_stat1_%d" % c):
            wait_stats(first, 0, c)
        with jax.named_scope("s_act%d" % c):
            sums = jnp.sum(first[c], axis=0)
            mean = sums[0:1] / nodes
            variance = sums[1:2] / nodes - mean * mean
            inverse = 1.0 / jnp.sqrt(variance + epsilon)
            inverses[c] = inverse
            slope_sum = jnp.zeros((1, chunk), f32)
            product_sum = jnp.zeros((1, chunk), f32)
            for b in range(into_blocks):
                span = slice(b * tile, (b + 1) * tile)
                normed = (own[span, cols] - mean) * inverse
                act = gain[:, cols] * normed + shift[:, cols]
                logistic = jax.nn.sigmoid(act)
                hidden_ref[span, cols] = (act * logistic).astype(bf16)
                slope = dh_v[span, cols].astype(f32) * logistic * (1.0 + act * (1.0 - logistic))
                normed_buf[span, cols] = normed
                slope_buf[span, cols] = slope
                slope_sum += jnp.sum(slope, axis=0, keepdims=True)
                product_sum += jnp.sum(slope * normed, axis=0, keepdims=True)
            local_b[c, 0:1] = slope_sum
            local_b[c, 1:2] = product_sum
            second[c, me] = local_b[c]
            send_stats(local_b, second, 1, c)

    def send_back(c):
        cols = cols_of(c)
        with jax.named_scope("s_stat2_%d" % c):
            wait_stats(second, 1, c)
        with jax.named_scope("s_dpre%d" % c):
            sums = jnp.sum(second[c], axis=0)
            shift_grad = sums[0:1] / nodes
            gain_grad = sums[1:2] / nodes
            sgrad_ref[:, cols] = shift_grad
            ggrad_ref[:, cols] = gain_grad
            factor = gain[:, cols] * inverses[c]
            for b in range(into_blocks):
                span = slice(b * tile, (b + 1) * tile)
                dpre = factor * (slope_buf[span, cols] - shift_grad - normed_buf[span, cols] * gain_grad)
                dself_ref[span, cols] = dpre.astype(bf16)
                mg[span, cols] = (dpre * scale_ref[span]).astype(bf16)
        with jax.named_scope("s_back%d" % c):
            for i in range(feat_size):
                group = group_to(i)
                span = rows_of(group, group_rows)
                edges = pl.ds(pl.multiple_of(node_rows + group * group_rows, tile), group_rows)
                back_out[c, span] = jnp.dot(ah_t[edges], mg[:, cols], preferred_element_type=f32).astype(bf16)
                send_group(back_out, returned, halo_recv, out_send.at[1], c, i)
            returned[c, mine] = back_out[c, mine]

    steps = {"S": send_rows, "H": take_rows, "P": sum_pre, "A": activate, "B": send_back}
    for step in "S10 S11 S12 S13 H00 H01 H02 H03 P0 H10 H11 H12 H13 P1 A0 A1 B0 B1".split():
        steps[step[0]](*(int(digit) for digit in step[1:]))
    with jax.named_scope("s_dlocal"):
        summed[...] = jnp.dot(ah_t[0:node_rows], mg[...], preferred_element_type=f32)
    peers_rows = pl.ds(0, (total - 1) * slots)
    with jax.named_scope("s_sendw"):
        for kind in range(2):
            pass_sent(kind)
        settled(xin, near_send.at[2])
        for kind in range(2):
            settled(part_out.at[kind], part_sems.at[0, kind])
        settled(outgoing.at[:, peers_rows], out_send.at[0])
        settled(first.at[:, pl.ds(0, total - 1)], out_send.at[2])
        settled(second.at[:, pl.ds(0, total - 1)], out_send.at[3])
    for c in range(chunks):
        cols = cols_of(c)
        with jax.named_scope("s_gather%d" % c):
            for i in range(feat_size):
                span = rows_of(group_from(i), group_rows)
                wait_group(returned, halo_recv, c, i)
                gathered = jnp.dot(pick_t[:, span], returned[c, span], preferred_element_type=f32)
                if i < feat_size - 1:
                    summed[:, cols] += gathered
                else:
                    dneigh_ref[:, cols] = (summed[:, cols] + gathered).astype(bf16)
    settled(back_out.at[:, peers_rows], out_send.at[1])


def finish_kernel(hidden, d_self, d_neigh, gain_grad, shift_grad,
                  hidden_out, dself_out, dneigh_out, ggrad_out, sgrad_out, flat_gain, flat_shift, sems):
    blocks = ((hidden, hidden_out.at[0, 0]), (d_self, dself_out.at[0, 0]), (d_neigh, dneigh_out.at[0, 0]))
    rows = ((flat_gain, ggrad_out), (flat_shift, sgrad_out))
    copies = [pltpu.make_async_copy(a, b, sems.at[i]) for i, (a, b) in enumerate(blocks + rows)]
    for copy in copies[:3]:
        copy.start()
    flat_gain[...] = gain_grad[...].reshape(flat_gain.shape)
    flat_shift[...] = shift_grad[...].reshape(flat_shift.shape)
    for copy in copies[3:]:
        copy.start()
    for copy in copies:
        copy.wait()


def shards(feat_size, dom_size, features, w_self, w_neigh, gain, shift, d_hidden, send_rows, send_count,
           tile_src, tile_dst, tile_count, tile_vals):
    node_rows, columns = features.shape[2], features.shape[3]
    width = w_self.shape[1]
    tiles, tile = tile_vals.shape[2], tile_vals.shape[3]
    parts, slots = send_rows.shape[2], send_rows.shape[3]
    own_blocks = node_rows // tile
    halo_rows = parts * slots
    all_rows = node_rows + halo_rows
    cells = own_blocks * (all_rows // tile)
    list_lanes = -(-max(tiles, cells) // 128) * 128
    chunks = width // 128
    chunk = width // chunks
    dma = pltpu.SemaphoreType.DMA
    shape = jax.ShapeDtypeStruct
    i32 = jnp.int32
    results = pl.pallas_call(
        functools.partial(layer_kernel, feat_size, dom_size, tile, chunks),
        out_shape=(
            pltpu.VMEM((node_rows, width), bf16),
            pltpu.VMEM((node_rows, width), bf16),
            pltpu.VMEM((node_rows, width), bf16),
            pltpu.VMEM((1, width), f32),
            pltpu.VMEM((1, width), f32),
        ),
        in_specs=[HB] * 12,
        out_specs=(VM,) * 5,
        scratch_shapes=[
            pltpu.VMEM(send_rows.shape, i32),
            pltpu.VMEM(send_count.shape, i32),
            pltpu.VMEM(tile_src.shape, i32),
            pltpu.VMEM(tile_dst.shape, i32),
            pltpu.VMEM(tile_count.shape, i32),
            pltpu.VMEM(gain.shape, f32),
            pltpu.VMEM(shift.shape, f32),
            pltpu.VMEM((node_rows, width), bf16),
            pltpu.VMEM((node_rows, columns), bf16),
            pltpu.VMEM((2, node_rows // 2, columns), bf16),
            pltpu.VMEM((4, node_rows // 2, columns), bf16),
            pltpu.VMEM((3 * columns, width), bf16),
            pltpu.VMEM((3 * columns, width), bf16),
            pltpu.VMEM((2, node_rows, width), bf16),
            pltpu.VMEM((2, node_rows, width), bf16),
            pltpu.VMEM((node_rows, width), f32),
            pltpu.VMEM((node_rows, width), f32),
            pltpu.VMEM((node_rows, width), bf16),
            pltpu.VMEM((chunks, halo_rows, chunk), bf16),
            pltpu.VMEM((chunks, halo_rows, chunk), bf16),
            pltpu.VMEM((halo_rows, node_rows), bf16),
            pltpu.VMEM((node_rows, halo_rows), bf16),
            pltpu.VMEM((node_rows, all_rows), bf16),
            pltpu.VMEM((all_rows, node_rows), bf16),
            pltpu.VMEM((node_rows, width), bf16),
            pltpu.VMEM((chunks, halo_rows, chunk), bf16),
            pltpu.VMEM((chunks, halo_rows, chunk), bf16),
            pltpu.VMEM((node_rows, width), f32),
            pltpu.VMEM((node_rows, width), f32),
            pltpu.VMEM((chunks, parts, 2, chunk), f32),
            pltpu.VMEM((chunks, parts, 2, chunk), f32),
            pltpu.VMEM((chunks, 2, chunk), f32),
            pltpu.VMEM((chunks, 2, chunk), f32),
            pltpu.VMEM((node_rows, 128), f32),
            pltpu.VMEM((tiles, tile, tile), bf16),
            pltpu.VMEM((tiles, tile, tile), f32),
            pltpu.VMEM((8, list_lanes), i32),
            pltpu.SMEM((8, list_lanes), i32),
            dma((11,)), dma((3,)), dma((4,)), dma((2,)), dma((2, 2)), dma((2, 2)),
            dma((chunks, feat_size)), dma((2, chunks)), dma((4,)), pltpu.SemaphoreType.REGULAR((2,)),
        ],
        compiler_params=pltpu.CompilerParams(
            collective_id=0, has_side_effects=True, vmem_limit_bytes=58 * 1024 * 1024),
        name="layer",
    )(features, w_self, w_neigh, send_rows, send_count, tile_src, tile_dst, tile_count, tile_vals, gain, shift, d_hidden)
    kept = [pltpu.with_memory_space_constraint(result, pltpu.VMEM) for result in results]
    out_shape = (1, 1, node_rows, width)
    return pl.pallas_call(
        finish_kernel,
        out_shape=(shape(out_shape, bf16),) * 3 + (shape((width,), f32),) * 2,
        in_specs=[VM] * 5,
        out_specs=(HB,) * 5,
        scratch_shapes=[pltpu.VMEM((width,), f32), pltpu.VMEM((width,), f32), dma((5,))],
        name="finish",
    )(*kept)


def solution(mesh):
    in_specs = (
        P(None, "dom", None, "feat"),
        P("feat", None),
        P("feat", None),
        P(),
        P(),
        P("feat", "dom", None, None),
        P("feat", "dom", None, None),
        P("feat", "dom", None),
        P("feat", "dom", None),
        P("feat", "dom", None),
        P("feat", "dom"),
        P("feat", "dom", None, None, None),
    )
    out_specs = (
        P("feat", "dom", None, None),
        P("feat", "dom", None, None),
        P("feat", "dom", None, None),
        P(),
        P(),
    )
    body = functools.partial(shards, mesh.shape["feat"], mesh.shape["dom"])
    return jax.shard_map(body, mesh=mesh, in_specs=in_specs, out_specs=out_specs, check_vma=False)
```

```python
import functools

import jax
import jax.numpy as jnp
from jax import lax
from jax.experimental import pallas as pl
from jax.experimental.pallas import tpu as pltpu
from jax.sharding import PartitionSpec as P

epsilon = 1e-05
MESH = pl.DeviceIdType.MESH
VM = pl.BlockSpec(memory_space=pltpu.VMEM)
HB = pl.BlockSpec(memory_space=pltpu.HBM)
f32 = jnp.float32
bf16 = jnp.bfloat16


def selection(rows_ref, count_ref, node_rows):
    rows = rows_ref[0, 0]
    parts, slots = rows.shape
    counts = jnp.broadcast_to(count_ref[0], (slots, parts)).T
    live = lax.broadcasted_iota(jnp.int32, (parts, slots), 1) < counts
    wanted = jnp.where(live, rows, -1)
    nodes = lax.broadcasted_iota(jnp.int32, (parts, slots, node_rows), 2)
    picked = wanted[:, :, None] == nodes
    return jnp.where(picked, 1.0, 0.0).astype(bf16).reshape(parts * slots, node_rows)


def tile_tables(from_ref, into_ref, live_ref, from_blocks, cells):
    tiles = from_ref.shape[2]
    spare = cells

    def turned(row):
        return jnp.broadcast_to(row, (tiles, tiles)).T

    at = lax.broadcasted_iota(jnp.int32, (1, tiles), 1)
    key = jnp.where(at < live_ref[...], into_ref[0] * from_blocks + from_ref[0], spare)
    key_down = turned(key)
    down = lax.broadcasted_iota(jnp.int32, (tiles, tiles), 0)
    across = lax.broadcasted_iota(jnp.int32, (tiles, tiles), 1)
    before = (key_down < key) | ((key_down == key) & (down < across))
    rank = jnp.sum(jnp.where(before, 1, 0), axis=0, keepdims=True)
    lands = turned(rank) == across
    order = jnp.sum(jnp.where(lands, down, 0), axis=0, keepdims=True)
    ordered_key = jnp.sum(jnp.where(lands, key_down, 0), axis=0, keepdims=True)
    cell = lax.broadcasted_iota(jnp.int32, (tiles, cells), 1)
    key_cells = jnp.broadcast_to(key, (cells, tiles)).T
    last = jnp.sum(jnp.where(key_cells <= cell, 1, 0), axis=0, keepdims=True) - 1
    found = jnp.sum(jnp.where(key_cells == cell, 1, 0), axis=0, keepdims=True)
    return order, ordered_key, last, found


def layer_kernel(feat_size, dom_size, tile, chunks, x_ref, ws_ref, wn_ref, rows_ref, count_ref, from_ref, into_ref,
                 live_ref, vals_ref, gain_ref, shift_ref, dh_ref,
                 hidden_ref, dself_ref, dneigh_ref, ggrad_ref, sgrad_ref,
                 rows_v, count_v, from_v, into_v, live_v, gain_v, shift_v, dh_v,
                 xown, xside, xin, wnbuf, wsbuf, part_out, part_in, own, summed, neigh, halo, outgoing, pick, pick_t, ah, ah_t,
                 mg, back_out, returned, normed_buf, slope_buf, first, second, local_a, local_b,
                 scale_ref, vbuf, history, lists_v, lists_s,
                 local_sems, near_send, near_recv, pass_send, pass_recv, part_sems, halo_recv, stat_recv, out_send, met):
    me_f, me_d = lax.axis_index("feat"), lax.axis_index("dom")
    me = me_f * dom_size + me_d
    total = feat_size * dom_size
    node_rows = x_ref.shape[2]
    columns, width = wn_ref.shape
    slots = rows_ref.shape[3]
    group_rows = dom_size * slots
    halo_rows = total * slots
    nodes = node_rows * total
    tiles = vbuf.shape[0]
    from_blocks = (node_rows + halo_rows) // tile
    into_blocks = node_rows // tile
    cells = into_blocks * from_blocks
    chunk = width // chunks
    half = node_rows // 2
    across, beside = jnp.bitwise_xor(me_f, 1), jnp.bitwise_xor(me_f, 2)
    facing = jnp.bitwise_xor(me_f, 3)
    sides = (across, beside)
    halves = (pl.ds(0, half), pl.ds(half, half))

    def team_of(limit):
        return next(size for size in (8, 4, 2, 1) if size <= limit and dom_size % size == 0 and columns % (16 * size) == 0)

    teams = (team_of(2), team_of(8))
    share_rows = tuple(columns // size for size in teams)
    seats = tuple(lax.rem(me_d, size) for size in teams)
    nears = range(1, feat_size)
    paired = total & (total - 1) == 0

    def near_of(k):
        return jnp.bitwise_xor(me_f, k) if paired else lax.rem(me_f + k, feat_size)

    def spot_of(k):
        return jnp.bitwise_xor(me_d, dom_size - 1 - k) if paired else lax.rem(me_d + 1 + k, dom_size)

    def group_to(i):
        return near_of(feat_size - 1 - i)

    def group_from(i):
        return near_of(feat_size - 1 - i) if paired else lax.rem(me_f + 1 + i, feat_size)

    def spots_of(i):
        return dom_size - 1 if i == feat_size - 1 else dom_size

    def each_peer(visit):
        for i in range(feat_size):
            def step(k, carry):
                visit(group_to(i), spot_of(k))
                return carry

            lax.fori_loop(0, spots_of(i), step, 0, unroll=True)

    def slab_of(slab):
        return slice(slab * columns, (slab + 1) * columns)

    def share_in(kind, slab, owner):
        rows = share_rows[kind]
        return pl.ds(pl.multiple_of(slab * columns + owner * rows, rows), rows)

    def rows_of(peer, count):
        return pl.ds(pl.multiple_of(peer * count, count), count)

    def cols_of(c):
        return slice(c * chunk, (c + 1) * chunk)

    barrier = pltpu.get_barrier_semaphore()
    split = dom_size % 2 == 0
    side = lax.rem(me_d, 2)
    sibling = me_d + 1 - 2 * side
    pairs = dom_size // 2
    role = 2 * me_f + side
    proxy, keeper = 0, 1

    def hail(where):
        pl.semaphore_signal(barrier, inc=1, device_id=where, device_id_type=MESH)

    def hail_keeper(k, carry):
        hail((0, 2 * lax.rem(lax.div(me_d, 2) + 1 + k, pairs) + 1))
        return carry

    if split:
        for other in sides:
            hail((other, me_d - side * (1 - jnp.minimum(other, 1))))

        @pl.when(role != proxy)
        def _():
            hail((me_f, sibling))

        lax.fori_loop(0, pairs - 1, hail_keeper, 0)

        @pl.when(role != keeper)
        def _():
            hail((0, me_d - side + 1))
    else:
        each_peer(lambda group, spot: hail((group, spot)))

    def meet_near():
        if not split:
            pl.semaphore_wait(barrier, total - 1)
            return

        @pl.when(role > keeper)
        def _():
            pl.semaphore_wait(barrier, 3)

        @pl.when(role == proxy)
        def _():
            pl.semaphore_wait(barrier, 5)
            pl.semaphore_signal(met.at[0], inc=1, device_id=(me_f, sibling), device_id_type=MESH)

        @pl.when(role == keeper)
        def _():
            pl.semaphore_wait(met.at[0], 1)

    def meet_far():
        if not split:
            return

        @pl.when(role == keeper)
        def _():
            pl.semaphore_wait(barrier, total - 1)
            for group in range(feat_size):
                for core in range(2):
                    if (group, core) != (0, 1):
                        where = (group, me_d - side + core)
                        pl.semaphore_signal(met.at[1], inc=1, device_id=where, device_id_type=MESH)

        @pl.when(role != keeper)
        def _():
            pl.semaphore_wait(met.at[1], 1)

    places = [
        (rows_ref, rows_v, 0), (count_ref, count_v, 1), (from_ref, from_v, 2), (into_ref, into_v, 3), (live_ref, live_v, 4),
        (vals_ref.at[0, 0], vbuf, 5), (wn_ref, wnbuf.at[slab_of(0)], 6), (ws_ref, wsbuf.at[slab_of(0)], 6),
        (x_ref.at[me_f, 0], xown, 7), (x_ref.at[beside, 0, halves[0]], xside.at[0], 7),
        (x_ref.at[across, 0, halves[1]], xside.at[1], 7), (gain_ref, gain_v, 8), (shift_ref, shift_v, 9),
        (dh_ref.at[0, 0], dh_v, 10),
    ]
    for source, target, i in places:
        pltpu.make_async_copy(source, target, local_sems.at[i]).start()

    def settled(block, sem):
        pltpu.make_async_copy(block, block, sem).wait()

    with jax.named_scope("s_meet"):
        meet_near()

    def push(source, target, send_sem, recv_sem, where):
        pltpu.make_async_remote_copy(
            src_ref=source,
            dst_ref=target,
            send_sem=send_sem,
            recv_sem=recv_sem,
            device_id=where,
            device_id_type=MESH,
        ).start()

    weights = (wnbuf, wsbuf)

    def evens(kind):
        return range(2, teams[kind], 2)

    def shares(kind, count):
        return weights[kind].at[pl.ds(0, 2 * count * share_rows[kind])]

    def hand_on(kind, slab, shift, flip):
        place = weights[kind].at[share_in(kind, slab, jnp.bitwise_xor(seats[kind], shift))]
        mate = me_d - seats[kind] + jnp.bitwise_xor(seats[kind], flip)
        push(place, place, pass_send.at[kind], pass_recv.at[kind, 1 if flip == 1 else 0], (me_f, mate))

    def pass_first(kind):
        settled(shares(kind, 1), near_recv.at[kind])
        if teams[kind] > 1:
            for slab in (1, 2):
                for flip in (*evens(kind), 1):
                    hand_on(kind, slab, 0, flip)

    def pass_second(kind):
        if teams[kind] > 2:
            settled(shares(kind, teams[kind] // 2 - 1), pass_recv.at[kind, 0])
            for slab in (1, 2):
                for shift in evens(kind):
                    hand_on(kind, slab, shift, 1)

    def pass_done(kind):
        if teams[kind] > 1:
            settled(shares(kind, teams[kind] // 2), pass_recv.at[kind, 1])

    def pass_sent(kind):
        settled(shares(kind, 1), near_send.at[kind])
        if teams[kind] > 1:
            settled(shares(kind, teams[kind] - 1), pass_send.at[kind])

    def side_part(kind, h):
        weight = weights[kind]
        return (
            jnp.dot(xside[h], weight[slab_of(0)], preferred_element_type=f32)
            + jnp.dot(xin[h], weight[slab_of(1 + h)], preferred_element_type=f32)
        )

    def own_part(kind, h):
        weight = weights[kind]
        return (
            jnp.dot(xown[halves[h]], weight[slab_of(0)], preferred_element_type=f32)
            + jnp.dot(xin[2 + h], weight[slab_of(1 + h)], preferred_element_type=f32)
        )

    def send_part(kind, h):
        part_out[kind, halves[h]] = side_part(kind, h).astype(bf16)
        push(part_out.at[kind, halves[h]], part_in.at[kind, halves[h]],
             part_sems.at[0, kind], part_sems.at[1, kind], (sides[1 - h], me_d))

    with jax.named_scope("s_near"):
        for kind, source in enumerate((wn_ref, ws_ref)):
            for h in range(2):
                push(source.at[share_in(kind, 0, seats[kind])], weights[kind].at[share_in(kind, 1 + h, seats[kind])],
                     near_send.at[kind], near_recv.at[kind], (sides[h], me_d))
        for h in range(2):
            push(x_ref.at[facing, 0, halves[h]], xin.at[h], near_send.at[2], near_recv.at[2], (sides[h], me_d))
        for h in range(2):
            push(x_ref.at[sides[h], 0, halves[h]], xin.at[2 + h], near_send.at[2], near_recv.at[3], (sides[h], me_d))

    with jax.named_scope("s_pick"):
        settled(rows_v, local_sems.at[0])
        settled(count_v, local_sems.at[1])
        pick[...] = selection(rows_v, count_v, node_rows)
    with jax.named_scope("s_tables"):
        for i, block in ((2, from_v), (3, into_v), (4, live_v)):
            settled(block, local_sems.at[i])
        order, ordered_key, last, found = tile_tables(from_v, into_v, live_v, from_blocks, cells)
        lists_v[...] = jnp.zeros_like(lists_v)
        lists_v[0:1, 0:tiles] = order
        lists_v[1:2, 0:tiles] = ordered_key
        lists_v[2:3, 0:cells] = last
        lists_v[3:4, 0:cells] = found
        to_scalars = pltpu.make_async_copy(lists_v, lists_s, local_sems.at[0])
        to_scalars.start()
    with jax.named_scope("s_lists"):
        to_scalars.wait()
        both_slabs = wnbuf.at[pl.ds(0, 2 * columns)]
        for i, block in ((5, vbuf), (6, both_slabs), (7, xin), (8, gain_v), (9, shift_v), (10, dh_v)):
            settled(block, local_sems.at[i])

    def add_tile(r, running):
        earlier = lists_s[1, jnp.maximum(r - 1, 0)]
        running = jnp.where(lists_s[1, r] == earlier, running, 0.0) + vbuf[lists_s[0, r]].astype(f32)
        history[r] = running
        return running

    with jax.named_scope("s_pass1"):
        pass_first(0)
    with jax.named_scope("s_addtile"):
        lax.fori_loop(0, tiles, add_tile, jnp.zeros((tile, tile), f32), unroll=2)
    with jax.named_scope("s_far"):
        meet_far()
        pass_first(1)

    def settle_block(b):
        span = slice(b * tile, (b + 1) * tile)

        def settle(s, weight):
            spot = b * from_blocks + s
            value = history[jnp.maximum(lists_s[2, spot], 0)]
            value = jnp.where(lists_s[3, spot] > 0, value, 0.0)
            high = value.astype(bf16)
            lanes = pl.ds(pl.multiple_of(s * tile, tile), tile)
            ah[span, lanes] = high
            ah_t[lanes, span] = high.T
            return weight + value

        weight = lax.fori_loop(0, from_blocks, settle, jnp.zeros((tile, tile), f32))
        inverse_degree = 1.0 / (1.0 + jnp.sum(weight, axis=1, keepdims=True))
        scale_ref[span] = jnp.broadcast_to(inverse_degree, (tile, 128))

    for b in range(into_blocks):
        if b == max(into_blocks - 3, 0):
            with jax.named_scope("s_wpart"):
                pass_done(0)
                settled(xin.at[pl.ds(0, 2)], near_recv.at[2])
            with jax.named_scope("s_part"):
                for h in range(2):
                    send_part(0, h)
        with jax.named_scope("s_settle%d" % b):
            settle_block(b)
    with jax.named_scope("s_pass2"):
        pass_second(1)
    with jax.named_scope("s_wown"):
        settled(xin.at[pl.ds(2, 2)], near_recv.at[3])
    with jax.named_scope("s_neigh"):
        for h in range(2):
            summed[halves[h]] = own_part(0, h)
    with jax.named_scope("s_wneigh"):
        settled(part_in.at[0], part_sems.at[1, 0])
    with jax.named_scope("s_round"):
        neigh[...] = (summed[...] + part_in[0].astype(f32)).astype(bf16)

    def send_group(source, target, recv_sems, send_sem, c, i):
        group = group_to(i)

        def start(k, carry):
            spot = spot_of(k)
            pltpu.make_async_remote_copy(
                src_ref=source.at[c, rows_of(group * dom_size + spot, slots)],
                dst_ref=target.at[c, rows_of(me, slots)],
                send_sem=send_sem,
                recv_sem=recv_sems.at[c, me_f],
                device_id=(group, spot),
                device_id_type=MESH,
            ).start()
            return carry

        lax.fori_loop(0, spots_of(i), start, 0)

    def wait_group(buffer, recv_sems, c, i):
        settled(buffer.at[c, pl.ds(0, spots_of(i) * slots)], recv_sems.at[c, group_from(i)])

    def send_stats(source, target, turn, c):
        def start(group, spot):
            pltpu.make_async_remote_copy(
                src_ref=source.at[c],
                dst_ref=target.at[c, me],
                send_sem=out_send.at[2 + turn],
                recv_sem=stat_recv.at[turn, c],
                device_id=(group, spot),
                device_id_type=MESH,
            ).start()

        each_peer(start)

    def wait_stats(target, turn, c):
        settled(target.at[c, pl.ds(0, total - 1)], stat_recv.at[turn, c])

    mine = rows_of(me, slots)
    with jax.named_scope("s_out"):
        for i in range(feat_size):
            span = rows_of(group_to(i), group_rows)
            picked = jnp.dot(pick[span], neigh[...], preferred_element_type=f32).astype(bf16)
            for c in range(chunks):
                outgoing[c, span] = picked[:, cols_of(c)]
            send_group(outgoing, halo, halo_recv, out_send.at[0], 0, i)
        for c in range(chunks):
            halo[c, mine] = outgoing[c, mine]
    with jax.named_scope("s_own"):
        pass_done(1)
        for h in range(2):
            send_part(1, h)
        summed[...] = jnp.dot(ah[:, 0:node_rows], neigh[...], preferred_element_type=f32)
        for h in range(2):
            own[halves[h]] = own_part(1, h)

    def turn_pick(s, carry):
        rows = rows_of(s, tile)
        pick_t[:, rows] = pick[rows, :].T
        return carry

    with jax.named_scope("s_turn"):
        lax.fori_loop(0, halo_rows // tile, turn_pick, 0)

    gain = gain_v[...].reshape(1, width)
    shift = shift_v[...].reshape(1, width)
    inverses = {}

    def send_rows(c, i):
        send_group(outgoing, halo, halo_recv, out_send.at[0], c, i)

    def take_rows(c, i):
        with jax.named_scope("s_halo%d%d" % (c, i)):
            group = group_from(i)
            edges = pl.ds(pl.multiple_of(node_rows + group * group_rows, tile), group_rows)
            wait_group(halo, halo_recv, c, i)
            summed[:, cols_of(c)] += jnp.dot(
                ah[:, edges], halo[c, rows_of(group, group_rows)], preferred_element_type=f32)

    def sum_pre(c):
        cols = cols_of(c)
        with jax.named_scope("s_wpre%d" % c):
            if c == 0:
                settled(part_in.at[1], part_sems.at[1, 1])
        with jax.named_scope("s_pre%d" % c):
            col_sum = jnp.zeros((1, chunk), f32)
            col_square = jnp.zeros((1, chunk), f32)
            for b in range(into_blocks):
                span = slice(b * tile, (b + 1) * tile)
                pre = own[span, cols] + part_in[1, span, cols].astype(f32) + summed[span, cols] * scale_ref[span]
                own[span, cols] = pre
                col_sum += jnp.sum(pre, axis=0, keepdims=True)
                col_square += jnp.sum(pre * pre, axis=0, keepdims=True)
            local_a[c, 0:1] = col_sum
            local_a[c, 1:2] = col_square
            first[c, me] = local_a[c]
            send_stats(local_a, first, 0, c)

    def activate(c):
        cols = cols_of(c)
        with jax.named_scope("s_stat1_%d" % c):
            wait_stats(first, 0, c)
        with jax.named_scope("s_act%d" % c):
            sums = jnp.sum(first[c], axis=0)
            mean = sums[0:1] / nodes
            variance = sums[1:2] / nodes - mean * mean
            inverse = 1.0 / jnp.sqrt(variance + epsilon)
            inverses[c] = inverse
            slope_sum = jnp.zeros((1, chunk), f32)
            product_sum = jnp.zeros((1, chunk), f32)
            for b in range(into_blocks):
                span = slice(b * tile, (b + 1) * tile)
                normed = (own[span, cols] - mean) * inverse
                act = gain[:, cols] * normed + shift[:, cols]
                logistic = jax.nn.sigmoid(act)
                hidden_ref[span, cols] = (act * logistic).astype(bf16)
                slope = dh_v[span, cols].astype(f32) * logistic * (1.0 + act * (1.0 - logistic))
                normed_buf[span, cols] = normed
                slope_buf[span, cols] = slope
                slope_sum += jnp.sum(slope, axis=0, keepdims=True)
                product_sum += jnp.sum(slope * normed, axis=0, keepdims=True)
            local_b[c, 0:1] = slope_sum
            local_b[c, 1:2] = product_sum
            second[c, me] = local_b[c]
            send_stats(local_b, second, 1, c)

    def send_back(c):
        cols = cols_of(c)
        with jax.named_scope("s_stat2_%d" % c):
            wait_stats(second, 1, c)
        with jax.named_scope("s_dpre%d" % c):
            sums = jnp.sum(second[c], axis=0)
            shift_grad = sums[0:1] / nodes
            gain_grad = sums[1:2] / nodes
            sgrad_ref[:, cols] = shift_grad
            ggrad_ref[:, cols] = gain_grad
            factor = gain[:, cols] * inverses[c]
            for b in range(into_blocks):
                span = slice(b * tile, (b + 1) * tile)
                dpre = factor * (slope_buf[span, cols] - shift_grad - normed_buf[span, cols] * gain_grad)
                dself_ref[span, cols] = dpre.astype(bf16)
                mg[span, cols] = (dpre * scale_ref[span]).astype(bf16)
        with jax.named_scope("s_back%d" % c):
            for i in range(feat_size):
                group = group_to(i)
                span = rows_of(group, group_rows)
                edges = pl.ds(pl.multiple_of(node_rows + group * group_rows, tile), group_rows)
                back_out[c, span] = jnp.dot(ah_t[edges], mg[:, cols], preferred_element_type=f32).astype(bf16)
                send_group(back_out, returned, halo_recv, out_send.at[1], c, i)
            returned[c, mine] = back_out[c, mine]

    steps = {"S": send_rows, "H": take_rows, "P": sum_pre, "A": activate, "B": send_back}
    for step in "H00 S10 S11 S12 S13 H01 H02 H03 P0 H10 H11 H12 H13 P1 A0 A1 B0 B1".split():
        steps[step[0]](*(int(digit) for digit in step[1:]))
    with jax.named_scope("s_dlocal"):
        summed[...] = jnp.dot(ah_t[0:node_rows], mg[...], preferred_element_type=f32)
    peers_rows = pl.ds(0, (total - 1) * slots)
    with jax.named_scope("s_sendw"):
        for kind in range(2):
            pass_sent(kind)
        settled(xin, near_send.at[2])
        for kind in range(2):
            settled(part_out.at[kind], part_sems.at[0, kind])
        settled(outgoing.at[:, peers_rows], out_send.at[0])
        settled(first.at[:, pl.ds(0, total - 1)], out_send.at[2])
        settled(second.at[:, pl.ds(0, total - 1)], out_send.at[3])
    for c in range(chunks):
        cols = cols_of(c)
        with jax.named_scope("s_gather%d" % c):
            for i in range(feat_size):
                span = rows_of(group_from(i), group_rows)
                wait_group(returned, halo_recv, c, i)
                gathered = jnp.dot(pick_t[:, span], returned[c, span], preferred_element_type=f32)
                if i < feat_size - 1:
                    summed[:, cols] += gathered
                else:
                    dneigh_ref[:, cols] = (summed[:, cols] + gathered).astype(bf16)
    settled(back_out.at[:, peers_rows], out_send.at[1])


def finish_kernel(hidden, d_self, d_neigh, gain_grad, shift_grad,
                  hidden_out, dself_out, dneigh_out, ggrad_out, sgrad_out, flat_gain, flat_shift, sems):
    blocks = ((hidden, hidden_out.at[0, 0]), (d_self, dself_out.at[0, 0]), (d_neigh, dneigh_out.at[0, 0]))
    rows = ((flat_gain, ggrad_out), (flat_shift, sgrad_out))
    copies = [pltpu.make_async_copy(a, b, sems.at[i]) for i, (a, b) in enumerate(blocks + rows)]
    for copy in copies[:3]:
        copy.start()
    flat_gain[...] = gain_grad[...].reshape(flat_gain.shape)
    flat_shift[...] = shift_grad[...].reshape(flat_shift.shape)
    for copy in copies[3:]:
        copy.start()
    for copy in copies:
        copy.wait()


def shards(feat_size, dom_size, features, w_self, w_neigh, gain, shift, d_hidden, send_rows, send_count,
           tile_src, tile_dst, tile_count, tile_vals):
    node_rows, columns = features.shape[2], features.shape[3]
    width = w_self.shape[1]
    tiles, tile = tile_vals.shape[2], tile_vals.shape[3]
    parts, slots = send_rows.shape[2], send_rows.shape[3]
    own_blocks = node_rows // tile
    halo_rows = parts * slots
    all_rows = node_rows + halo_rows
    cells = own_blocks * (all_rows // tile)
    list_lanes = -(-max(tiles, cells) // 128) * 128
    chunks = width // 128
    chunk = width // chunks
    dma = pltpu.SemaphoreType.DMA
    shape = jax.ShapeDtypeStruct
    i32 = jnp.int32
    results = pl.pallas_call(
        functools.partial(layer_kernel, feat_size, dom_size, tile, chunks),
        out_shape=(
            pltpu.VMEM((node_rows, width), bf16),
            pltpu.VMEM((node_rows, width), bf16),
            pltpu.VMEM((node_rows, width), bf16),
            pltpu.VMEM((1, width), f32),
            pltpu.VMEM((1, width), f32),
        ),
        in_specs=[HB] * 12,
        out_specs=(VM,) * 5,
        scratch_shapes=[
            pltpu.VMEM(send_rows.shape, i32),
            pltpu.VMEM(send_count.shape, i32),
            pltpu.VMEM(tile_src.shape, i32),
            pltpu.VMEM(tile_dst.shape, i32),
            pltpu.VMEM(tile_count.shape, i32),
            pltpu.VMEM(gain.shape, f32),
            pltpu.VMEM(shift.shape, f32),
            pltpu.VMEM((node_rows, width), bf16),
            pltpu.VMEM((node_rows, columns), bf16),
            pltpu.VMEM((2, node_rows // 2, columns), bf16),
            pltpu.VMEM((4, node_rows // 2, columns), bf16),
            pltpu.VMEM((3 * columns, width), bf16),
            pltpu.VMEM((3 * columns, width), bf16),
            pltpu.VMEM((2, node_rows, width), bf16),
            pltpu.VMEM((2, node_rows, width), bf16),
            pltpu.VMEM((node_rows, width), f32),
            pltpu.VMEM((node_rows, width), f32),
            pltpu.VMEM((node_rows, width), bf16),
            pltpu.VMEM((chunks, halo_rows, chunk), bf16),
            pltpu.VMEM((chunks, halo_rows, chunk), bf16),
            pltpu.VMEM((halo_rows, node_rows), bf16),
            pltpu.VMEM((node_rows, halo_rows), bf16),
            pltpu.VMEM((node_rows, all_rows), bf16),
            pltpu.VMEM((all_rows, node_rows), bf16),
            pltpu.VMEM((node_rows, width), bf16),
            pltpu.VMEM((chunks, halo_rows, chunk), bf16),
            pltpu.VMEM((chunks, halo_rows, chunk), bf16),
            pltpu.VMEM((node_rows, width), f32),
            pltpu.VMEM((node_rows, width), f32),
            pltpu.VMEM((chunks, parts, 2, chunk), f32),
            pltpu.VMEM((chunks, parts, 2, chunk), f32),
            pltpu.VMEM((chunks, 2, chunk), f32),
            pltpu.VMEM((chunks, 2, chunk), f32),
            pltpu.VMEM((node_rows, 128), f32),
            pltpu.VMEM((tiles, tile, tile), bf16),
            pltpu.VMEM((tiles, tile, tile), f32),
            pltpu.VMEM((8, list_lanes), i32),
            pltpu.SMEM((8, list_lanes), i32),
            dma((11,)), dma((3,)), dma((4,)), dma((2,)), dma((2, 2)), dma((2, 2)),
            dma((chunks, feat_size)), dma((2, chunks)), dma((4,)), pltpu.SemaphoreType.REGULAR((2,)),
        ],
        compiler_params=pltpu.CompilerParams(
            collective_id=0, has_side_effects=True, vmem_limit_bytes=58 * 1024 * 1024),
        name="layer",
    )(features, w_self, w_neigh, send_rows, send_count, tile_src, tile_dst, tile_count, tile_vals, gain, shift, d_hidden)
    kept = [pltpu.with_memory_space_constraint(result, pltpu.VMEM) for result in results]
    out_shape = (1, 1, node_rows, width)
    return pl.pallas_call(
        finish_kernel,
        out_shape=(shape(out_shape, bf16),) * 3 + (shape((width,), f32),) * 2,
        in_specs=[VM] * 5,
        out_specs=(HB,) * 5,
        scratch_shapes=[pltpu.VMEM((width,), f32), pltpu.VMEM((width,), f32), dma((5,))],
        name="finish",
    )(*kept)


def solution(mesh):
    in_specs = (
        P(None, "dom", None, "feat"),
        P("feat", None),
        P("feat", None),
        P(),
        P(),
        P("feat", "dom", None, None),
        P("feat", "dom", None, None),
        P("feat", "dom", None),
        P("feat", "dom", None),
        P("feat", "dom", None),
        P("feat", "dom"),
        P("feat", "dom", None, None, None),
    )
    out_specs = (
        P("feat", "dom", None, None),
        P("feat", "dom", None, None),
        P("feat", "dom", None, None),
        P(),
        P(),
    )
    body = functools.partial(shards, mesh.shape["feat"], mesh.shape["dom"])
    return jax.shard_map(body, mesh=mesh, in_specs=in_specs, out_specs=out_specs, check_vma=False)
```
